32 devices in a mesh: band: 8 (over z, x), dom: 4 (over y, core).
Axes of the slice: x: 2, y: 2, z: 4, core: 2. Of those that a mesh axis runs over, the one named last changes fastest.
Arguments:
- orbitals: bfloat16 [512, 16, 2048], P('band', 'dom'), may hold values from -6 to 6
- potential: float32 [16, 2048], P('dom'), may hold values from 0 to 2
- bounds: float32 [2], replicated, may hold values from 1 to 10, as said below
Outputs:
- rotated: bfloat16 [512, 16, 2048], P('band', 'dom')
- projected: float32 [512, 512], replicated
The draws below stay inside these ranges and needn't reach their ends.
Inputs may be any that keep to these rules, and one draw needn't show every extreme that they name: bounds[0] lies in 1 to 2 and bounds[1] in 8.5 to 10, above the whole spectrum of H.
All inputs are finite; a program needn't handle non-finite values.
Results may differ from the reference program's by a relative error of at most 0.006.
Values may be sent and summed in bfloat16 or wider, within the bound.
A program may use at most 128 MiB of HBM per device.

```python
import math
import jax
import jax.numpy as jnp
from jax import lax

BANDS = 512
GRID_Y = 64
GRID_Z = 32
DEG = 8
NS_STEPS = 8
GRID_X = 16
GRID_YZ = 2048


def draw_bounds(key, part):
    first_key, second_key = jax.random.split(jax.random.fold_in(key, 17))
    lower_cut = jax.random.uniform(first_key, (), jnp.float32, 1.0, 2.0)
    upper_cut = jax.random.uniform(second_key, (), jnp.float32, 8.5, 10.0)
    return jnp.stack([lower_cut, upper_cut]).astype(jnp.float32)


def block_scale(rng, extent, pieces, smallest, largest):
    factor_of = 1.0
    for dim, parts in pieces:
        steps = jax.random.uniform(jax.random.fold_in(jax.random.fold_in(rng, 6), dim), (parts,), jnp.float32, smallest / len(pieces), largest / len(pieces))
        factor_of = factor_of * jnp.repeat(jnp.exp(steps), extent[dim] // parts).reshape((-1,) + (1,) * (len(extent) - 1 - dim))
    return factor_of


def centred(key, dims, width, bound, pieces=(), kind=jnp.bfloat16):
    entries = jax.random.normal(key, dims, jnp.float32) * width
    if len(pieces) > 0:
        entries = block_scale(key, dims, pieces, -0.22, 0.18) * entries
    return jnp.clip(entries, min=-bound, max=bound).astype(kind)


def setup_inputs(seed: int = 0) -> dict:
    key_of = jax.random.split(jax.random.key(seed), 4)
    orbitals = centred(key_of[0], (BANDS, GRID_X, GRID_YZ), 1.0, 6.0, ((0, 8), (1, 4)))
    potential = jnp.clip(2.0 * jax.random.uniform(key_of[1], (GRID_X, GRID_YZ), jnp.float32) ** block_scale(key_of[1], (GRID_X, GRID_YZ), ((0, 4),), -0.2, 0.2), 0.0, 2.0)
    bounds = draw_bounds(jax.random.fold_in(key_of[3], 71), 0)
    return dict(orbitals=orbitals, potential=potential, bounds=bounds)


def hamiltonian(field, pot_grid):
    beside = jnp.roll(field, -1, 1) + jnp.roll(field, 1, 1)
    beside = beside + jnp.roll(field, -1, 2) + jnp.roll(field, 1, 2)
    beside = beside + jnp.roll(field, -1, 3) + jnp.roll(field, 1, 3)
    return -0.5 * (beside - 6.0 * field) + pot_grid * field

def filter_group(orbital_block, pot_grid, lower_cut, upper_cut):
    half_width = (upper_cut - lower_cut) / 2.0
    centre = (upper_cut + lower_cut) / 2.0
    start = orbital_block.astype(jnp.float32)
    earlier = start
    current = (hamiltonian(start, pot_grid) - centre * start) / half_width
    for repeat in range(DEG - 1):
        following = 2.0 * (hamiltonian(current, pot_grid) - centre * current) / half_width - earlier
        earlier = current
        current = following
    applied = hamiltonian(current, pot_grid)
    return (current.astype(jnp.bfloat16), applied.astype(jnp.bfloat16))

def reference(orbitals, potential, bounds):
    grid_x = orbitals.shape[1]
    group_size = math.gcd(BANDS, 64)
    pot_grid = potential.reshape(grid_x, GRID_Y, GRID_Z)
    blocks = orbitals.reshape(BANDS // group_size, group_size, grid_x, GRID_Y, GRID_Z)
    lower_cut = bounds[0]
    upper_cut = bounds[1]
    filt, applied = lax.map(lambda item: filter_group(item, pot_grid, lower_cut, upper_cut), blocks)
    points = grid_x * GRID_Y * GRID_Z
    filt = filt.reshape(BANDS, points)
    applied = applied.reshape(BANDS, points)
    cell_volume = 1.0 / points
    correlation = jnp.dot(filt, filt.T, preferred_element_type=jnp.float32) * cell_volume
    hamil_sub = jnp.dot(filt, applied.T, preferred_element_type=jnp.float32) * cell_volume
    scale = jnp.sqrt(jnp.sum(correlation * correlation) + 1e-06)
    scaled = correlation / scale
    identity = jnp.eye(BANDS, dtype=jnp.float32)
    inverse = identity
    high = lax.Precision.HIGHEST
    for repeat in range(NS_STEPS):
        factor = 1.5 * identity - 0.5 * jnp.dot(inverse, scaled, precision=high)
        scaled = jnp.dot(factor, scaled, precision=high)
        inverse = jnp.dot(factor, inverse, precision=high)
    transform = inverse / jnp.sqrt(scale)
    projected = jnp.dot(jnp.dot(transform.T, hamil_sub, precision=high), transform, precision=high)
    rotated = jnp.dot(transform.T, filt.astype(jnp.float32), precision=high).astype(jnp.bfloat16)
    return (rotated.reshape(BANDS, grid_x, GRID_Y * GRID_Z), projected)
```

```python
import functools

import jax
import jax.numpy as jnp
from jax import lax
from jax.experimental import pallas as pl
from jax.experimental.pallas import tpu as pltpu
from jax.sharding import PartitionSpec as P

GRID_Z = 32
DEG = 8
NS_STEPS = 8
LANES = 128
TILE_ROWS = 8


def filter_kernel(scal_ref, cells_ref, pot_ref, sums_ref, filt_ref, applied_ref, field, high, low, coef):
    planes, bands, width = cells_ref.shape
    rows = planes * bands
    blocks_per_plane = filt_ref.shape[0] // planes
    block = filt_ref.shape[2]
    tile = sums_ref.shape[1]
    inv_half = scal_ref[0]
    centre = scal_ref[1]

    for x in range(planes):
        mine = pl.ds(x * bands, bands)
        coef[mine, :] = jnp.broadcast_to(3.0 + pot_ref[x], (bands, width))
        start = cells_ref[x].astype(jnp.float32)
        field[0, mine, :] = start
    for c in range(width // tile):
        cols = pl.ds(c * tile, tile)
        start = field[0, :, cols]
        high[0, :, cols] = start.astype(jnp.bfloat16)
        low[0, :, cols] = jnp.zeros((rows, tile), jnp.bfloat16)

    def shifted(v, by):
        if bands % 8 == 0:
            return jnp.concatenate([v[by:], v[:by]], axis=0)
        return pltpu.roll(v, (rows - by) % rows, 0)

    def neighbours(slot, c, v):
        cols = pl.ds(pl.multiple_of(c * tile, tile), tile)
        left = pl.ds(pl.multiple_of(lax.rem(c * tile + width - LANES, width), LANES), LANES)
        right = pl.ds(pl.multiple_of(lax.rem(c * tile + tile, width), LANES), LANES)

        def part(ref):
            wide = jnp.concatenate([ref[slot, :, left], ref[slot, :, cols], ref[slot, :, right]], axis=1)
            return dot(wide, sums_ref[...])

        return part(high) + part(low) + (shifted(v, bands) + shifted(v, rows - bands))

    def sweep(slot, other, weight, diagonal, first):
        def run(c, carry):
            cols = pl.ds(pl.multiple_of(c * tile, tile), tile)
            v = field[slot, :, cols]
            fresh = weight * neighbours(slot, c, v) + (coef[:, cols] * diagonal[0] + diagonal[1]) * v
            if not first:
                fresh = fresh - field[other, :, cols]
            field[other, :, cols] = fresh
            top, rest = split(fresh)
            high[other, :, cols] = top
            low[other, :, cols] = rest
            return carry

        lax.fori_loop(0, width // tile, run, 0)

    sweep(0, 1, -0.5 * inv_half, (inv_half, -centre * inv_half), True)

    def middle(k, carry):
        slot = lax.rem(k, 2)
        sweep(slot, 1 - slot, -inv_half, (2.0 * inv_half, -2.0 * centre * inv_half), False)
        return carry

    lax.fori_loop(1, DEG, middle, 0)
    slot = DEG % 2
    for c in range(width // tile):
        cols = pl.ds(c * tile, tile)
        v = field[slot, :, cols]
        applied = coef[:, cols] * v - 0.5 * neighbours(slot, c, v)
        piece, inner = divmod(c * tile, block)
        for x in range(planes):
            where = (x * blocks_per_plane + piece, slice(None), pl.ds(inner, tile))
            filt_ref[where] = v[x * bands : (x + 1) * bands].astype(jnp.bfloat16)
            applied_ref[where] = applied[x * bands : (x + 1) * bands].astype(jnp.bfloat16)


def neighbour_sums(tile):
    source = lax.broadcasted_iota(jnp.int32, (tile + 2 * LANES, tile), 0) - LANES
    target = lax.broadcasted_iota(jnp.int32, (tile + 2 * LANES, tile), 1)
    step = source - target
    same_row = (source >= 0) & (source // GRID_Z == target // GRID_Z)
    apart = lax.rem(step + GRID_Z, GRID_Z)
    beside_z = same_row & ((apart == 1) | (apart == GRID_Z - 1))
    beside_y = (step == GRID_Z) | (step == -GRID_Z)
    return (beside_z | beside_y).astype(jnp.bfloat16)


def filter_bands(cells, potential, scalars, devices):
    planes, bands, width = cells.shape
    rows = planes * bands
    block = planes * width // devices
    out = jax.ShapeDtypeStruct((devices, bands, block), jnp.bfloat16)
    vmem = pl.BlockSpec(memory_space=pltpu.VMEM)
    return pl.pallas_call(
        filter_kernel,
        out_shape=(out, out),
        in_specs=[pl.BlockSpec(memory_space=pltpu.SMEM), vmem, vmem, vmem],
        out_specs=(vmem, vmem),
        scratch_shapes=[
            pltpu.VMEM((2, rows, width), jnp.float32),
            pltpu.VMEM((2, rows, width), jnp.bfloat16),
            pltpu.VMEM((2, rows, width), jnp.bfloat16),
            pltpu.VMEM((rows, width), jnp.float32),
        ],
        compiler_params=pltpu.CompilerParams(vmem_limit_bytes=48 << 20),
    )(scalars, cells, potential, neighbour_sums(min(256, block)))


def split(value):
    spread = value * 65537.0
    high = spread - (spread - value)
    return high.astype(jnp.bfloat16), (value - high).astype(jnp.bfloat16)


def dot(a, b):
    return jnp.dot(a, b, preferred_element_type=jnp.float32)


def dot3(a, b):
    (a_high, a_low), (b_high, b_low) = a, b
    return dot(a_high, b_high) + (dot(a_high, b_low) + dot(a_low, b_high))


def exchange_bits(doms, groups):
    dom = [("dom", 1 << i) for i in range(1, (doms - 1).bit_length())]
    band = [("band", 1 << i) for i in range((groups - 1).bit_length())]
    core = [("dom", 1)]
    return core + band[:1] + dom + band[1:], core + dom + band


def gram_sum(bits, cell_volume, filt_ref, other_ref, total, send, recv, gath, send_sem, recv_sem):
    size = filt_ref.shape[0] // 2
    index = {axis: lax.axis_index(axis) for axis in ("dom", "band")}

    def partner(axis, bit):
        mine = lax.rem(index[axis] // bit, 2)
        return mine, {axis: index[axis] + bit - 2 * bit * mine}

    barrier = pltpu.get_barrier_semaphore()
    for axis, bit in bits[0]:
        pl.semaphore_signal(
            barrier, inc=1, device_id=partner(axis, bit)[1], device_id_type=pl.DeviceIdType.MESH
        )

    pairs = (((1,), (1,)), ((), ()))
    for stream in range(2):
        total[stream] = cell_volume * lax.dot_general(
            filt_ref[pl.ds(stream * size, size), :],
            other_ref[...],
            pairs,
            preferred_element_type=jnp.float32,
        )
    pl.semaphore_wait(barrier, len(bits[0]))

    def copy(stream, number, source, target, device):
        made = pltpu.make_async_remote_copy(
            src_ref=source,
            dst_ref=target,
            send_sem=send_sem.at[stream, number],
            recv_sem=recv_sem.at[stream, number],
            device_id=device,
            device_id_type=pl.DeviceIdType.MESH,
        )
        made.start()
        return made

    stages = len(bits[0])
    start = [jnp.int32(0)] * 2
    halved = [[], []]
    length, offset = size, 0
    for stage in range(stages):
        halve = length >= 2 * TILE_ROWS
        count = length // 2 if halve else length
        space = pl.ds(offset, count)
        flight = []
        for stream in range(2):
            axis, bit = bits[stream][stage]
            mine, device = partner(axis, bit)
            give = start[stream] + (1 - mine) * count if halve else start[stream]
            keep = start[stream] + mine * count if halve else start[stream]
            give = pl.multiple_of(give, TILE_ROWS)
            send[stream, space, :] = total[stream, pl.ds(give, count), :]
            flight.append(
                copy(stream, stage, send.at[stream, space], recv.at[stream, space], device)
            )
            start[stream] = pl.multiple_of(keep, TILE_ROWS)
            if halve:
                halved[stream].append((stage, mine, device))
        for stream in range(2):
            flight[stream].wait()
            kept = pl.ds(start[stream], count)
            if halve:
                own = total[stream, kept, :]
            else:
                own = send[stream, space, :]
            total[stream, kept, :] = own + recv[stream, space, :]
        length = count
        offset += count

    for stream in range(2):
        kept = pl.ds(start[stream], length)
        gath[stream, kept, :] = total[stream, kept, :]
    for back in range(len(halved[0]) - 1, -1, -1):
        flight = []
        for stream in range(2):
            stage, mine, device = halved[stream][back]
            area = gath.at[stream, pl.ds(start[stream], length)]
            flight.append(copy(stream, stages + stage, area, area, device))
            start[stream] = pl.multiple_of(start[stream] - mine * length, TILE_ROWS)
        for made in flight:
            made.wait()
        length *= 2


def orthonormal_kernel(
    bits, cell_volume, groups, filt_ref, out_ref, trans_ref,
    total, send, recv, gath, y_ref, z_ref, t_ref, send_sem, recv_sem,
):
    gram_sum(bits, cell_volume, filt_ref, filt_ref, total, send, recv, gath, send_sem, recv_sem)
    size = filt_ref.shape[0]
    outer, inner, width = groups
    row = lax.broadcasted_iota(jnp.int32, (size, size), 0)
    col = lax.broadcasted_iota(jnp.int32, (size, size), 1)
    diag = jnp.where(row == col, 1.5, 0.0)
    corr = gath[...].reshape(size, size)
    scale = jnp.sqrt(jnp.sum(corr * corr) + 1e-06)
    scaled = corr / scale
    factor = diag - 0.5 * scaled
    z_ref[...] = factor
    y_ref[...] = dot3(split(factor), split(scaled))

    def step(k, carry):
        y = split(y_ref[...])
        z = split(z_ref[...])
        factor = split(diag - 0.5 * dot3(z, y))
        y_ref[...] = dot3(factor, y)
        z_ref[...] = dot3(factor, z)
        return carry

    lax.fori_loop(1, NS_STEPS - 1, step, 0)
    y = split(y_ref[...])
    z = split(z_ref[...])
    factor = split(diag - 0.5 * dot3(z, y))
    t_ref[...] = dot3(factor, z) / jnp.sqrt(scale)
    for i in range(outer):
        for j in range(inner):
            trans_ref[pl.ds((j * outer + i) * width, width), :] = t_ref[
                pl.ds((i * inner + j) * width, width), :
            ]
    trans = split(trans_ref[...])
    filt = filt_ref[...]
    out_ref[...] = (dot(trans[0], filt) + dot(trans[1], filt)).astype(jnp.bfloat16)


def project_kernel(
    bits, cell_volume, filt_ref, applied_ref, trans_ref, proj_ref,
    total, send, recv, gath, send_sem, recv_sem,
):
    gram_sum(bits, cell_volume, filt_ref, applied_ref, total, send, recv, gath, send_sem, recv_sem)
    size = filt_ref.shape[0]
    trans = split(trans_ref[...])
    half = split(dot3(trans, split(gath[...].reshape(size, size))))
    contract = (((1,), (1,)), ((), ()))

    def dot_t(a, b):
        return lax.dot_general(a, b, contract, preferred_element_type=jnp.float32)

    proj_ref[...] = dot_t(half[0], trans[0]) + (
        dot_t(half[0], trans[1]) + dot_t(half[1], trans[0])
    )


def sum_call(kernel, operands, out_shape, squares, bits, number, flops):
    size = operands[0].shape[0]
    vmem = pl.BlockSpec(memory_space=pltpu.VMEM)
    room = size // 2 + TILE_ROWS * len(bits[0])
    sems = pltpu.SemaphoreType.DMA((2, 2 * len(bits[0])))
    halves = pltpu.VMEM((2, size // 2, size), jnp.float32)
    stage = pltpu.VMEM((2, room, size), jnp.float32)
    return pl.pallas_call(
        kernel,
        out_shape=out_shape,
        in_specs=[vmem] * len(operands),
        out_specs=jax.tree.map(lambda _: vmem, out_shape),
        scratch_shapes=[halves, stage, stage, halves]
        + [pltpu.VMEM((size, size), jnp.float32)] * squares
        + [sems, sems],
        cost_estimate=pl.CostEstimate(flops=flops, bytes_accessed=8 << 20, transcendentals=0),
        compiler_params=pltpu.CompilerParams(
            vmem_limit_bytes=32 << 20, collective_id=number, has_side_effects=True
        ),
    )(*operands)


def device_of(position, groups):
    return {"dom": position // groups, "band": lax.rem(position, groups)}


def remote(source, target, send_sem, recv_sem, device):
    return pltpu.make_async_remote_copy(
        src_ref=source,
        dst_ref=target,
        send_sem=send_sem,
        recv_sem=recv_sem,
        device_id=device,
        device_id_type=pl.DeviceIdType.MESH,
    )


def signal_all(devices, groups, me):
    barrier = pltpu.get_barrier_semaphore()

    def greet(r, carry):
        pl.semaphore_signal(
            barrier,
            inc=1,
            device_id=device_of(lax.rem(me + r, devices), groups),
            device_id_type=pl.DeviceIdType.MESH,
        )
        return carry

    lax.fori_loop(1, devices, greet, 0)
    pl.semaphore_wait(barrier, devices - 1)


def lane_orders(perm, back):
    size = perm.shape[0]
    high = size // LANES
    row = lax.broadcasted_iota(jnp.int32, (size, size), 0)
    col = lax.broadcasted_iota(jnp.int32, (size, size), 1)
    grouped = lax.rem(row // GRID_Z, high) * LANES + lax.rem(row, GRID_Z) * high + row // LANES
    perm[...] = jnp.where(grouped == col, 1.0, 0.0).astype(jnp.bfloat16)
    natural = lax.rem(row, high) * LANES + row // LANES * GRID_Z + lax.rem(row // high, GRID_Z)
    back[...] = jnp.where(natural == col, 1.0, 0.0).astype(jnp.bfloat16)


def exchange_filter(
    groups, bounds_ref, sent_ref, pot_ref, filt_ref, applied_ref,
    stage, pots, perm, back, field, diag, send_f, send_a, in_send, in_recv, pot_send, pot_recv, out_send, out_recv,
):
    doms, slab, mine, width = stage.shape
    devices = doms * groups
    dom = lax.axis_index("dom")
    band = lax.axis_index("band")
    me = dom * groups + band
    planes = doms * slab
    part = min(mine, 8)
    chunks = mine // part
    rows = planes * part
    lanes = width // groups
    levels = width // LANES
    high = LANES // GRID_Z
    spans = levels // high
    half_width = (bounds_ref[1] - bounds_ref[0]) / 2.0
    centre = (bounds_ref[1] + bounds_ref[0]) / 2.0
    inv_half = 1.0 / half_width

    signal_all(devices, groups, me)

    def incoming(c, r):
        peer = lax.rem(dom + r, doms)
        some = pl.ds(c * part, part)
        source, target = sent_ref.at[peer, :, some, :], stage.at[dom, :, some, :]
        if r == 0:
            return pltpu.make_async_copy(source, target, in_recv.at[c, r])
        return remote(source, target, in_send.at[c, r], in_recv.at[c, r], {"dom": peer})

    def potential(r):
        if r == 0:
            return pltpu.make_async_copy(pot_ref, pots.at[dom], pot_recv.at[r])
        return remote(pot_ref, pots.at[dom], pot_send.at[r], pot_recv.at[r], {"dom": lax.rem(dom + r, doms)})

    for r in range(doms):
        potential(r).start()
    for c in range(chunks):
        for r in range(doms):
            incoming(c, r).start()

    lane_orders(perm, back)
    lane = lax.broadcasted_iota(jnp.int32, (rows, LANES), 1)
    first_high = lax.rem(lane, high) == 0
    last_high = lax.rem(lane, high) == high - 1

    for r in range(doms):
        potential(r).wait()
    for k in range(spans):
        pot = jnp.concatenate(
            [pots[:, :, pl.ds((h * spans + k) * LANES, LANES)].reshape(planes, LANES) for h in range(high)], axis=1
        )
        ordered = jnp.zeros(pot.shape, jnp.float32)
        for piece in range(3):
            top = pot.astype(jnp.bfloat16)
            ordered = ordered + dot(top, perm[...])
            pot = pot - top.astype(jnp.float32)
        scaled = (3.0 + ordered - centre) * (2.0 * inv_half)
        for b in range(high):
            line = scaled[:, b * LANES : (b + 1) * LANES]
            diag[k * high + b] = jnp.broadcast_to(line[:, None, :], (planes, part, LANES)).reshape(rows, LANES)

    def edges(slot):
        top = field[slot, levels]
        field[slot, 0] = jnp.where(
            first_high, pltpu.roll(top, LANES - (high - 1), 1), pltpu.roll(top, 1, 1)
        )
        low = field[slot, 1]
        field[slot, levels + 1] = jnp.where(
            last_high, pltpu.roll(low, high - 1, 1), pltpu.roll(low, LANES - 1, 1)
        )

    def image(slot, i):
        v = field[slot, i]
        around = pltpu.roll(v, high, 1) + pltpu.roll(v, LANES - high, 1)
        around = around + (field[slot, i - 1] + field[slot, i + 1])
        around = around + (
            jnp.concatenate([v[part:], v[:part]], axis=0) + jnp.concatenate([v[rows - part :], v[: rows - part]], axis=0)
        )
        return diag[i - 1] * v - inv_half * around, v

    def outgoing(source, target, which, c, r):
        position = lax.rem(me + r, devices)
        device = device_of(position, groups)
        piece = source.at[
            pl.ds(device["dom"] * slab, slab),
            pl.ds(c * part, part),
            pl.ds(pl.multiple_of(device["band"] * lanes, LANES), lanes),
        ]
        row = pl.multiple_of((band * doms + dom) * mine + c * part, part)
        place = target.at[:, pl.ds(row, part), :]
        return piece, place, out_send.at[which, c, r], out_recv.at[which, c, r], device

    def send_out(source, target, which, c):
        piece, place, _, sem, _ = outgoing(source, target, which, c, 0)
        pltpu.make_async_copy(piece, place, sem).start()

        def run(r, carry):
            remote(*outgoing(source, target, which, c, r)).start()
            return carry

        lax.fori_loop(1, devices, run, 0)

    def wait_out(source, target, which, c):
        piece, place, _, sem, _ = outgoing(source, target, which, c, 0)
        pltpu.make_async_copy(piece, place, sem).wait()

        def run(r, carry):
            remote(*outgoing(source, target, which, c, r)).wait()
            return carry

        lax.fori_loop(1, devices, run, 0)

    for c in range(chunks):
        for r in range(doms):
            incoming(c, r).wait()
        some = pl.ds(c * part, part)
        for k in range(spans):
            cells = jnp.concatenate(
                [
                    stage[:, :, some, pl.ds((h * spans + k) * LANES, LANES)].astype(jnp.float32).reshape(rows, LANES)
                    for h in range(high)
                ],
                axis=1,
            )
            ordered = dot(cells.astype(jnp.bfloat16), perm[...])
            for b in range(high):
                field[0, 1 + k * high + b] = ordered[:, b * LANES : (b + 1) * LANES]
        edges(0)

        def first(i, carry):
            field[1, i] = 0.5 * image(0, i)[0]
            return carry

        lax.fori_loop(1, levels + 1, first, 0)
        edges(1)

        def middle(k, carry):
            slot = lax.rem(k, 2)

            def run(i, inner):
                field[1 - slot, i] = image(slot, i)[0] - field[1 - slot, i]
                return inner

            lax.fori_loop(1, levels + 1, run, 0)
            edges(1 - slot)
            return carry

        lax.fori_loop(1, DEG, middle, 0)
        slot = DEG % 2

        def restore(values, target, k):
            natural = dot(jnp.concatenate(values, axis=1).astype(jnp.bfloat16), back[...])
            for h in range(high):
                target[:, some, pl.ds((h * spans + k) * LANES, LANES)] = (
                    natural[:, h * LANES : (h + 1) * LANES].reshape(planes, part, LANES).astype(jnp.bfloat16)
                )

        for k in range(spans):
            restore([field[slot, 1 + k * high + b] for b in range(high)], send_f, k)
        send_out(send_f, filt_ref, 0, c)
        for k in range(spans):
            values = []
            for b in range(high):
                twice, v = image(slot, 1 + k * high + b)
                values.append((0.5 * half_width) * twice + centre * v)
            restore(values, send_a, k)
    for c in range(chunks):
        send_out(send_a, applied_ref, 1, c)
    for c in range(chunks):
        wait_out(send_f, filt_ref, 0, c)
        wait_out(send_a, applied_ref, 1, c)


def exchange_filter_call(sent, potential, bounds, groups):
    doms, slab, mine, width = sent.shape
    devices = doms * groups
    planes = doms * slab
    part = min(mine, 8)
    chunks = mine // part
    levels = width // LANES
    lanes = width // groups
    size = LANES * (LANES // GRID_Z)
    out = jax.ShapeDtypeStruct((slab, devices * mine, lanes), jnp.bfloat16)
    vmem = pl.BlockSpec(memory_space=pltpu.VMEM)
    hbm = pl.BlockSpec(memory_space=pl.ANY)
    whole = pltpu.VMEM((planes, mine, width), jnp.bfloat16)
    order = pltpu.VMEM((size, size), jnp.bfloat16)
    dma = pltpu.SemaphoreType.DMA
    return pl.pallas_call(
        functools.partial(exchange_filter, groups),
        out_shape=(out, out),
        in_specs=[pl.BlockSpec(memory_space=pltpu.SMEM), hbm, vmem],
        out_specs=(vmem, vmem),
        scratch_shapes=[
            pltpu.VMEM(sent.shape, jnp.bfloat16),
            pltpu.VMEM((doms, slab, width), jnp.float32),
            order,
            order,
            pltpu.VMEM((2, levels + 2, planes * part, LANES), jnp.float32),
            pltpu.VMEM((levels, planes * part, LANES), jnp.float32),
            whole,
            whole,
            dma((chunks, doms)),
            dma((chunks, doms)),
            dma((doms,)),
            dma((doms,)),
            dma((2, chunks, devices)),
            dma((2, chunks, devices)),
        ],
        compiler_params=pltpu.CompilerParams(vmem_limit_bytes=40 << 20, collective_id=2, has_side_effects=True),
    )(bounds, sent, potential)


def body_plain(orbitals, potential, bounds):
    bands, slab, width = orbitals.shape
    doms = lax.axis_size("dom")
    groups = lax.axis_size("band")
    devices = doms * groups
    total_bands = bands * groups
    mine = bands // doms
    everyone = ("dom", "band")
    half_width = (bounds[1] - bounds[0]) / 2.0
    centre = (bounds[1] + bounds[0]) / 2.0
    cell_volume = 1.0 / (slab * doms * width)

    sent = orbitals.reshape(doms, mine, slab, width).transpose(0, 2, 1, 3)
    cells = lax.all_to_all(sent, "dom", split_axis=0, concat_axis=0, tiled=True)
    cells = cells.reshape(doms * slab, mine, width)
    pot = lax.all_to_all(
        jnp.broadcast_to(potential, (doms, slab, width)), "dom", split_axis=0, concat_axis=0, tiled=True
    ).reshape(doms * slab, 1, width)
    filt, applied = filter_bands(cells, pot, jnp.stack([1.0 / half_width, centre]), devices)
    filt = lax.all_to_all(filt, everyone, split_axis=0, concat_axis=0, tiled=True)
    applied = lax.all_to_all(applied, everyone, split_axis=0, concat_axis=0, tiled=True)
    filt = filt.reshape(total_bands, -1)
    applied = applied.reshape(total_bands, -1)
    bits = exchange_bits(doms, groups)
    square = jax.ShapeDtypeStruct((total_bands, total_bands), jnp.float32)
    rotated, trans = sum_call(
        functools.partial(orthonormal_kernel, bits, cell_volume, (doms, groups, mine)),
        (filt,),
        (jax.ShapeDtypeStruct(filt.shape, jnp.bfloat16), square),
        3,
        bits,
        0,
        40 * total_bands**3,
    )
    out = lax.all_to_all(rotated, "band", split_axis=0, concat_axis=1, tiled=True)
    projected = sum_call(
        functools.partial(project_kernel, bits, cell_volume),
        (filt, applied, trans),
        square,
        0,
        bits,
        1,
        40 * total_bands**3,
    )
    return out.reshape(bands, slab, width), projected


def body(orbitals, potential, bounds):
    bands, slab, width = orbitals.shape
    doms = lax.axis_size("dom")
    groups = lax.axis_size("band")
    mine = bands // doms
    if mine % 8 or width % (groups * LANES):
        return body_plain(orbitals, potential, bounds)
    total_bands = bands * groups
    cell_volume = 1.0 / (slab * doms * width)
    sent = orbitals.reshape(doms, mine, slab, width).transpose(0, 2, 1, 3)
    filt, applied = exchange_filter_call(sent, potential, bounds, groups)
    filt = filt.transpose(1, 0, 2).reshape(total_bands, -1)
    applied = applied.transpose(1, 0, 2).reshape(total_bands, -1)
    bits = exchange_bits(doms, groups)
    square = jax.ShapeDtypeStruct((total_bands, total_bands), jnp.float32)
    rotated, trans = sum_call(
        functools.partial(orthonormal_kernel, bits, cell_volume, (1, 1, total_bands)),
        (filt,),
        (jax.ShapeDtypeStruct(filt.shape, jnp.bfloat16), square),
        3,
        bits,
        0,
        40 * total_bands**3,
    )
    out = lax.all_to_all(rotated, "band", split_axis=0, concat_axis=1, tiled=True)
    out = out.reshape(bands, groups, slab, width // groups).transpose(0, 2, 1, 3)
    projected = sum_call(
        functools.partial(project_kernel, bits, cell_volume),
        (filt, applied, trans),
        square,
        0,
        bits,
        1,
        40 * total_bands**3,
    )
    return out.reshape(bands, slab, width), projected


def solution(mesh):
    return jax.shard_map(
        body,
        mesh=mesh,
        in_specs=(P("band", "dom", None), P("dom", None), P()),
        out_specs=(P("band", "dom", None), P()),
        check_vma=False,
    )
```

```python
import functools

import jax
import jax.numpy as jnp
from jax import lax
from jax.experimental import pallas as pl
from jax.experimental.pallas import tpu as pltpu
from jax.sharding import PartitionSpec as P

GRID_Z = 32
DEG = 8
NS_STEPS = 8
LANES = 128
UNROLL = 8
PAUSE = 2
TILE_ROWS = 8


def filter_kernel(scal_ref, cells_ref, pot_ref, sums_ref, filt_ref, applied_ref, field, high, low, coef):
    planes, bands, width = cells_ref.shape
    rows = planes * bands
    blocks_per_plane = filt_ref.shape[0] // planes
    block = filt_ref.shape[2]
    tile = sums_ref.shape[1]
    inv_half = scal_ref[0]
    centre = scal_ref[1]

    for x in range(planes):
        mine = pl.ds(x * bands, bands)
        coef[mine, :] = jnp.broadcast_to(3.0 + pot_ref[x], (bands, width))
        start = cells_ref[x].astype(jnp.float32)
        field[0, mine, :] = start
    for c in range(width // tile):
        cols = pl.ds(c * tile, tile)
        start = field[0, :, cols]
        high[0, :, cols] = start.astype(jnp.bfloat16)
        low[0, :, cols] = jnp.zeros((rows, tile), jnp.bfloat16)

    def shifted(v, by):
        if bands % 8 == 0:
            return jnp.concatenate([v[by:], v[:by]], axis=0)
        return pltpu.roll(v, (rows - by) % rows, 0)

    def neighbours(slot, c, v):
        cols = pl.ds(pl.multiple_of(c * tile, tile), tile)
        left = pl.ds(pl.multiple_of(lax.rem(c * tile + width - LANES, width), LANES), LANES)
        right = pl.ds(pl.multiple_of(lax.rem(c * tile + tile, width), LANES), LANES)

        def part(ref):
            wide = jnp.concatenate([ref[slot, :, left], ref[slot, :, cols], ref[slot, :, right]], axis=1)
            return dot(wide, sums_ref[...])

        return part(high) + part(low) + (shifted(v, bands) + shifted(v, rows - bands))

    def sweep(slot, other, weight, diagonal, first):
        def run(c, carry):
            cols = pl.ds(pl.multiple_of(c * tile, tile), tile)
            v = field[slot, :, cols]
            fresh = weight * neighbours(slot, c, v) + (coef[:, cols] * diagonal[0] + diagonal[1]) * v
            if not first:
                fresh = fresh - field[other, :, cols]
            field[other, :, cols] = fresh
            top, rest = split(fresh)
            high[other, :, cols] = top
            low[other, :, cols] = rest
            return carry

        lax.fori_loop(0, width // tile, run, 0)

    sweep(0, 1, -0.5 * inv_half, (inv_half, -centre * inv_half), True)

    def middle(k, carry):
        slot = lax.rem(k, 2)
        sweep(slot, 1 - slot, -inv_half, (2.0 * inv_half, -2.0 * centre * inv_half), False)
        return carry

    lax.fori_loop(1, DEG, middle, 0)
    slot = DEG % 2
    for c in range(width // tile):
        cols = pl.ds(c * tile, tile)
        v = field[slot, :, cols]
        applied = coef[:, cols] * v - 0.5 * neighbours(slot, c, v)
        piece, inner = divmod(c * tile, block)
        for x in range(planes):
            where = (x * blocks_per_plane + piece, slice(None), pl.ds(inner, tile))
            filt_ref[where] = v[x * bands : (x + 1) * bands].astype(jnp.bfloat16)
            applied_ref[where] = applied[x * bands : (x + 1) * bands].astype(jnp.bfloat16)


def neighbour_sums(tile):
    source = lax.broadcasted_iota(jnp.int32, (tile + 2 * LANES, tile), 0) - LANES
    target = lax.broadcasted_iota(jnp.int32, (tile + 2 * LANES, tile), 1)
    step = source - target
    same_row = (source >= 0) & (source // GRID_Z == target // GRID_Z)
    apart = lax.rem(step + GRID_Z, GRID_Z)
    beside_z = same_row & ((apart == 1) | (apart == GRID_Z - 1))
    beside_y = (step == GRID_Z) | (step == -GRID_Z)
    return (beside_z | beside_y).astype(jnp.bfloat16)


def filter_bands(cells, potential, scalars, devices):
    planes, bands, width = cells.shape
    rows = planes * bands
    block = planes * width // devices
    out = jax.ShapeDtypeStruct((devices, bands, block), jnp.bfloat16)
    vmem = pl.BlockSpec(memory_space=pltpu.VMEM)
    return pl.pallas_call(
        filter_kernel,
        out_shape=(out, out),
        in_specs=[pl.BlockSpec(memory_space=pltpu.SMEM), vmem, vmem, vmem],
        out_specs=(vmem, vmem),
        scratch_shapes=[
            pltpu.VMEM((2, rows, width), jnp.float32),
            pltpu.VMEM((2, rows, width), jnp.bfloat16),
            pltpu.VMEM((2, rows, width), jnp.bfloat16),
            pltpu.VMEM((rows, width), jnp.float32),
        ],
        compiler_params=pltpu.CompilerParams(vmem_limit_bytes=48 << 20),
    )(scalars, cells, potential, neighbour_sums(min(256, block)))


def split(value):
    spread = value * 65537.0
    high = spread - (spread - value)
    return high.astype(jnp.bfloat16), (value - high).astype(jnp.bfloat16)


def dot(a, b):
    return jnp.dot(a, b, preferred_element_type=jnp.float32)


def dot3(a, b):
    (a_high, a_low), (b_high, b_low) = a, b
    return dot(a_high, b_high) + (dot(a_high, b_low) + dot(a_low, b_high))


def exchange_bits(doms, groups):
    dom = [("dom", 1 << i) for i in range(1, (doms - 1).bit_length())]
    band = [("band", 1 << i) for i in range((groups - 1).bit_length())]
    core = [("dom", 1)]
    return core + band[:1] + dom + band[1:], core + dom + band


def gram_sum(bits, cell_volume, filt_ref, other_ref, total, send, recv, gath, send_sem, recv_sem):
    size = filt_ref.shape[0] // 2
    index = {axis: lax.axis_index(axis) for axis in ("dom", "band")}

    def partner(axis, bit):
        mine = lax.rem(index[axis] // bit, 2)
        return mine, {axis: index[axis] + bit - 2 * bit * mine}

    barrier = pltpu.get_barrier_semaphore()
    for axis, bit in bits[0]:
        pl.semaphore_signal(
            barrier, inc=1, device_id=partner(axis, bit)[1], device_id_type=pl.DeviceIdType.MESH
        )

    pairs = (((1,), (1,)), ((), ()))
    for stream in range(2):
        total[stream] = cell_volume * lax.dot_general(
            filt_ref[pl.ds(stream * size, size), :],
            other_ref[...],
            pairs,
            preferred_element_type=jnp.float32,
        )
    pl.semaphore_wait(barrier, len(bits[0]))

    def copy(stream, number, source, target, device):
        made = pltpu.make_async_remote_copy(
            src_ref=source,
            dst_ref=target,
            send_sem=send_sem.at[stream, number],
            recv_sem=recv_sem.at[stream, number],
            device_id=device,
            device_id_type=pl.DeviceIdType.MESH,
        )
        made.start()
        return made

    stages = len(bits[0])
    start = [jnp.int32(0)] * 2
    halved = [[], []]
    length, offset = size, 0
    for stage in range(stages):
        halve = length >= 2 * TILE_ROWS
        count = length // 2 if halve else length
        space = pl.ds(offset, count)
        flight = []
        for stream in range(2):
            axis, bit = bits[stream][stage]
            mine, device = partner(axis, bit)
            give = start[stream] + (1 - mine) * count if halve else start[stream]
            keep = start[stream] + mine * count if halve else start[stream]
            give = pl.multiple_of(give, TILE_ROWS)
            send[stream, space, :] = total[stream, pl.ds(give, count), :]
            flight.append(
                copy(stream, stage, send.at[stream, space], recv.at[stream, space], device)
            )
            start[stream] = pl.multiple_of(keep, TILE_ROWS)
            if halve:
                halved[stream].append((stage, mine, device))
        for stream in range(2):
            flight[stream].wait()
            kept = pl.ds(start[stream], count)
            if halve:
                own = total[stream, kept, :]
            else:
                own = send[stream, space, :]
            total[stream, kept, :] = own + recv[stream, space, :]
        length = count
        offset += count

    for stream in range(2):
        kept = pl.ds(start[stream], length)
        gath[stream, kept, :] = total[stream, kept, :]
    for back in range(len(halved[0]) - 1, -1, -1):
        flight = []
        for stream in range(2):
            stage, mine, device = halved[stream][back]
            area = gath.at[stream, pl.ds(start[stream], length)]
            flight.append(copy(stream, stages + stage, area, area, device))
            start[stream] = pl.multiple_of(start[stream] - mine * length, TILE_ROWS)
        for made in flight:
            made.wait()
        length *= 2


def orthonormal_kernel(
    bits, cell_volume, groups, filt_ref, out_ref, trans_ref,
    total, send, recv, gath, y_ref, z_ref, t_ref, send_sem, recv_sem,
):
    gram_sum(bits, cell_volume, filt_ref, filt_ref, total, send, recv, gath, send_sem, recv_sem)
    size = filt_ref.shape[0]
    outer, inner, width = groups
    row = lax.broadcasted_iota(jnp.int32, (size, size), 0)
    col = lax.broadcasted_iota(jnp.int32, (size, size), 1)
    diag = jnp.where(row == col, 1.5, 0.0)
    corr = gath[...].reshape(size, size)
    scale = jnp.sqrt(jnp.sum(corr * corr) + 1e-06)
    scaled = corr / scale
    factor = diag - 0.5 * scaled
    z_ref[...] = factor
    y_ref[...] = dot3(split(factor), split(scaled))

    def step(k, carry):
        y = split(y_ref[...])
        z = split(z_ref[...])
        factor = split(diag - 0.5 * dot3(z, y))
        y_ref[...] = dot3(factor, y)
        z_ref[...] = dot3(factor, z)
        return carry

    lax.fori_loop(1, NS_STEPS - 1, step, 0)
    y = split(y_ref[...])
    z = split(z_ref[...])
    factor = split(diag - 0.5 * dot3(z, y))
    t_ref[...] = dot3(factor, z) / jnp.sqrt(scale)
    for i in range(outer):
        for j in range(inner):
            trans_ref[pl.ds((j * outer + i) * width, width), :] = t_ref[
                pl.ds((i * inner + j) * width, width), :
            ]
    trans = split(trans_ref[...])
    filt = filt_ref[...]
    out_ref[...] = (dot(trans[0], filt) + dot(trans[1], filt)).astype(jnp.bfloat16)


def project_kernel(
    bits, cell_volume, filt_ref, applied_ref, trans_ref, proj_ref,
    total, send, recv, gath, send_sem, recv_sem,
):
    gram_sum(bits, cell_volume, filt_ref, applied_ref, total, send, recv, gath, send_sem, recv_sem)
    size = filt_ref.shape[0]
    trans = split(trans_ref[...])
    half = split(dot3(trans, split(gath[...].reshape(size, size))))
    contract = (((1,), (1,)), ((), ()))

    def dot_t(a, b):
        return lax.dot_general(a, b, contract, preferred_element_type=jnp.float32)

    proj_ref[...] = dot_t(half[0], trans[0]) + (
        dot_t(half[0], trans[1]) + dot_t(half[1], trans[0])
    )


def sum_call(kernel, operands, out_shape, squares, bits, number, flops):
    size = operands[0].shape[0]
    vmem = pl.BlockSpec(memory_space=pltpu.VMEM)
    room = size // 2 + TILE_ROWS * len(bits[0])
    sems = pltpu.SemaphoreType.DMA((2, 2 * len(bits[0])))
    halves = pltpu.VMEM((2, size // 2, size), jnp.float32)
    stage = pltpu.VMEM((2, room, size), jnp.float32)
    return pl.pallas_call(
        kernel,
        out_shape=out_shape,
        in_specs=[vmem] * len(operands),
        out_specs=jax.tree.map(lambda _: vmem, out_shape),
        scratch_shapes=[halves, stage, stage, halves]
        + [pltpu.VMEM((size, size), jnp.float32)] * squares
        + [sems, sems],
        cost_estimate=pl.CostEstimate(flops=flops, bytes_accessed=8 << 20, transcendentals=0),
        compiler_params=pltpu.CompilerParams(
            vmem_limit_bytes=32 << 20, collective_id=number, has_side_effects=True
        ),
    )(*operands)


def peers(doms, groups):
    dom = lax.axis_index("dom")
    band = lax.axis_index("band")
    rows = [lax.rem(dom + r, doms) for r in range(doms)]
    columns = [lax.rem(band + r, groups) for r in range(groups)]
    return [{"dom": d, "band": b} for b in columns for d in rows]


def remote(source, target, send_sem, recv_sem, device):
    return pltpu.make_async_remote_copy(
        src_ref=source,
        dst_ref=target,
        send_sem=send_sem,
        recv_sem=recv_sem,
        device_id=device,
        device_id_type=pl.DeviceIdType.MESH,
    )


def greet(others):
    barrier = pltpu.get_barrier_semaphore()
    for other in others:
        pl.semaphore_signal(barrier, inc=1, device_id=other, device_id_type=pl.DeviceIdType.MESH)
    pl.semaphore_wait(barrier, len(others))


def lane_orders(perm, back):
    size = perm.shape[0]
    high = size // LANES
    row = lax.broadcasted_iota(jnp.int32, (size, size), 0)
    col = lax.broadcasted_iota(jnp.int32, (size, size), 1)
    grouped = lax.rem(row // GRID_Z, high) * LANES + lax.rem(row, GRID_Z) * high + row // LANES
    perm[...] = jnp.where(grouped == col, 1.0, 0.0).astype(jnp.bfloat16)
    natural = lax.rem(row, high) * LANES + row // LANES * GRID_Z + lax.rem(row // high, GRID_Z)
    back[...] = jnp.where(natural == col, 1.0, 0.0).astype(jnp.bfloat16)


class BlockSum:
    def __init__(self, total, recv, gath, send_sem, recv_sem, levels):
        self.total, self.recv, self.gath = total, recv, gath
        self.send_sem, self.recv_sem, self.levels = send_sem, recv_sem, levels
        self.start, self.length = jnp.int32(0), total.shape[0]
        self.offset, self.copies = 0, []

    def steps(self):
        for level in range(len(self.levels)):
            yield functools.partial(self.scatter, level)
            yield functools.partial(self.add, level)
        for level in range(len(self.levels) - 1, -1, -1):
            yield functools.partial(self.gather, level)
            yield functools.partial(self.join, level)

    def scatter(self, level):
        at, size, device = self.levels[level]
        rows = self.length // size
        self.copies = []
        for r in range(1, size):
            to = lax.rem(at + r, size)
            source = pl.ds(pl.multiple_of(self.start + to * rows, TILE_ROWS), rows)
            place = pl.ds(self.offset + (r - 1) * rows, rows)
            self.copies.append(
                remote(
                    self.total.at[source], self.recv.at[place],
                    self.send_sem.at[0, level, r], self.recv_sem.at[0, level, r], device(to),
                )
            )
        for made in self.copies:
            made.start()

    def add(self, level):
        at, size, _ = self.levels[level]
        rows = self.length // size
        self.start = pl.multiple_of(self.start + at * rows, TILE_ROWS)
        self.length = rows
        kept = pl.ds(self.start, rows)
        for made in self.copies:
            made.wait()
        value = self.total[kept]
        for r in range(1, size):
            value = value + self.recv[pl.ds(self.offset + (r - 1) * rows, rows)]
        self.offset += (size - 1) * rows
        self.total[kept] = value
        if level == len(self.levels) - 1:
            self.gath[kept] = value

    def gather(self, level):
        at, size, device = self.levels[level]
        area = self.gath.at[pl.ds(self.start, self.length)]
        self.copies = [
            remote(area, area, self.send_sem.at[1, level, r], self.recv_sem.at[1, level, r], device(lax.rem(at + r, size)))
            for r in range(1, size)
        ]
        for made in self.copies:
            made.start()

    def join(self, level):
        at, size, _ = self.levels[level]
        for made in self.copies:
            made.wait()
        self.start = pl.multiple_of(self.start - at * self.length, TILE_ROWS)
        self.length *= size


def sum_levels(doms, groups):
    dom = lax.axis_index("dom")
    band = lax.axis_index("band")
    core, chip = lax.rem(dom, 2), dom // 2
    low, high = lax.rem(band, 2), band // 2
    return [
        (core, 2, lambda to: {"dom": chip * 2 + to}),
        (chip * 2 + low, doms, lambda to: {"dom": to // 2 * 2 + core, "band": high * 2 + lax.rem(to, 2)}),
        (high, groups // 2, lambda to: {"band": to * 2 + low}),
    ]


def upper_blocks(total):
    count = total // LANES
    return [(i, j) for i in range(count) for j in range(i, count)]


def gram(cell_volume, left, right, packed):
    slab, total, _ = left.shape
    size = 2 * LANES
    where = {pair: n for n, pair in enumerate(upper_blocks(total))}
    for i in range(total // size):
        for j in range(i, total // size):
            block = jnp.zeros((size, size), jnp.float32)
            for x in range(slab):
                block = block + lax.dot_general(
                    left[x, pl.ds(i * size, size), :],
                    right[x, pl.ds(j * size, size), :],
                    (((1,), (1,)), ((), ())),
                    preferred_element_type=jnp.float32,
                )
            block = block * cell_volume
            for a in range(2):
                for b in range(2):
                    pair = (2 * i + a, 2 * j + b)
                    if pair in where:
                        packed[pl.ds(where[pair] * LANES, LANES)] = block[
                            a * LANES : (a + 1) * LANES, b * LANES : (b + 1) * LANES
                        ]


def unpack(packed, full):
    for n, (i, j) in enumerate(upper_blocks(full.shape[0])):
        block = packed[pl.ds(n * LANES, LANES)]
        full[pl.ds(i * LANES, LANES), pl.ds(j * LANES, LANES)] = block
        if i != j:
            full[pl.ds(j * LANES, LANES), pl.ds(i * LANES, LANES)] = block.T


def split_rounding(value):
    high = value.astype(jnp.bfloat16)
    return high, (value - high.astype(jnp.float32)).astype(jnp.bfloat16)


def inverse_root(full, work, other, pause):
    size = full.shape[0]
    row = lax.broadcasted_iota(jnp.int32, (size, size), 0)
    col = lax.broadcasted_iota(jnp.int32, (size, size), 1)

    def diagonal(value):
        return jnp.where(row == col, value, 0.0)

    corr = full[...]
    scale = jnp.sqrt(jnp.sum(corr * corr) + 1e-06)
    work[...] = corr / scale
    for double in range(NS_STEPS // 2 - 1):
        held = split_rounding(work[...])
        other[...] = dot3(held, held)
        pause()
        square = other[...]
        rest = dot3(split_rounding(square), split_rounding(0.0625 * square - 0.5625 * work[...]))
        factor = split_rounding(diagonal(2.25) - 2.4375 * work[...] + (1.6875 * square + rest))
        pause()
        if double == 0:
            full[...] = factor[0].astype(jnp.float32) + factor[1].astype(jnp.float32)
        else:
            full[...] = dot3(split_rounding(full[...]), factor)
            pause()
        other[...] = dot3(held, factor)
        pause()
        work[...] = dot3(split_rounding(other[...]), factor)
        pause()
    left = diagonal(1.0) - work[...]
    rounded = left.astype(jnp.bfloat16)
    square = dot(rounded, rounded)
    rest = 0.5 * left + 0.375 * square
    rest = rest + dot(square.astype(jnp.bfloat16), (0.3125 * left + 0.0625 * square).astype(jnp.bfloat16))
    pause()
    value = full[...]
    value = value + dot(value.astype(jnp.bfloat16), rest.astype(jnp.bfloat16))
    return value / jnp.sqrt(scale)


def step_kernel(
    groups, cell_volume, bounds_ref, sent_ref, pot_ref, out_ref, proj_ref,
    filt_ref, applied_ref, stage, pots, perm, back, even, odd, diag, send_f, send_a,
    corr_sum, corr_recv, corr_gath, hamil_sum, hamil_recv, hamil_gath, full, work, other, trans, spread, turned,
    in_send, in_recv, pot_send, pot_recv, out_send, out_recv, corr_send, corr_arrive, hamil_send, hamil_arrive, back_send, back_recv,
):
    doms, slab, mine, width = stage.shape
    devices = doms * groups
    dom = lax.axis_index("dom")
    band = lax.axis_index("band")
    planes = doms * slab
    part = min(mine, 8)
    chunks = mine // part
    rows = planes * part
    lanes = width // groups
    levels = width // LANES
    high = LANES // GRID_Z
    spans = levels // high
    half_width = (bounds_ref[1] - bounds_ref[0]) / 2.0
    centre = (bounds_ref[1] + bounds_ref[0]) / 2.0
    inv_half = 1.0 / half_width

    everyone = peers(doms, groups)
    greet(everyone[1:])

    def incoming(c, r):
        peer = lax.rem(dom + r, doms)
        some = pl.ds(c * part, part)
        source, target = sent_ref.at[peer, :, some, :], stage.at[dom, :, some, :]
        if r == 0:
            return pltpu.make_async_copy(source, target, in_recv.at[c, r])
        return remote(source, target, in_send.at[c, r], in_recv.at[c, r], {"dom": peer})

    def potential(r):
        if r == 0:
            return pltpu.make_async_copy(pot_ref, pots.at[dom], pot_recv.at[r])
        return remote(pot_ref, pots.at[dom], pot_send.at[r], pot_recv.at[r], {"dom": lax.rem(dom + r, doms)})

    for r in range(doms):
        potential(r).start()
    for c in range(chunks):
        for r in range(doms):
            incoming(c, r).start()

    lane_orders(perm, back)
    lane = lax.broadcasted_iota(jnp.int32, (rows, LANES), 1)
    first_high = lax.rem(lane, high) == 0
    last_high = lax.rem(lane, high) == high - 1

    for r in range(doms):
        potential(r).wait()
    for k in range(spans):
        pot = jnp.concatenate(
            [pots[:, :, pl.ds((h * spans + k) * LANES, LANES)].reshape(planes, LANES) for h in range(high)], axis=1
        )
        ordered = jnp.zeros(pot.shape, jnp.float32)
        for piece in range(3):
            top = pot.astype(jnp.bfloat16)
            ordered = ordered + dot(top, perm[...])
            pot = pot - top.astype(jnp.float32)
        scaled = (3.0 + ordered - centre) * (2.0 * inv_half)
        for b in range(high):
            line = scaled[:, b * LANES : (b + 1) * LANES]
            diag[k * high + b] = jnp.broadcast_to(line[:, None, :], (planes, part, LANES)).reshape(rows, LANES)

    def edges(field):
        top = field[levels]
        field[0] = jnp.where(first_high, pltpu.roll(top, LANES - (high - 1), 1), pltpu.roll(top, 1, 1))
        low = field[1]
        field[levels + 1] = jnp.where(last_high, pltpu.roll(low, high - 1, 1), pltpu.roll(low, LANES - 1, 1))

    def image(field, i):
        v = field[i]
        around = pltpu.roll(v, high, 1) + pltpu.roll(v, LANES - high, 1)
        around = around + (field[i - 1] + field[i + 1])
        around = around + (
            jnp.concatenate([v[part:], v[:part]], axis=0) + jnp.concatenate([v[rows - part :], v[: rows - part]], axis=0)
        )
        return diag[i - 1] * v - inv_half * around, v

    def sweep(source, target, first):
        def run(j, carry):
            for i in range(UNROLL):
                i = 1 + j * UNROLL + i
                fresh = image(source, i)[0]
                target[i] = 0.5 * fresh if first else fresh - target[i]
            return carry

        lax.fori_loop(0, levels // UNROLL, run, 0)
        edges(target)

    def outgoing(source, target, which, c):
        copies = []
        row = pl.multiple_of((band * doms + dom) * mine + c * part, part)
        place = target.at[:, pl.ds(row, part), :]
        for r, device in enumerate(everyone):
            piece = source.at[
                pl.ds(device["dom"] * slab, slab),
                pl.ds(c * part, part),
                pl.ds(pl.multiple_of(device["band"] * lanes, LANES), lanes),
            ]
            recv = out_recv.at[which, c, r]
            if r == 0:
                copies.append(pltpu.make_async_copy(piece, place, recv))
            else:
                copies.append(remote(piece, place, out_send.at[which, c, r], recv, device))
        return copies

    def send_out(source, target, which, c):
        for copy in outgoing(source, target, which, c):
            copy.start()

    def wait_out(source, target, which, c):
        for copy in outgoing(source, target, which, c):
            copy.wait()

    for c in range(chunks):
        for r in range(doms):
            incoming(c, r).wait()
        some = pl.ds(c * part, part)
        for k in range(spans):
            cells = jnp.concatenate(
                [
                    stage[:, :, some, pl.ds((h * spans + k) * LANES, LANES)].astype(jnp.float32).reshape(rows, LANES)
                    for h in range(high)
                ],
                axis=1,
            )
            ordered = dot(cells.astype(jnp.bfloat16), perm[...])
            for b in range(high):
                even[1 + k * high + b] = ordered[:, b * LANES : (b + 1) * LANES]
        edges(even)
        sweep(even, odd, True)

        def pair(k, carry):
            sweep(odd, even, False)
            sweep(even, odd, False)
            return carry

        lax.fori_loop(0, (DEG - 1) // 2, pair, 0)
        last = odd
        if DEG % 2 == 0:
            sweep(odd, even, False)
            last = even

        def restore(values, target, k):
            natural = dot(jnp.concatenate(values, axis=1).astype(jnp.bfloat16), back[...])
            for h in range(high):
                target[:, some, pl.ds((h * spans + k) * LANES, LANES)] = (
                    natural[:, h * LANES : (h + 1) * LANES].reshape(planes, part, LANES).astype(jnp.bfloat16)
                )

        for k in range(spans):
            restore([last[1 + k * high + b] for b in range(high)], send_f, k)
        send_out(send_f, filt_ref, 0, c)
        for k in range(spans):
            values = []
            for b in range(high):
                twice, v = image(last, 1 + k * high + b)
                values.append((0.5 * half_width) * twice + centre * v)
            restore(values, send_a, k)
    for c in range(chunks):
        send_out(send_a, applied_ref, 1, c)
    for c in range(chunks):
        wait_out(send_f, filt_ref, 0, c)

    total = filt_ref.shape[1]
    gram(cell_volume, filt_ref, filt_ref, corr_sum)
    corr = BlockSum(corr_sum, corr_recv, corr_gath, corr_send, corr_arrive, sum_levels(doms, groups))
    for step in corr.steps():
        step()
    unpack(corr_gath, full)

    for c in range(chunks):
        wait_out(send_a, applied_ref, 1, c)
    gram(cell_volume, filt_ref, applied_ref, hamil_sum)
    hamil = BlockSum(hamil_sum, hamil_recv, hamil_gath, hamil_send, hamil_arrive, sum_levels(doms, groups))
    pending = list(hamil.steps())
    pending.pop(0)()

    def pause():
        for _ in range(2):
            if len(pending) > 1:
                pending.pop(0)()

    calls = [0]

    def sometimes():
        calls[0] += 1
        if calls[0] % PAUSE == 0:
            pause()

    value = inverse_root(full, work, other, sometimes)
    trans[...] = value
    turn = split_rounding(value.T)

    bands = out_ref.shape[0]
    half = total // 2
    returned = []
    for part_rows in range(2):
        for x in range(slab):
            points = filt_ref[x]
            piece = [t[part_rows * half : (part_rows + 1) * half] for t in turn]
            product = dot(piece[0], points) + dot(piece[1], points)
            for n in range(lanes // LANES):
                spread[n, pl.ds(x, half, stride=slab), :] = product[:, n * LANES : (n + 1) * LANES]
        for n in range(lanes // LANES):
            turned[pl.ds(part_rows * half, half), :, pl.ds(n * LANES, LANES)] = (
                spread[n].reshape(half, slab, LANES).astype(jnp.bfloat16)
            )
        place = out_ref.at[:, :, pl.ds(pl.multiple_of(band * lanes, LANES), lanes)]
        for q in range(groups // 2):
            to = part_rows * (groups // 2) + q
            source = turned.at[pl.ds(to * bands, bands)]
            returned.append((to, source, place))

            @pl.when(band == to)
            def _():
                pltpu.make_async_copy(source, place, back_recv.at[band]).start()

            @pl.when(band != to)
            def _():
                remote(source, place, back_send.at[to], back_recv.at[band], {"band": to}).start()

    while pending:
        pending.pop(0)()
    unpack(hamil_gath, full)
    transposed = split_rounding(trans[...].T)
    halfway = split_rounding(dot3(transposed, split_rounding(full[...])))
    proj_ref[...] = dot3(halfway, split_rounding(trans[...]))

    for to, source, place in returned:
        theirs = out_ref.at[:, :, pl.ds(to * lanes, lanes)]

        @pl.when(band == to)
        def _():
            pltpu.make_async_copy(source, place, back_recv.at[band]).wait()

        @pl.when(band != to)
        def _():
            remote(source, place, back_send.at[to], back_recv.at[band], {"band": to}).wait_send()
            remote(source, theirs, back_send.at[to], back_recv.at[to], {"band": to}).wait_recv()


def step_call(sent, potential, bounds, groups, cell_volume):
    doms, slab, mine, width = sent.shape
    devices = doms * groups
    total = devices * mine
    planes = doms * slab
    part = min(mine, 8)
    chunks = mine // part
    levels = width // LANES
    lanes = width // groups
    size = LANES * (LANES // GRID_Z)
    packed = LANES * len(upper_blocks(total))
    vmem = pl.BlockSpec(memory_space=pltpu.VMEM)
    hbm = pl.BlockSpec(memory_space=pl.ANY)
    gathered = pltpu.VMEM((slab, total, lanes), jnp.bfloat16)
    whole = pltpu.VMEM((planes, mine, width), jnp.bfloat16)
    order = pltpu.VMEM((size, size), jnp.bfloat16)
    field = pltpu.VMEM((levels + 2, planes * part, LANES), jnp.float32)
    triangle = pltpu.VMEM((packed, LANES), jnp.float32)
    square = pltpu.VMEM((total, total), jnp.float32)
    dma = pltpu.SemaphoreType.DMA
    most = max(2, doms, groups // 2)
    return pl.pallas_call(
        functools.partial(step_kernel, groups, cell_volume),
        out_shape=(
            jax.ShapeDtypeStruct((mine * doms, slab, width), jnp.bfloat16),
            jax.ShapeDtypeStruct((total, total), jnp.float32),
        ),
        in_specs=[pl.BlockSpec(memory_space=pltpu.SMEM), hbm, vmem],
        out_specs=(hbm, vmem),
        scratch_shapes=[
            gathered,
            gathered,
            pltpu.VMEM(sent.shape, jnp.bfloat16),
            pltpu.VMEM((doms, slab, width), jnp.float32),
            order,
            order,
            field,
            field,
            pltpu.VMEM((levels, planes * part, LANES), jnp.float32),
            whole,
            whole,
        ]
        + [triangle] * 6
        + [square] * 4
        + [
            pltpu.VMEM((lanes // LANES, total // 2 * slab, LANES), jnp.float32),
            pltpu.VMEM((total, slab, lanes), jnp.bfloat16),
            dma((chunks, doms)),
            dma((chunks, doms)),
            dma((doms,)),
            dma((doms,)),
            dma((2, chunks, devices)),
            dma((2, chunks, devices)),
        ]
        + [dma((2, 3, most))] * 4
        + [dma((groups,))] * 2,
        cost_estimate=pl.CostEstimate(flops=60 * total**3, bytes_accessed=8 << 20, transcendentals=0),
        compiler_params=pltpu.CompilerParams(vmem_limit_bytes=48 << 20, collective_id=2, has_side_effects=True),
    )(bounds, sent, potential)


def body_plain(orbitals, potential, bounds):
    bands, slab, width = orbitals.shape
    doms = lax.axis_size("dom")
    groups = lax.axis_size("band")
    devices = doms * groups
    total_bands = bands * groups
    mine = bands // doms
    everyone = ("dom", "band")
    half_width = (bounds[1] - bounds[0]) / 2.0
    centre = (bounds[1] + bounds[0]) / 2.0
    cell_volume = 1.0 / (slab * doms * width)

    sent = orbitals.reshape(doms, mine, slab, width).transpose(0, 2, 1, 3)
    cells = lax.all_to_all(sent, "dom", split_axis=0, concat_axis=0, tiled=True)
    cells = cells.reshape(doms * slab, mine, width)
    pot = lax.all_to_all(
        jnp.broadcast_to(potential, (doms, slab, width)), "dom", split_axis=0, concat_axis=0, tiled=True
    ).reshape(doms * slab, 1, width)
    filt, applied = filter_bands(cells, pot, jnp.stack([1.0 / half_width, centre]), devices)
    filt = lax.all_to_all(filt, everyone, split_axis=0, concat_axis=0, tiled=True)
    applied = lax.all_to_all(applied, everyone, split_axis=0, concat_axis=0, tiled=True)
    filt = filt.reshape(total_bands, -1)
    applied = applied.reshape(total_bands, -1)
    bits = exchange_bits(doms, groups)
    square = jax.ShapeDtypeStruct((total_bands, total_bands), jnp.float32)
    rotated, trans = sum_call(
        functools.partial(orthonormal_kernel, bits, cell_volume, (doms, groups, mine)),
        (filt,),
        (jax.ShapeDtypeStruct(filt.shape, jnp.bfloat16), square),
        3,
        bits,
        0,
        40 * total_bands**3,
    )
    out = lax.all_to_all(rotated, "band", split_axis=0, concat_axis=1, tiled=True)
    projected = sum_call(
        functools.partial(project_kernel, bits, cell_volume),
        (filt, applied, trans),
        square,
        0,
        bits,
        1,
        40 * total_bands**3,
    )
    return out.reshape(bands, slab, width), projected


def body(orbitals, potential, bounds):
    bands, slab, width = orbitals.shape
    doms = lax.axis_size("dom")
    groups = lax.axis_size("band")
    mine = bands // doms
    total = bands * groups
    blocks = len(upper_blocks(total))
    if mine % 8 or width % (groups * LANES) or total % (2 * LANES) or blocks * LANES % (8 * doms * groups):
        return body_plain(orbitals, potential, bounds)
    cell_volume = 1.0 / (slab * doms * width)
    sent = orbitals.reshape(doms, mine, slab, width).transpose(0, 2, 1, 3)
    return step_call(sent, potential, bounds, groups, cell_volume)


def solution(mesh):
    return jax.shard_map(
        body,
        mesh=mesh,
        in_specs=(P("band", "dom", None), P("dom", None), P()),
        out_specs=(P("band", "dom", None), P()),
        check_vma=False,
    )
```

```python
import functools

import jax
import jax.numpy as jnp
from jax import lax
from jax.experimental import pallas as pl
from jax.experimental.pallas import tpu as pltpu
from jax.sharding import PartitionSpec as P

GRID_Z = 32
DEG = 8
NS_STEPS = 8
LANES = 128
UNROLL = 8
PAUSE = 3
TILE_ROWS = 8


def filter_kernel(scal_ref, cells_ref, pot_ref, sums_ref, filt_ref, applied_ref, field, high, low, coef):
    planes, bands, width = cells_ref.shape
    rows = planes * bands
    blocks_per_plane = filt_ref.shape[0] // planes
    block = filt_ref.shape[2]
    tile = sums_ref.shape[1]
    inv_half = scal_ref[0]
    centre = scal_ref[1]

    for x in range(planes):
        mine = pl.ds(x * bands, bands)
        coef[mine, :] = jnp.broadcast_to(3.0 + pot_ref[x], (bands, width))
        start = cells_ref[x].astype(jnp.float32)
        field[0, mine, :] = start
    for c in range(width // tile):
        cols = pl.ds(c * tile, tile)
        start = field[0, :, cols]
        high[0, :, cols] = start.astype(jnp.bfloat16)
        low[0, :, cols] = jnp.zeros((rows, tile), jnp.bfloat16)

    def shifted(v, by):
        if bands % 8 == 0:
            return jnp.concatenate([v[by:], v[:by]], axis=0)
        return pltpu.roll(v, (rows - by) % rows, 0)

    def neighbours(slot, c, v):
        cols = pl.ds(pl.multiple_of(c * tile, tile), tile)
        left = pl.ds(pl.multiple_of(lax.rem(c * tile + width - LANES, width), LANES), LANES)
        right = pl.ds(pl.multiple_of(lax.rem(c * tile + tile, width), LANES), LANES)

        def part(ref):
            wide = jnp.concatenate([ref[slot, :, left], ref[slot, :, cols], ref[slot, :, right]], axis=1)
            return dot(wide, sums_ref[...])

        return part(high) + part(low) + (shifted(v, bands) + shifted(v, rows - bands))

    def sweep(slot, other, weight, diagonal, first):
        def run(c, carry):
            cols = pl.ds(pl.multiple_of(c * tile, tile), tile)
            v = field[slot, :, cols]
            fresh = weight * neighbours(slot, c, v) + (coef[:, cols] * diagonal[0] + diagonal[1]) * v
            if not first:
                fresh = fresh - field[other, :, cols]
            field[other, :, cols] = fresh
            top, rest = split(fresh)
            high[other, :, cols] = top
            low[other, :, cols] = rest
            return carry

        lax.fori_loop(0, width // tile, run, 0)

    sweep(0, 1, -0.5 * inv_half, (inv_half, -centre * inv_half), True)

    def middle(k, carry):
        slot = lax.rem(k, 2)
        sweep(slot, 1 - slot, -inv_half, (2.0 * inv_half, -2.0 * centre * inv_half), False)
        return carry

    lax.fori_loop(1, DEG, middle, 0)
    slot = DEG % 2
    for c in range(width // tile):
        cols = pl.ds(c * tile, tile)
        v = field[slot, :, cols]
        applied = coef[:, cols] * v - 0.5 * neighbours(slot, c, v)
        piece, inner = divmod(c * tile, block)
        for x in range(planes):
            where = (x * blocks_per_plane + piece, slice(None), pl.ds(inner, tile))
            filt_ref[where] = v[x * bands : (x + 1) * bands].astype(jnp.bfloat16)
            applied_ref[where] = applied[x * bands : (x + 1) * bands].astype(jnp.bfloat16)


def neighbour_sums(tile):
    source = lax.broadcasted_iota(jnp.int32, (tile + 2 * LANES, tile), 0) - LANES
    target = lax.broadcasted_iota(jnp.int32, (tile + 2 * LANES, tile), 1)
    step = source - target
    same_row = (source >= 0) & (source // GRID_Z == target // GRID_Z)
    apart = lax.rem(step + GRID_Z, GRID_Z)
    beside_z = same_row & ((apart == 1) | (apart == GRID_Z - 1))
    beside_y = (step == GRID_Z) | (step == -GRID_Z)
    return (beside_z | beside_y).astype(jnp.bfloat16)


def filter_bands(cells, potential, scalars, devices):
    planes, bands, width = cells.shape
    rows = planes * bands
    block = planes * width // devices
    out = jax.ShapeDtypeStruct((devices, bands, block), jnp.bfloat16)
    vmem = pl.BlockSpec(memory_space=pltpu.VMEM)
    return pl.pallas_call(
        filter_kernel,
        out_shape=(out, out),
        in_specs=[pl.BlockSpec(memory_space=pltpu.SMEM), vmem, vmem, vmem],
        out_specs=(vmem, vmem),
        scratch_shapes=[
            pltpu.VMEM((2, rows, width), jnp.float32),
            pltpu.VMEM((2, rows, width), jnp.bfloat16),
            pltpu.VMEM((2, rows, width), jnp.bfloat16),
            pltpu.VMEM((rows, width), jnp.float32),
        ],
        compiler_params=pltpu.CompilerParams(vmem_limit_bytes=48 << 20),
    )(scalars, cells, potential, neighbour_sums(min(256, block)))


def split(value):
    spread = value * 65537.0
    high = spread - (spread - value)
    return high.astype(jnp.bfloat16), (value - high).astype(jnp.bfloat16)


def dot(a, b):
    return jnp.dot(a, b, preferred_element_type=jnp.float32)


def dot3(a, b):
    (a_high, a_low), (b_high, b_low) = a, b
    return dot(a_high, b_high) + (dot(a_high, b_low) + dot(a_low, b_high))


def exchange_bits(doms, groups):
    dom = [("dom", 1 << i) for i in range(1, (doms - 1).bit_length())]
    band = [("band", 1 << i) for i in range((groups - 1).bit_length())]
    core = [("dom", 1)]
    return core + band[:1] + dom + band[1:], core + dom + band


def gram_sum(bits, cell_volume, filt_ref, other_ref, total, send, recv, gath, send_sem, recv_sem):
    size = filt_ref.shape[0] // 2
    index = {axis: lax.axis_index(axis) for axis in ("dom", "band")}

    def partner(axis, bit):
        mine = lax.rem(index[axis] // bit, 2)
        return mine, {axis: index[axis] + bit - 2 * bit * mine}

    barrier = pltpu.get_barrier_semaphore()
    for axis, bit in bits[0]:
        pl.semaphore_signal(
            barrier, inc=1, device_id=partner(axis, bit)[1], device_id_type=pl.DeviceIdType.MESH
        )

    pairs = (((1,), (1,)), ((), ()))
    for stream in range(2):
        total[stream] = cell_volume * lax.dot_general(
            filt_ref[pl.ds(stream * size, size), :],
            other_ref[...],
            pairs,
            preferred_element_type=jnp.float32,
        )
    pl.semaphore_wait(barrier, len(bits[0]))

    def copy(stream, number, source, target, device):
        made = pltpu.make_async_remote_copy(
            src_ref=source,
            dst_ref=target,
            send_sem=send_sem.at[stream, number],
            recv_sem=recv_sem.at[stream, number],
            device_id=device,
            device_id_type=pl.DeviceIdType.MESH,
        )
        made.start()
        return made

    stages = len(bits[0])
    start = [jnp.int32(0)] * 2
    halved = [[], []]
    length, offset = size, 0
    for stage in range(stages):
        halve = length >= 2 * TILE_ROWS
        count = length // 2 if halve else length
        space = pl.ds(offset, count)
        flight = []
        for stream in range(2):
            axis, bit = bits[stream][stage]
            mine, device = partner(axis, bit)
            give = start[stream] + (1 - mine) * count if halve else start[stream]
            keep = start[stream] + mine * count if halve else start[stream]
            give = pl.multiple_of(give, TILE_ROWS)
            send[stream, space, :] = total[stream, pl.ds(give, count), :]
            flight.append(
                copy(stream, stage, send.at[stream, space], recv.at[stream, space], device)
            )
            start[stream] = pl.multiple_of(keep, TILE_ROWS)
            if halve:
                halved[stream].append((stage, mine, device))
        for stream in range(2):
            flight[stream].wait()
            kept = pl.ds(start[stream], count)
            if halve:
                own = total[stream, kept, :]
            else:
                own = send[stream, space, :]
            total[stream, kept, :] = own + recv[stream, space, :]
        length = count
        offset += count

    for stream in range(2):
        kept = pl.ds(start[stream], length)
        gath[stream, kept, :] = total[stream, kept, :]
    for back in range(len(halved[0]) - 1, -1, -1):
        flight = []
        for stream in range(2):
            stage, mine, device = halved[stream][back]
            area = gath.at[stream, pl.ds(start[stream], length)]
            flight.append(copy(stream, stages + stage, area, area, device))
            start[stream] = pl.multiple_of(start[stream] - mine * length, TILE_ROWS)
        for made in flight:
            made.wait()
        length *= 2


def orthonormal_kernel(
    bits, cell_volume, groups, filt_ref, out_ref, trans_ref,
    total, send, recv, gath, y_ref, z_ref, t_ref, send_sem, recv_sem,
):
    gram_sum(bits, cell_volume, filt_ref, filt_ref, total, send, recv, gath, send_sem, recv_sem)
    size = filt_ref.shape[0]
    outer, inner, width = groups
    row = lax.broadcasted_iota(jnp.int32, (size, size), 0)
    col = lax.broadcasted_iota(jnp.int32, (size, size), 1)
    diag = jnp.where(row == col, 1.5, 0.0)
    corr = gath[...].reshape(size, size)
    scale = jnp.sqrt(jnp.sum(corr * corr) + 1e-06)
    scaled = corr / scale
    factor = diag - 0.5 * scaled
    z_ref[...] = factor
    y_ref[...] = dot3(split(factor), split(scaled))

    def step(k, carry):
        y = split(y_ref[...])
        z = split(z_ref[...])
        factor = split(diag - 0.5 * dot3(z, y))
        y_ref[...] = dot3(factor, y)
        z_ref[...] = dot3(factor, z)
        return carry

    lax.fori_loop(1, NS_STEPS - 1, step, 0)
    y = split(y_ref[...])
    z = split(z_ref[...])
    factor = split(diag - 0.5 * dot3(z, y))
    t_ref[...] = dot3(factor, z) / jnp.sqrt(scale)
    for i in range(outer):
        for j in range(inner):
            trans_ref[pl.ds((j * outer + i) * width, width), :] = t_ref[
                pl.ds((i * inner + j) * width, width), :
            ]
    trans = split(trans_ref[...])
    filt = filt_ref[...]
    out_ref[...] = (dot(trans[0], filt) + dot(trans[1], filt)).astype(jnp.bfloat16)


def project_kernel(
    bits, cell_volume, filt_ref, applied_ref, trans_ref, proj_ref,
    total, send, recv, gath, send_sem, recv_sem,
):
    gram_sum(bits, cell_volume, filt_ref, applied_ref, total, send, recv, gath, send_sem, recv_sem)
    size = filt_ref.shape[0]
    trans = split(trans_ref[...])
    half = split(dot3(trans, split(gath[...].reshape(size, size))))
    contract = (((1,), (1,)), ((), ()))

    def dot_t(a, b):
        return lax.dot_general(a, b, contract, preferred_element_type=jnp.float32)

    proj_ref[...] = dot_t(half[0], trans[0]) + (
        dot_t(half[0], trans[1]) + dot_t(half[1], trans[0])
    )


def sum_call(kernel, operands, out_shape, squares, bits, number, flops):
    size = operands[0].shape[0]
    vmem = pl.BlockSpec(memory_space=pltpu.VMEM)
    room = size // 2 + TILE_ROWS * len(bits[0])
    sems = pltpu.SemaphoreType.DMA((2, 2 * len(bits[0])))
    halves = pltpu.VMEM((2, size // 2, size), jnp.float32)
    stage = pltpu.VMEM((2, room, size), jnp.float32)
    return pl.pallas_call(
        kernel,
        out_shape=out_shape,
        in_specs=[vmem] * len(operands),
        out_specs=jax.tree.map(lambda _: vmem, out_shape),
        scratch_shapes=[halves, stage, stage, halves]
        + [pltpu.VMEM((size, size), jnp.float32)] * squares
        + [sems, sems],
        cost_estimate=pl.CostEstimate(flops=flops, bytes_accessed=8 << 20, transcendentals=0),
        compiler_params=pltpu.CompilerParams(
            vmem_limit_bytes=32 << 20, collective_id=number, has_side_effects=True
        ),
    )(*operands)


def peers(doms, groups):
    dom = lax.axis_index("dom")
    band = lax.axis_index("band")
    rows = [lax.rem(dom + r, doms) for r in range(doms)]
    columns = [lax.rem(band + r, groups) for r in range(groups)]
    return [{"dom": d, "band": b} for b in columns for d in rows]


def remote(source, target, send_sem, recv_sem, device):
    return pltpu.make_async_remote_copy(
        src_ref=source,
        dst_ref=target,
        send_sem=send_sem,
        recv_sem=recv_sem,
        device_id=device,
        device_id_type=pl.DeviceIdType.MESH,
    )


def greet(others):
    barrier = pltpu.get_barrier_semaphore()
    for other in others:
        pl.semaphore_signal(barrier, inc=1, device_id=other, device_id_type=pl.DeviceIdType.MESH)
    return barrier


def lane_orders(perm, back):
    size = perm.shape[0]
    high = size // LANES
    row = lax.broadcasted_iota(jnp.int32, (size, size), 0)
    col = lax.broadcasted_iota(jnp.int32, (size, size), 1)
    grouped = lax.rem(row // GRID_Z, high) * LANES + lax.rem(row, GRID_Z) * high + row // LANES
    perm[...] = jnp.where(grouped == col, 1.0, 0.0).astype(jnp.bfloat16)
    natural = lax.rem(row, high) * LANES + row // LANES * GRID_Z + lax.rem(row // high, GRID_Z)
    back[...] = jnp.where(natural == col, 1.0, 0.0).astype(jnp.bfloat16)


class BlockSum:
    def __init__(self, total, recv, gath, send_sem, recv_sem, levels):
        self.total, self.recv, self.gath = total, recv, gath
        self.send_sem, self.recv_sem, self.levels = send_sem, recv_sem, levels
        self.start, self.length = jnp.int32(0), total.shape[0]
        self.offset, self.copies = 0, []

    def steps(self):
        for level in range(len(self.levels)):
            yield functools.partial(self.scatter, level)
            yield functools.partial(self.add, level)
        for level in range(len(self.levels) - 1, -1, -1):
            yield functools.partial(self.gather, level)
            yield functools.partial(self.join, level)

    def scatter(self, level):
        at, size, device = self.levels[level]
        rows = self.length // size
        self.copies = []
        for r in range(1, size):
            to = lax.rem(at + r, size)
            source = pl.ds(pl.multiple_of(self.start + to * rows, TILE_ROWS), rows)
            place = pl.ds(self.offset + (r - 1) * rows, rows)
            self.copies.append(
                remote(
                    self.total.at[source], self.recv.at[place],
                    self.send_sem.at[0, level, r], self.recv_sem.at[0, level, r], device(to),
                )
            )
        for made in self.copies:
            made.start()

    def add(self, level):
        at, size, _ = self.levels[level]
        rows = self.length // size
        self.start = pl.multiple_of(self.start + at * rows, TILE_ROWS)
        self.length = rows
        kept = pl.ds(self.start, rows)
        for made in self.copies:
            made.wait()
        value = self.total[kept]
        for r in range(1, size):
            value = value + self.recv[pl.ds(self.offset + (r - 1) * rows, rows)]
        self.offset += (size - 1) * rows
        self.total[kept] = value
        if level == len(self.levels) - 1:
            self.gath[kept] = value

    def gather(self, level):
        at, size, device = self.levels[level]
        area = self.gath.at[pl.ds(self.start, self.length)]
        self.copies = [
            remote(area, area, self.send_sem.at[1, level, r], self.recv_sem.at[1, level, r], device(lax.rem(at + r, size)))
            for r in range(1, size)
        ]
        for made in self.copies:
            made.start()

    def join(self, level):
        at, size, _ = self.levels[level]
        for made in self.copies:
            made.wait()
        self.start = pl.multiple_of(self.start - at * self.length, TILE_ROWS)
        self.length *= size


def sum_levels(doms, groups):
    dom = lax.axis_index("dom")
    band = lax.axis_index("band")
    core, chip = lax.rem(dom, 2), dom // 2
    low, high = lax.rem(band, 2), band // 2
    return [
        (core, 2, lambda to: {"dom": chip * 2 + to}),
        (chip * 2 + low, doms, lambda to: {"dom": to // 2 * 2 + core, "band": high * 2 + lax.rem(to, 2)}),
        (high, groups // 2, lambda to: {"band": to * 2 + low}),
    ]


def upper_blocks(total):
    count = total // LANES
    return [(i, j) for i in range(count) for j in range(i, count)]


def next_cells(nexts):
    size = nexts.shape[0]
    row = lax.broadcasted_iota(jnp.int32, (size, size), 0)
    col = lax.broadcasted_iota(jnp.int32, (size, size), 1)
    ahead = col // GRID_Z * GRID_Z + lax.rem(col + 1, GRID_Z)
    nexts[...] = jnp.where((row == ahead) | (row == col + GRID_Z), 1.0, 0.0).astype(jnp.bfloat16)


def gram(factor, pairs, slab, packed):
    total = pairs[0][0].shape[1]
    size = 2 * LANES
    where = {pair: n for n, pair in enumerate(upper_blocks(total))}
    for i in range(total // size):
        for j in range(i, total // size):
            block = jnp.zeros((size, size), jnp.float32)
            for x in range(slab):
                for left, right in pairs:
                    block = block + lax.dot_general(
                        left[x, pl.ds(i * size, size), :],
                        right[x, pl.ds(j * size, size), :],
                        (((1,), (1,)), ((), ())),
                        preferred_element_type=jnp.float32,
                    )
            block = block * factor
            for a in range(2):
                for b in range(2):
                    pair = (2 * i + a, 2 * j + b)
                    if pair in where:
                        packed[pl.ds(where[pair] * LANES, LANES)] = block[
                            a * LANES : (a + 1) * LANES, b * LANES : (b + 1) * LANES
                        ]


def unpack(packed, full):
    for n, (i, j) in enumerate(upper_blocks(full.shape[0])):
        block = packed[pl.ds(n * LANES, LANES)]
        full[pl.ds(i * LANES, LANES), pl.ds(j * LANES, LANES)] = block
        if i != j:
            full[pl.ds(j * LANES, LANES), pl.ds(i * LANES, LANES)] = block.T


def split_rounding(value):
    high = value.astype(jnp.bfloat16)
    return high, (value - high.astype(jnp.float32)).astype(jnp.bfloat16)


def inverse_root(full, work, other, pause):
    size = full.shape[0]
    row = lax.broadcasted_iota(jnp.int32, (size, size), 0)
    col = lax.broadcasted_iota(jnp.int32, (size, size), 1)

    def diagonal(value):
        return jnp.where(row == col, value, 0.0)

    corr = full[...]
    scale = jnp.sqrt(jnp.sum(corr * corr) + 1e-06)
    work[...] = corr / scale
    for double in range(NS_STEPS // 2 - 1):
        held = split_rounding(work[...])
        other[...] = dot3(held, held)
        pause()
        square = other[...]
        rest = dot3(split_rounding(square), split_rounding(0.0625 * square - 0.5625 * work[...]))
        factor = split_rounding(diagonal(2.25) - 2.4375 * work[...] + (1.6875 * square + rest))
        pause()
        if double == 0:
            full[...] = factor[0].astype(jnp.float32) + factor[1].astype(jnp.float32)
        else:
            full[...] = dot3(split_rounding(full[...]), factor)
            pause()
        other[...] = dot3(held, factor)
        pause()
        work[...] = dot3(split_rounding(other[...]), factor)
        pause()
    left = diagonal(1.0) - work[...]
    rounded = left.astype(jnp.bfloat16)
    square = dot(rounded, rounded)
    rest = 0.5 * left + 0.375 * square
    rest = rest + dot(square.astype(jnp.bfloat16), (0.3125 * left + 0.0625 * square).astype(jnp.bfloat16))
    pause()
    value = full[...]
    value = value + dot(value.astype(jnp.bfloat16), rest.astype(jnp.bfloat16))
    return value / jnp.sqrt(scale)


def step_kernel(
    groups, cell_volume, bounds_ref, sent_ref, pot_ref, out_ref, proj_ref,
    filt_ref, beyond, image_ref, nexts, stage, pots, perm, back, even, odd, diag, send_f, send_y,
    corr_sum, corr_recv, corr_gath, hamil_sum, hamil_recv, hamil_gath, full, work, other, trans, spread, turned,
    in_send, in_recv, pot_send, pot_recv, out_send, out_recv, corr_send, corr_arrive, hamil_send, hamil_arrive, back_send, back_recv,
):
    doms, slab, mine, width = stage.shape
    devices = doms * groups
    dom = lax.axis_index("dom")
    band = lax.axis_index("band")
    planes = doms * slab
    part = min(mine, 8)
    chunks = mine // part
    rows = planes * part
    lanes = width // groups
    levels = width // LANES
    high = LANES // GRID_Z
    spans = levels // high
    half_width = (bounds_ref[1] - bounds_ref[0]) / 2.0
    centre = (bounds_ref[1] + bounds_ref[0]) / 2.0
    inv_half = 1.0 / half_width

    everyone = peers(doms, groups)
    barrier = greet(everyone[1:])
    lane_orders(perm, back)
    pl.semaphore_wait(barrier, len(everyone) - 1)

    def incoming(c, r):
        peer = lax.rem(dom + r, doms)
        some = pl.ds(c * part, part)
        source, target = sent_ref.at[peer, :, some, :], stage.at[dom, :, some, :]
        if r == 0:
            return pltpu.make_async_copy(source, target, in_recv.at[c, r])
        return remote(source, target, in_send.at[c, r], in_recv.at[c, r], {"dom": peer})

    def potential(r):
        if r == 0:
            return pltpu.make_async_copy(pot_ref, pots.at[dom], pot_recv.at[r])
        return remote(pot_ref, pots.at[dom], pot_send.at[r], pot_recv.at[r], {"dom": lax.rem(dom + r, doms)})

    for r in range(doms):
        potential(r).start()
    for c in range(chunks):
        for r in range(doms):
            incoming(c, r).start()

    lane = lax.broadcasted_iota(jnp.int32, (rows, LANES), 1)
    row_of_lane = lax.broadcasted_iota(jnp.int32, (doms, part, LANES), 2) // GRID_Z
    first_high = lax.rem(lane, high) == 0
    last_high = lax.rem(lane, high) == high - 1

    for r in range(doms):
        potential(r).wait()
    for k in range(spans):
        pot = jnp.concatenate(
            [pots[:, :, pl.ds((h * spans + k) * LANES, LANES)].reshape(planes, LANES) for h in range(high)], axis=1
        )
        ordered = jnp.zeros(pot.shape, jnp.float32)
        for piece in range(3):
            top = pot.astype(jnp.bfloat16)
            ordered = ordered + dot(top, perm[...])
            pot = pot - top.astype(jnp.float32)
        scaled = (3.0 + ordered - centre) * (2.0 * inv_half)
        for b in range(high):
            line = scaled[:, b * LANES : (b + 1) * LANES]
            diag[k * high + b] = jnp.broadcast_to(line[:, None, :], (planes, part, LANES)).reshape(rows, LANES)

    def edges(field):
        top = field[levels]
        field[0] = jnp.where(first_high, pltpu.roll(top, LANES - (high - 1), 1), pltpu.roll(top, 1, 1))
        low = field[1]
        field[levels + 1] = jnp.where(last_high, pltpu.roll(low, high - 1, 1), pltpu.roll(low, LANES - 1, 1))

    def image(field, i):
        v = field[i]
        around = pltpu.roll(v, high, 1) + pltpu.roll(v, LANES - high, 1)
        around = around + (field[i - 1] + field[i + 1])
        around = around + (
            jnp.concatenate([v[part:], v[:part]], axis=0) + jnp.concatenate([v[rows - part :], v[: rows - part]], axis=0)
        )
        return diag[i - 1] * v - inv_half * around, v

    def sweep(source, target, first):
        def run(j, carry):
            for i in range(UNROLL):
                i = 1 + j * UNROLL + i
                fresh = image(source, i)[0]
                target[i] = 0.5 * fresh if first else fresh - target[i]
            return carry

        lax.fori_loop(0, levels // UNROLL, run, 0)
        edges(target)

    def outgoing(c):
        copies = []
        row = pl.multiple_of((band * doms + dom) * mine + c * part, part)
        some = pl.ds(c * part, part)
        for r, device in enumerate(everyone):
            here = pl.ds(pl.multiple_of(device["band"] * lanes, LANES), lanes)
            above = pl.ds(pl.multiple_of(lax.rem(device["band"] + 1, groups) * LANES, LANES), LANES)
            pairs = (
                (send_f.at[pl.ds(device["dom"] * slab, slab + 1), some, here], filt_ref.at[:, pl.ds(row, part), :]),
                (send_y.at[device["dom"], some, above], beyond.at[pl.ds(row, part), :]),
            )
            for which, (piece, place) in enumerate(pairs):
                recv = out_recv.at[which, c, r]
                if r == 0:
                    copies.append(pltpu.make_async_copy(piece, place, recv))
                else:
                    copies.append(remote(piece, place, out_send.at[which, c, r], recv, device))
        return copies

    for c in range(chunks):
        for r in range(doms):
            incoming(c, r).wait()
        some = pl.ds(c * part, part)
        for k in range(spans):
            cells = jnp.concatenate(
                [
                    stage[:, :, some, pl.ds((h * spans + k) * LANES, LANES)].astype(jnp.float32).reshape(rows, LANES)
                    for h in range(high)
                ],
                axis=1,
            )
            ordered = dot(cells.astype(jnp.bfloat16), perm[...])
            for b in range(high):
                even[1 + k * high + b] = ordered[:, b * LANES : (b + 1) * LANES]
        edges(even)
        sweep(even, odd, True)

        def pair(k, carry):
            sweep(odd, even, False)
            sweep(even, odd, False)
            return carry

        lax.fori_loop(0, (DEG - 1) // 2, pair, 0)
        last = odd
        if DEG % 2 == 0:
            sweep(odd, even, False)
            last = even

        for k in range(spans):
            values = [last[1 + k * high + b] for b in range(high)]
            natural = dot(jnp.concatenate(values, axis=1).astype(jnp.bfloat16), back[...])
            for h in range(high):
                column = (h * spans + k) * LANES
                value = natural[:, h * LANES : (h + 1) * LANES].reshape(planes, part, LANES)
                send_f[pl.ds(0, planes), some, pl.ds(column, LANES)] = value.astype(jnp.bfloat16)
                send_f[planes, some, pl.ds(column, LANES)] = value[0].astype(jnp.bfloat16)
                if column % lanes == 0:
                    value = value.reshape(doms, slab * part, LANES)
                    edge = value[:, :part]
                    for x in range(1, slab):
                        moved = value[:, x * part : (x + 1) * part].reshape(doms * part, LANES)
                        moved = pltpu.roll(moved, x * GRID_Z, 1).reshape(doms, part, LANES)
                        edge = jnp.where(row_of_lane == x, moved, edge)
                    send_y[:, some, pl.ds(column // lanes * LANES, LANES)] = edge.astype(jnp.bfloat16)
        for copy in outgoing(c):
            copy.start()
    next_cells(nexts)
    for c in range(chunks):
        for copy in outgoing(c):
            copy.wait()

    total = filt_ref.shape[1]
    gram(cell_volume, ((filt_ref, filt_ref),), slab, corr_sum)
    corr = BlockSum(corr_sum, corr_recv, corr_gath, corr_send, corr_arrive, sum_levels(doms, groups))
    steps = list(corr.steps())
    for step in steps[:1]:
        step()
    edge = lax.broadcasted_iota(jnp.int32, (total, LANES), 1) >= LANES - GRID_Z
    for x in range(slab):
        pot = 3.0 + pot_ref[pl.ds(x, 1), pl.ds(pl.multiple_of(band * lanes, LANES), lanes)]
        value = filt_ref[x].astype(jnp.float32) * pot - filt_ref[x + 1].astype(jnp.float32)
        value = value - dot(filt_ref[x], nexts[...])
        after = pltpu.roll(beyond[...].astype(jnp.float32), (LANES - GRID_Z - x * GRID_Z) % LANES, 1)
        image_ref[x, :, pl.ds(0, lanes - LANES)] = value[:, : lanes - LANES].astype(jnp.bfloat16)
        image_ref[x, :, pl.ds(lanes - LANES, LANES)] = (
            value[:, lanes - LANES :] - jnp.where(edge, after, 0.0)
        ).astype(jnp.bfloat16)
    for step in steps[1:3]:
        step()
    gram(0.5 * cell_volume, ((filt_ref, image_ref), (image_ref, filt_ref)), slab, hamil_sum)
    for step in steps[3:]:
        step()
    unpack(corr_gath, full)

    hamil = BlockSum(hamil_sum, hamil_recv, hamil_gath, hamil_send, hamil_arrive, sum_levels(doms, groups))
    pending = list(hamil.steps())
    pending.pop(0)()

    def pause():
        for _ in range(2):
            if len(pending) > 1:
                pending.pop(0)()

    calls = [0]

    def sometimes():
        calls[0] += 1
        if calls[0] % PAUSE == 0:
            pause()

    value = inverse_root(full, work, other, sometimes)
    trans[...] = value
    turn = split(value.T)

    bands = out_ref.shape[0]
    half = total // 2
    returned = []
    for part_rows in range(2):
        for x in range(slab):
            points = filt_ref[x]
            piece = [t[part_rows * half : (part_rows + 1) * half] for t in turn]
            product = dot(piece[0], points) + dot(piece[1], points)
            for n in range(lanes // LANES):
                spread[n, pl.ds(x, half, stride=slab), :] = product[:, n * LANES : (n + 1) * LANES]
        for n in range(lanes // LANES):
            turned[pl.ds(part_rows * half, half), :, pl.ds(n * LANES, LANES)] = (
                spread[n].reshape(half, slab, LANES).astype(jnp.bfloat16)
            )
        place = out_ref.at[:, :, pl.ds(pl.multiple_of(band * lanes, LANES), lanes)]
        for q in range(groups // 2):
            to = part_rows * (groups // 2) + q
            source = turned.at[pl.ds(to * bands, bands)]
            returned.append((to, source, place))

            @pl.when(band == to)
            def _():
                pltpu.make_async_copy(source, place, back_recv.at[band]).start()

            @pl.when(band != to)
            def _():
                remote(source, place, back_send.at[to], back_recv.at[band], {"band": to}).start()

    while pending:
        pending.pop(0)()
    unpack(hamil_gath, full)
    transposed = split_rounding(trans[...].T)
    halfway = split_rounding(dot3(transposed, split_rounding(full[...])))
    proj_ref[...] = dot3(halfway, split_rounding(trans[...]))

    for to, source, place in returned:
        theirs = out_ref.at[:, :, pl.ds(to * lanes, lanes)]

        @pl.when(band == to)
        def _():
            pltpu.make_async_copy(source, place, back_recv.at[band]).wait()

        @pl.when(band != to)
        def _():
            remote(source, place, back_send.at[to], back_recv.at[band], {"band": to}).wait_send()
            remote(source, theirs, back_send.at[to], back_recv.at[to], {"band": to}).wait_recv()


def step_call(sent, potential, bounds, groups, cell_volume):
    doms, slab, mine, width = sent.shape
    devices = doms * groups
    total = devices * mine
    planes = doms * slab
    part = min(mine, 8)
    chunks = mine // part
    levels = width // LANES
    lanes = width // groups
    size = LANES * (LANES // GRID_Z)
    packed = LANES * len(upper_blocks(total))
    vmem = pl.BlockSpec(memory_space=pltpu.VMEM)
    hbm = pl.BlockSpec(memory_space=pl.ANY)
    order = pltpu.VMEM((size, size), jnp.bfloat16)
    field = pltpu.VMEM((levels + 2, planes * part, LANES), jnp.float32)
    triangle = pltpu.VMEM((packed, LANES), jnp.float32)
    square = pltpu.VMEM((total, total), jnp.float32)
    dma = pltpu.SemaphoreType.DMA
    most = max(2, doms, groups // 2)
    return pl.pallas_call(
        functools.partial(step_kernel, groups, cell_volume),
        out_shape=(
            jax.ShapeDtypeStruct((mine * doms, slab, width), jnp.bfloat16),
            jax.ShapeDtypeStruct((total, total), jnp.float32),
        ),
        in_specs=[pl.BlockSpec(memory_space=pltpu.SMEM), hbm, vmem],
        out_specs=(hbm, vmem),
        scratch_shapes=[
            pltpu.VMEM((slab + 1, total, lanes), jnp.bfloat16),
            pltpu.VMEM((total, LANES), jnp.bfloat16),
            pltpu.VMEM((slab, total, lanes), jnp.bfloat16),
            pltpu.VMEM((lanes, lanes), jnp.bfloat16),
            pltpu.VMEM(sent.shape, jnp.bfloat16),
            pltpu.VMEM((doms, slab, width), jnp.float32),
            order,
            order,
            field,
            field,
            pltpu.VMEM((levels, planes * part, LANES), jnp.float32),
            pltpu.VMEM((planes + 1, mine, width), jnp.bfloat16),
            pltpu.VMEM((doms, mine, groups * LANES), jnp.bfloat16),
        ]
        + [triangle] * 6
        + [square] * 4
        + [
            pltpu.VMEM((lanes // LANES, total // 2 * slab, LANES), jnp.float32),
            pltpu.VMEM((total, slab, lanes), jnp.bfloat16),
            dma((chunks, doms)),
            dma((chunks, doms)),
            dma((doms,)),
            dma((doms,)),
            dma((2, chunks, devices)),
            dma((2, chunks, devices)),
        ]
        + [dma((2, 3, most))] * 4
        + [dma((groups,))] * 2,
        cost_estimate=pl.CostEstimate(flops=60 * total**3, bytes_accessed=8 << 20, transcendentals=0),
        compiler_params=pltpu.CompilerParams(vmem_limit_bytes=48 << 20, collective_id=2, has_side_effects=True),
    )(bounds, sent, potential)


def body_plain(orbitals, potential, bounds):
    bands, slab, width = orbitals.shape
    doms = lax.axis_size("dom")
    groups = lax.axis_size("band")
    devices = doms * groups
    total_bands = bands * groups
    mine = bands // doms
    everyone = ("dom", "band")
    half_width = (bounds[1] - bounds[0]) / 2.0
    centre = (bounds[1] + bounds[0]) / 2.0
    cell_volume = 1.0 / (slab * doms * width)

    sent = orbitals.reshape(doms, mine, slab, width).transpose(0, 2, 1, 3)
    cells = lax.all_to_all(sent, "dom", split_axis=0, concat_axis=0, tiled=True)
    cells = cells.reshape(doms * slab, mine, width)
    pot = lax.all_to_all(
        jnp.broadcast_to(potential, (doms, slab, width)), "dom", split_axis=0, concat_axis=0, tiled=True
    ).reshape(doms * slab, 1, width)
    filt, applied = filter_bands(cells, pot, jnp.stack([1.0 / half_width, centre]), devices)
    filt = lax.all_to_all(filt, everyone, split_axis=0, concat_axis=0, tiled=True)
    applied = lax.all_to_all(applied, everyone, split_axis=0, concat_axis=0, tiled=True)
    filt = filt.reshape(total_bands, -1)
    applied = applied.reshape(total_bands, -1)
    bits = exchange_bits(doms, groups)
    square = jax.ShapeDtypeStruct((total_bands, total_bands), jnp.float32)
    rotated, trans = sum_call(
        functools.partial(orthonormal_kernel, bits, cell_volume, (doms, groups, mine)),
        (filt,),
        (jax.ShapeDtypeStruct(filt.shape, jnp.bfloat16), square),
        3,
        bits,
        0,
        40 * total_bands**3,
    )
    out = lax.all_to_all(rotated, "band", split_axis=0, concat_axis=1, tiled=True)
    projected = sum_call(
        functools.partial(project_kernel, bits, cell_volume),
        (filt, applied, trans),
        square,
        0,
        bits,
        1,
        40 * total_bands**3,
    )
    return out.reshape(bands, slab, width), projected


def body(orbitals, potential, bounds):
    bands, slab, width = orbitals.shape
    doms = lax.axis_size("dom")
    groups = lax.axis_size("band")
    mine = bands // doms
    total = bands * groups
    blocks = len(upper_blocks(total))
    if mine % 8 or slab * GRID_Z != LANES or width % (groups * LANES) or total % (2 * LANES) or blocks * LANES % (8 * doms * groups):
        return body_plain(orbitals, potential, bounds)
    cell_volume = 1.0 / (slab * doms * width)
    sent = orbitals.reshape(doms, mine, slab, width).transpose(0, 2, 1, 3)
    return step_call(sent, potential, bounds, groups, cell_volume)


def solution(mesh):
    return jax.shard_map(
        body,
        mesh=mesh,
        in_specs=(P("band", "dom", None), P("dom", None), P()),
        out_specs=(P("band", "dom", None), P()),
        check_vma=False,
    )
```

```python
import functools

import jax
import jax.numpy as jnp
from jax import lax
from jax.experimental import pallas as pl
from jax.experimental.pallas import tpu as pltpu
from jax.sharding import PartitionSpec as P

GRID_Z = 32
DEG = 8
NS_STEPS = 8
LANES = 128
UNROLL = 8
PAUSE = 3
TILE_ROWS = 8


def filter_kernel(scal_ref, cells_ref, pot_ref, sums_ref, filt_ref, applied_ref, field, high, low, coef):
    planes, bands, width = cells_ref.shape
    rows = planes * bands
    blocks_per_plane = filt_ref.shape[0] // planes
    block = filt_ref.shape[2]
    tile = sums_ref.shape[1]
    inv_half = scal_ref[0]
    centre = scal_ref[1]

    for x in range(planes):
        mine = pl.ds(x * bands, bands)
        coef[mine, :] = jnp.broadcast_to(3.0 + pot_ref[x], (bands, width))
        start = cells_ref[x].astype(jnp.float32)
        field[0, mine, :] = start
    for c in range(width // tile):
        cols = pl.ds(c * tile, tile)
        start = field[0, :, cols]
        high[0, :, cols] = start.astype(jnp.bfloat16)
        low[0, :, cols] = jnp.zeros((rows, tile), jnp.bfloat16)

    def shifted(v, by):
        if bands % 8 == 0:
            return jnp.concatenate([v[by:], v[:by]], axis=0)
        return pltpu.roll(v, (rows - by) % rows, 0)

    def neighbours(slot, c, v):
        cols = pl.ds(pl.multiple_of(c * tile, tile), tile)
        left = pl.ds(pl.multiple_of(lax.rem(c * tile + width - LANES, width), LANES), LANES)
        right = pl.ds(pl.multiple_of(lax.rem(c * tile + tile, width), LANES), LANES)

        def part(ref):
            wide = jnp.concatenate([ref[slot, :, left], ref[slot, :, cols], ref[slot, :, right]], axis=1)
            return dot(wide, sums_ref[...])

        return part(high) + part(low) + (shifted(v, bands) + shifted(v, rows - bands))

    def sweep(slot, other, weight, diagonal, first):
        def run(c, carry):
            cols = pl.ds(pl.multiple_of(c * tile, tile), tile)
            v = field[slot, :, cols]
            fresh = weight * neighbours(slot, c, v) + (coef[:, cols] * diagonal[0] + diagonal[1]) * v
            if not first:
                fresh = fresh - field[other, :, cols]
            field[other, :, cols] = fresh
            top, rest = split(fresh)
            high[other, :, cols] = top
            low[other, :, cols] = rest
            return carry

        lax.fori_loop(0, width // tile, run, 0)

    sweep(0, 1, -0.5 * inv_half, (inv_half, -centre * inv_half), True)

    def middle(k, carry):
        slot = lax.rem(k, 2)
        sweep(slot, 1 - slot, -inv_half, (2.0 * inv_half, -2.0 * centre * inv_half), False)
        return carry

    lax.fori_loop(1, DEG, middle, 0)
    slot = DEG % 2
    for c in range(width // tile):
        cols = pl.ds(c * tile, tile)
        v = field[slot, :, cols]
        applied = coef[:, cols] * v - 0.5 * neighbours(slot, c, v)
        piece, inner = divmod(c * tile, block)
        for x in range(planes):
            where = (x * blocks_per_plane + piece, slice(None), pl.ds(inner, tile))
            filt_ref[where] = v[x * bands : (x + 1) * bands].astype(jnp.bfloat16)
            applied_ref[where] = applied[x * bands : (x + 1) * bands].astype(jnp.bfloat16)


def neighbour_sums(tile):
    source = lax.broadcasted_iota(jnp.int32, (tile + 2 * LANES, tile), 0) - LANES
    target = lax.broadcasted_iota(jnp.int32, (tile + 2 * LANES, tile), 1)
    step = source - target
    same_row = (source >= 0) & (source // GRID_Z == target // GRID_Z)
    apart = lax.rem(step + GRID_Z, GRID_Z)
    beside_z = same_row & ((apart == 1) | (apart == GRID_Z - 1))
    beside_y = (step == GRID_Z) | (step == -GRID_Z)
    return (beside_z | beside_y).astype(jnp.bfloat16)


def filter_bands(cells, potential, scalars, devices):
    planes, bands, width = cells.shape
    rows = planes * bands
    block = planes * width // devices
    out = jax.ShapeDtypeStruct((devices, bands, block), jnp.bfloat16)
    vmem = pl.BlockSpec(memory_space=pltpu.VMEM)
    return pl.pallas_call(
        filter_kernel,
        out_shape=(out, out),
        in_specs=[pl.BlockSpec(memory_space=pltpu.SMEM), vmem, vmem, vmem],
        out_specs=(vmem, vmem),
        scratch_shapes=[
            pltpu.VMEM((2, rows, width), jnp.float32),
            pltpu.VMEM((2, rows, width), jnp.bfloat16),
            pltpu.VMEM((2, rows, width), jnp.bfloat16),
            pltpu.VMEM((rows, width), jnp.float32),
        ],
        compiler_params=pltpu.CompilerParams(vmem_limit_bytes=48 << 20),
    )(scalars, cells, potential, neighbour_sums(min(256, block)))


def split(value):
    spread = value * 65537.0
    high = spread - (spread - value)
    return high.astype(jnp.bfloat16), (value - high).astype(jnp.bfloat16)


def dot(a, b):
    return jnp.dot(a, b, preferred_element_type=jnp.float32)


def dot3(a, b):
    (a_high, a_low), (b_high, b_low) = a, b
    return dot(a_high, b_high) + (dot(a_high, b_low) + dot(a_low, b_high))


def exchange_bits(doms, groups):
    dom = [("dom", 1 << i) for i in range(1, (doms - 1).bit_length())]
    band = [("band", 1 << i) for i in range((groups - 1).bit_length())]
    core = [("dom", 1)]
    return core + band[:1] + dom + band[1:], core + dom + band


def gram_sum(bits, cell_volume, filt_ref, other_ref, total, send, recv, gath, send_sem, recv_sem):
    size = filt_ref.shape[0] // 2
    index = {axis: lax.axis_index(axis) for axis in ("dom", "band")}

    def partner(axis, bit):
        mine = lax.rem(index[axis] // bit, 2)
        return mine, {axis: index[axis] + bit - 2 * bit * mine}

    barrier = pltpu.get_barrier_semaphore()
    for axis, bit in bits[0]:
        pl.semaphore_signal(
            barrier, inc=1, device_id=partner(axis, bit)[1], device_id_type=pl.DeviceIdType.MESH
        )

    pairs = (((1,), (1,)), ((), ()))
    for stream in range(2):
        total[stream] = cell_volume * lax.dot_general(
            filt_ref[pl.ds(stream * size, size), :],
            other_ref[...],
            pairs,
            preferred_element_type=jnp.float32,
        )
    pl.semaphore_wait(barrier, len(bits[0]))

    def copy(stream, number, source, target, device):
        made = pltpu.make_async_remote_copy(
            src_ref=source,
            dst_ref=target,
            send_sem=send_sem.at[stream, number],
            recv_sem=recv_sem.at[stream, number],
            device_id=device,
            device_id_type=pl.DeviceIdType.MESH,
        )
        made.start()
        return made

    stages = len(bits[0])
    start = [jnp.int32(0)] * 2
    halved = [[], []]
    length, offset = size, 0
    for stage in range(stages):
        halve = length >= 2 * TILE_ROWS
        count = length // 2 if halve else length
        space = pl.ds(offset, count)
        flight = []
        for stream in range(2):
            axis, bit = bits[stream][stage]
            mine, device = partner(axis, bit)
            give = start[stream] + (1 - mine) * count if halve else start[stream]
            keep = start[stream] + mine * count if halve else start[stream]
            give = pl.multiple_of(give, TILE_ROWS)
            send[stream, space, :] = total[stream, pl.ds(give, count), :]
            flight.append(
                copy(stream, stage, send.at[stream, space], recv.at[stream, space], device)
            )
            start[stream] = pl.multiple_of(keep, TILE_ROWS)
            if halve:
                halved[stream].append((stage, mine, device))
        for stream in range(2):
            flight[stream].wait()
            kept = pl.ds(start[stream], count)
            if halve:
                own = total[stream, kept, :]
            else:
                own = send[stream, space, :]
            total[stream, kept, :] = own + recv[stream, space, :]
        length = count
        offset += count

    for stream in range(2):
        kept = pl.ds(start[stream], length)
        gath[stream, kept, :] = total[stream, kept, :]
    for back in range(len(halved[0]) - 1, -1, -1):
        flight = []
        for stream in range(2):
            stage, mine, device = halved[stream][back]
            area = gath.at[stream, pl.ds(start[stream], length)]
            flight.append(copy(stream, stages + stage, area, area, device))
            start[stream] = pl.multiple_of(start[stream] - mine * length, TILE_ROWS)
        for made in flight:
            made.wait()
        length *= 2


def orthonormal_kernel(
    bits, cell_volume, groups, filt_ref, out_ref, trans_ref,
    total, send, recv, gath, y_ref, z_ref, t_ref, send_sem, recv_sem,
):
    gram_sum(bits, cell_volume, filt_ref, filt_ref, total, send, recv, gath, send_sem, recv_sem)
    size = filt_ref.shape[0]
    outer, inner, width = groups
    row = lax.broadcasted_iota(jnp.int32, (size, size), 0)
    col = lax.broadcasted_iota(jnp.int32, (size, size), 1)
    diag = jnp.where(row == col, 1.5, 0.0)
    corr = gath[...].reshape(size, size)
    scale = jnp.sqrt(jnp.sum(corr * corr) + 1e-06)
    scaled = corr / scale
    factor = diag - 0.5 * scaled
    z_ref[...] = factor
    y_ref[...] = dot3(split(factor), split(scaled))

    def step(k, carry):
        y = split(y_ref[...])
        z = split(z_ref[...])
        factor = split(diag - 0.5 * dot3(z, y))
        y_ref[...] = dot3(factor, y)
        z_ref[...] = dot3(factor, z)
        return carry

    lax.fori_loop(1, NS_STEPS - 1, step, 0)
    y = split(y_ref[...])
    z = split(z_ref[...])
    factor = split(diag - 0.5 * dot3(z, y))
    t_ref[...] = dot3(factor, z) / jnp.sqrt(scale)
    for i in range(outer):
        for j in range(inner):
            trans_ref[pl.ds((j * outer + i) * width, width), :] = t_ref[
                pl.ds((i * inner + j) * width, width), :
            ]
    trans = split(trans_ref[...])
    filt = filt_ref[...]
    out_ref[...] = (dot(trans[0], filt) + dot(trans[1], filt)).astype(jnp.bfloat16)


def project_kernel(
    bits, cell_volume, filt_ref, applied_ref, trans_ref, proj_ref,
    total, send, recv, gath, send_sem, recv_sem,
):
    gram_sum(bits, cell_volume, filt_ref, applied_ref, total, send, recv, gath, send_sem, recv_sem)
    size = filt_ref.shape[0]
    trans = split(trans_ref[...])
    half = split(dot3(trans, split(gath[...].reshape(size, size))))
    contract = (((1,), (1,)), ((), ()))

    def dot_t(a, b):
        return lax.dot_general(a, b, contract, preferred_element_type=jnp.float32)

    proj_ref[...] = dot_t(half[0], trans[0]) + (
        dot_t(half[0], trans[1]) + dot_t(half[1], trans[0])
    )


def sum_call(kernel, operands, out_shape, squares, bits, number, flops):
    size = operands[0].shape[0]
    vmem = pl.BlockSpec(memory_space=pltpu.VMEM)
    room = size // 2 + TILE_ROWS * len(bits[0])
    sems = pltpu.SemaphoreType.DMA((2, 2 * len(bits[0])))
    halves = pltpu.VMEM((2, size // 2, size), jnp.float32)
    stage = pltpu.VMEM((2, room, size), jnp.float32)
    return pl.pallas_call(
        kernel,
        out_shape=out_shape,
        in_specs=[vmem] * len(operands),
        out_specs=jax.tree.map(lambda _: vmem, out_shape),
        scratch_shapes=[halves, stage, stage, halves]
        + [pltpu.VMEM((size, size), jnp.float32)] * squares
        + [sems, sems],
        cost_estimate=pl.CostEstimate(flops=flops, bytes_accessed=8 << 20, transcendentals=0),
        compiler_params=pltpu.CompilerParams(
            vmem_limit_bytes=32 << 20, collective_id=number, has_side_effects=True
        ),
    )(*operands)


def peers(doms, groups):
    dom = lax.axis_index("dom")
    band = lax.axis_index("band")
    rows = [lax.rem(dom + r, doms) for r in range(doms)]
    columns = [lax.rem(band + r, groups) for r in range(groups)]
    return [{"dom": d, "band": b} for b in columns for d in rows]


def remote(source, target, send_sem, recv_sem, device):
    return pltpu.make_async_remote_copy(
        src_ref=source,
        dst_ref=target,
        send_sem=send_sem,
        recv_sem=recv_sem,
        device_id=device,
        device_id_type=pl.DeviceIdType.MESH,
    )


def greet(others):
    barrier = pltpu.get_barrier_semaphore()
    for other in others:
        pl.semaphore_signal(barrier, inc=1, device_id=other, device_id_type=pl.DeviceIdType.MESH)
    return barrier


def lane_orders(perm, back):
    size = perm.shape[0]
    high = size // LANES
    row = lax.broadcasted_iota(jnp.int32, (size, size), 0)
    col = lax.broadcasted_iota(jnp.int32, (size, size), 1)
    grouped = lax.rem(row // GRID_Z, high) * LANES + lax.rem(row, GRID_Z) * high + row // LANES
    perm[...] = jnp.where(grouped == col, 1.0, 0.0).astype(jnp.bfloat16)
    natural = lax.rem(row, high) * LANES + row // LANES * GRID_Z + lax.rem(row // high, GRID_Z)
    back[...] = jnp.where(natural == col, 1.0, 0.0).astype(jnp.bfloat16)


class BlockSum:
    def __init__(self, total, recv, gath, send_sem, recv_sem, levels):
        self.total, self.recv, self.gath = total, recv, gath
        self.send_sem, self.recv_sem, self.levels = send_sem, recv_sem, levels
        self.start, self.length = jnp.int32(0), total.shape[0]
        self.offset, self.copies = 0, []

    def steps(self):
        for level in range(len(self.levels)):
            yield functools.partial(self.scatter, level)
            yield functools.partial(self.add, level)
        for level in range(len(self.levels) - 1, -1, -1):
            yield functools.partial(self.gather, level)
            yield functools.partial(self.join, level)

    def scatter(self, level):
        at, size, device = self.levels[level]
        rows = self.length // size
        self.copies = []
        for r in range(1, size):
            to = lax.rem(at + r, size)
            source = pl.ds(pl.multiple_of(self.start + to * rows, TILE_ROWS), rows)
            place = pl.ds(self.offset + (r - 1) * rows, rows)
            self.copies.append(
                remote(
                    self.total.at[source], self.recv.at[place],
                    self.send_sem.at[0, level, r], self.recv_sem.at[0, level, r], device(to),
                )
            )
        for made in self.copies:
            made.start()

    def add(self, level):
        at, size, _ = self.levels[level]
        rows = self.length // size
        self.start = pl.multiple_of(self.start + at * rows, TILE_ROWS)
        self.length = rows
        kept = pl.ds(self.start, rows)
        for made in self.copies:
            made.wait()
        value = self.total[kept]
        for r in range(1, size):
            value = value + self.recv[pl.ds(self.offset + (r - 1) * rows, rows)]
        self.offset += (size - 1) * rows
        self.total[kept] = value
        if level == len(self.levels) - 1:
            self.gath[kept] = value

    def gather(self, level):
        at, size, device = self.levels[level]
        area = self.gath.at[pl.ds(self.start, self.length)]
        self.copies = [
            remote(area, area, self.send_sem.at[1, level, r], self.recv_sem.at[1, level, r], device(lax.rem(at + r, size)))
            for r in range(1, size)
        ]
        for made in self.copies:
            made.start()

    def join(self, level):
        at, size, _ = self.levels[level]
        for made in self.copies:
            made.wait()
        self.start = pl.multiple_of(self.start - at * self.length, TILE_ROWS)
        self.length *= size


def sum_levels(doms, groups):
    dom = lax.axis_index("dom")
    band = lax.axis_index("band")
    core, chip = lax.rem(dom, 2), dom // 2
    low, high = lax.rem(band, 2), band // 2
    return [
        (core, 2, lambda to: {"dom": chip * 2 + to}),
        (chip * 2 + low, doms, lambda to: {"dom": to // 2 * 2 + core, "band": high * 2 + lax.rem(to, 2)}),
        (high, groups // 2, lambda to: {"band": to * 2 + low}),
    ]


def upper_blocks(total):
    count = total // LANES
    return [(i, j) for i in range(count) for j in range(i, count)]


def next_cells(nexts):
    size = nexts.shape[0]
    row = lax.broadcasted_iota(jnp.int32, (size, size), 0)
    col = lax.broadcasted_iota(jnp.int32, (size, size), 1)
    ahead = col // GRID_Z * GRID_Z + lax.rem(col + 1, GRID_Z)
    nexts[...] = jnp.where((row == ahead) | (row == col + GRID_Z), 1.0, 0.0).astype(jnp.bfloat16)


def gram(factor, left, flipped, packed, halve):
    slab, lanes, total = flipped.shape
    size = 2 * LANES
    count = total // size
    product = {}
    for i in range(count):
        first = 0 if halve else i * size
        block = jnp.zeros((size, total - first), jnp.float32)
        for x in range(slab):
            block = block + dot(left[x, pl.ds(i * size, size), :], flipped[x, :, pl.ds(first, total - first)])
        for a in range(2):
            for j in range(first // LANES, total // LANES):
                column = j * LANES - first
                product[2 * i + a, j] = block[a * LANES : (a + 1) * LANES, column : column + LANES]
    for n, (i, j) in enumerate(upper_blocks(total)):
        value = product[i, j]
        if halve:
            value = 0.5 * (value + product[j, i].T)
        packed[pl.ds(n * LANES, LANES)] = value * factor


def unpack(packed, full):
    for n, (i, j) in enumerate(upper_blocks(full.shape[0])):
        block = packed[pl.ds(n * LANES, LANES)]
        full[pl.ds(i * LANES, LANES), pl.ds(j * LANES, LANES)] = block
        if i != j:
            full[pl.ds(j * LANES, LANES), pl.ds(i * LANES, LANES)] = block.T


def inverse_root(full, work, other, pause):
    size = full.shape[0]
    row = lax.broadcasted_iota(jnp.int32, (size, size), 0)
    col = lax.broadcasted_iota(jnp.int32, (size, size), 1)

    def diagonal(value):
        return jnp.where(row == col, value, 0.0)

    corr = full[...]
    scale = jnp.sqrt(jnp.sum(corr * corr) + 1e-06)
    work[...] = corr / scale
    for double in range(NS_STEPS // 2 - 1):
        held = split(work[...])
        other[...] = dot3(held, held)
        pause()
        square = other[...]
        rest = dot3(split(square), split(0.0625 * square - 0.5625 * work[...]))
        factor = split(diagonal(2.25) - 2.4375 * work[...] + (1.6875 * square + rest))
        pause()
        if double == 0:
            full[...] = factor[0].astype(jnp.float32) + factor[1].astype(jnp.float32)
        else:
            full[...] = dot3(split(full[...]), factor)
            pause()
        other[...] = dot3(held, factor)
        pause()
        work[...] = dot3(split(other[...]), factor)
        pause()
    left = diagonal(1.0) - work[...]
    rounded = left.astype(jnp.bfloat16)
    square = dot(rounded, rounded)
    rest = 0.5 * left + 0.375 * square
    rest = rest + dot(square.astype(jnp.bfloat16), (0.3125 * left + 0.0625 * square).astype(jnp.bfloat16))
    pause()
    value = full[...]
    value = value + dot(value.astype(jnp.bfloat16), rest.astype(jnp.bfloat16))
    return value / jnp.sqrt(scale)


def step_kernel(
    groups, cell_volume, bounds_ref, sent_ref, pot_ref, out_ref, proj_ref,
    filt_ref, beyond, image_ref, flipped, nexts, stage, pots, perm, back, even, odd, diag, send_f, send_y,
    corr_sum, corr_recv, corr_gath, hamil_sum, hamil_recv, hamil_gath, full, work, other, trans, spread, turned,
    in_send, in_recv, pot_send, pot_recv, out_send, out_recv, corr_send, corr_arrive, hamil_send, hamil_arrive, back_send, back_recv,
):
    doms, slab, mine, width = stage.shape
    devices = doms * groups
    dom = lax.axis_index("dom")
    band = lax.axis_index("band")
    planes = doms * slab
    part = min(mine, 8)
    chunks = mine // part
    rows = planes * part
    lanes = width // groups
    levels = width // LANES
    high = LANES // GRID_Z
    spans = levels // high
    half_width = (bounds_ref[1] - bounds_ref[0]) / 2.0
    centre = (bounds_ref[1] + bounds_ref[0]) / 2.0
    inv_half = 1.0 / half_width

    everyone = peers(doms, groups)
    barrier = greet(everyone[1:])
    lane_orders(perm, back)
    pl.semaphore_wait(barrier, len(everyone) - 1)

    def incoming(c, r):
        peer = lax.rem(dom + r, doms)
        some = pl.ds(c * part, part)
        source, target = sent_ref.at[peer, :, some, :], stage.at[dom, :, some, :]
        if r == 0:
            return pltpu.make_async_copy(source, target, in_recv.at[c, r])
        return remote(source, target, in_send.at[c, r], in_recv.at[c, r], {"dom": peer})

    def potential(r):
        if r == 0:
            return pltpu.make_async_copy(pot_ref, pots.at[dom], pot_recv.at[r])
        return remote(pot_ref, pots.at[dom], pot_send.at[r], pot_recv.at[r], {"dom": lax.rem(dom + r, doms)})

    for r in range(doms):
        potential(r).start()
    for c in range(chunks):
        for r in range(doms):
            incoming(c, r).start()

    lane = lax.broadcasted_iota(jnp.int32, (rows, LANES), 1)
    row_of_lane = lax.broadcasted_iota(jnp.int32, (doms, part, LANES), 2) // GRID_Z
    first_high = lax.rem(lane, high) == 0
    last_high = lax.rem(lane, high) == high - 1

    for r in range(doms):
        potential(r).wait()
    for k in range(spans):
        pot = jnp.concatenate(
            [pots[:, :, pl.ds((h * spans + k) * LANES, LANES)].reshape(planes, LANES) for h in range(high)], axis=1
        )
        ordered = jnp.zeros(pot.shape, jnp.float32)
        for piece in range(3):
            top = pot.astype(jnp.bfloat16)
            ordered = ordered + dot(top, perm[...])
            pot = pot - top.astype(jnp.float32)
        scaled = (3.0 + ordered - centre) * (2.0 * inv_half)
        for b in range(high):
            line = scaled[:, b * LANES : (b + 1) * LANES]
            diag[k * high + b] = jnp.broadcast_to(line[:, None, :], (planes, part, LANES)).reshape(rows, LANES)

    def edges(field):
        top = field[levels]
        field[0] = jnp.where(first_high, pltpu.roll(top, LANES - (high - 1), 1), pltpu.roll(top, 1, 1))
        low = field[1]
        field[levels + 1] = jnp.where(last_high, pltpu.roll(low, high - 1, 1), pltpu.roll(low, LANES - 1, 1))

    def image(field, i):
        v = field[i]
        around = pltpu.roll(v, high, 1) + pltpu.roll(v, LANES - high, 1)
        around = around + (field[i - 1] + field[i + 1])
        around = around + (
            jnp.concatenate([v[part:], v[:part]], axis=0) + jnp.concatenate([v[rows - part :], v[: rows - part]], axis=0)
        )
        return diag[i - 1] * v - inv_half * around, v

    def sweep(source, target, first):
        def run(j, carry):
            for i in range(UNROLL):
                i = 1 + j * UNROLL + i
                fresh = image(source, i)[0]
                target[i] = 0.5 * fresh if first else fresh - target[i]
            return carry

        lax.fori_loop(0, levels // UNROLL, run, 0)
        edges(target)

    first_row = pl.multiple_of((band * doms + dom) * mine, part)

    def outgoing(pieces):
        copies = []
        for r, device in enumerate(everyone):
            for which, piece, place in pieces(device):
                recv = out_recv.at[which, r]
                if r == 0:
                    copies.append(pltpu.make_async_copy(piece, place, recv))
                else:
                    copies.append(remote(piece, place, out_send.at[which, r], recv, device))
        return copies

    def block(device):
        return pl.ds(pl.multiple_of(device["band"] * lanes, LANES), lanes)

    def main(c, device):
        source = send_f.at[pl.ds(device["dom"] * slab, slab), pl.ds(c * part, part), block(device)]
        return [(c, source, filt_ref.at[pl.ds(0, slab), pl.ds(first_row + c * part, part), :])]

    def halo(device):
        above = pl.ds(pl.multiple_of(lax.rem(device["band"] + 1, groups) * LANES, LANES), LANES)
        rows_here = pl.ds(first_row, mine)
        return [
            (chunks, send_f.at[device["dom"] * slab + slab, :, block(device)], filt_ref.at[slab, rows_here, :]),
            (chunks + 1, send_y.at[device["dom"], :, above], beyond.at[rows_here, :]),
        ]

    for c in range(chunks):
        for r in range(doms):
            incoming(c, r).wait()
        some = pl.ds(c * part, part)
        for k in range(spans):
            cells = jnp.concatenate(
                [
                    stage[:, :, some, pl.ds((h * spans + k) * LANES, LANES)].astype(jnp.float32).reshape(rows, LANES)
                    for h in range(high)
                ],
                axis=1,
            )
            ordered = dot(cells.astype(jnp.bfloat16), perm[...])
            for b in range(high):
                even[1 + k * high + b] = ordered[:, b * LANES : (b + 1) * LANES]
        edges(even)
        sweep(even, odd, True)

        def pair(k, carry):
            sweep(odd, even, False)
            sweep(even, odd, False)
            return carry

        lax.fori_loop(0, (DEG - 1) // 2, pair, 0)
        last = odd
        if DEG % 2 == 0:
            sweep(odd, even, False)
            last = even

        for k in range(spans):
            values = [last[1 + k * high + b] for b in range(high)]
            natural = dot(jnp.concatenate(values, axis=1).astype(jnp.bfloat16), back[...])
            for h in range(high):
                column = (h * spans + k) * LANES
                value = natural[:, h * LANES : (h + 1) * LANES].reshape(planes, part, LANES)
                send_f[pl.ds(0, planes), some, pl.ds(column, LANES)] = value.astype(jnp.bfloat16)
                send_f[planes, some, pl.ds(column, LANES)] = value[0].astype(jnp.bfloat16)
                if column % lanes == 0:
                    value = value.reshape(doms, slab * part, LANES)
                    edge = value[:, :part]
                    for x in range(1, slab):
                        moved = value[:, x * part : (x + 1) * part].reshape(doms * part, LANES)
                        moved = pltpu.roll(moved, x * GRID_Z, 1).reshape(doms, part, LANES)
                        edge = jnp.where(row_of_lane == x, moved, edge)
                    send_y[:, some, pl.ds(column // lanes * LANES, LANES)] = edge.astype(jnp.bfloat16)
        for copy in outgoing(functools.partial(main, c)):
            copy.start()
    for copy in outgoing(halo):
        copy.start()
    next_cells(nexts)
    for c in range(chunks):
        for copy in outgoing(functools.partial(main, c)):
            copy.wait()

    total = filt_ref.shape[1]
    for x in range(slab):
        flipped[x] = filt_ref[x].T
    gram(cell_volume, filt_ref, flipped, corr_sum, False)
    corr = BlockSum(corr_sum, corr_recv, corr_gath, corr_send, corr_arrive, sum_levels(doms, groups))
    steps = list(corr.steps())
    steps[0]()
    for copy in outgoing(halo):
        copy.wait()
    edge = lax.broadcasted_iota(jnp.int32, (total, LANES), 1) >= LANES - GRID_Z
    for x in range(slab):
        pot = 3.0 + pot_ref[pl.ds(x, 1), pl.ds(pl.multiple_of(band * lanes, LANES), lanes)]
        value = filt_ref[x].astype(jnp.float32) * pot - filt_ref[x + 1].astype(jnp.float32)
        value = value - dot(filt_ref[x], nexts[...])
        after = pltpu.roll(beyond[...].astype(jnp.float32), (LANES - GRID_Z - x * GRID_Z) % LANES, 1)
        image_ref[x, :, pl.ds(0, lanes - LANES)] = value[:, : lanes - LANES].astype(jnp.bfloat16)
        image_ref[x, :, pl.ds(lanes - LANES, LANES)] = (
            value[:, lanes - LANES :] - jnp.where(edge, after, 0.0)
        ).astype(jnp.bfloat16)
    for step in steps[1:3]:
        step()
    gram(cell_volume, image_ref, flipped, hamil_sum, True)
    hamil = BlockSum(hamil_sum, hamil_recv, hamil_gath, hamil_send, hamil_arrive, sum_levels(doms, groups))
    pending = list(hamil.steps())
    pending.pop(0)()
    steps = steps[3:]
    while steps:
        for _ in range(2):
            if steps:
                steps.pop(0)()
        for _ in range(2):
            if steps:
                pending.pop(0)()
    unpack(corr_gath, full)

    def pause():
        for _ in range(2):
            if len(pending) > 1:
                pending.pop(0)()

    calls = [0]

    def sometimes():
        calls[0] += 1
        if calls[0] % PAUSE == 0:
            pause()

    value = inverse_root(full, work, other, sometimes)
    trans[...] = value
    turn = split(value.T)

    bands = out_ref.shape[0]
    half = total // 2
    returned = []
    for part_rows in range(2):
        for x in range(slab):
            points = filt_ref[x]
            piece = [t[part_rows * half : (part_rows + 1) * half] for t in turn]
            product = dot(piece[0], points) + dot(piece[1], points)
            for n in range(lanes // LANES):
                spread[n, pl.ds(x, half, stride=slab), :] = product[:, n * LANES : (n + 1) * LANES]
        for n in range(lanes // LANES):
            turned[pl.ds(part_rows * half, half), :, pl.ds(n * LANES, LANES)] = (
                spread[n].reshape(half, slab, LANES).astype(jnp.bfloat16)
            )
        place = out_ref.at[:, :, pl.ds(pl.multiple_of(band * lanes, LANES), lanes)]
        for q in range(groups // 2):
            to = part_rows * (groups // 2) + q
            source = turned.at[pl.ds(to * bands, bands)]
            returned.append((to, source, place))

            @pl.when(band == to)
            def _():
                pltpu.make_async_copy(source, place, back_recv.at[band]).start()

            @pl.when(band != to)
            def _():
                remote(source, place, back_send.at[to], back_recv.at[band], {"band": to}).start()

    while pending:
        pending.pop(0)()
    unpack(hamil_gath, full)
    transposed = split(trans[...].T)
    halfway = split(dot3(transposed, split(full[...])))
    proj_ref[...] = dot3(halfway, split(trans[...]))

    for to, source, place in returned:
        theirs = out_ref.at[:, :, pl.ds(to * lanes, lanes)]

        @pl.when(band == to)
        def _():
            pltpu.make_async_copy(source, place, back_recv.at[band]).wait()

        @pl.when(band != to)
        def _():
            remote(source, place, back_send.at[to], back_recv.at[band], {"band": to}).wait_send()
            remote(source, theirs, back_send.at[to], back_recv.at[to], {"band": to}).wait_recv()


def step_call(sent, potential, bounds, groups, cell_volume):
    doms, slab, mine, width = sent.shape
    devices = doms * groups
    total = devices * mine
    planes = doms * slab
    part = min(mine, 8)
    chunks = mine // part
    levels = width // LANES
    lanes = width // groups
    size = LANES * (LANES // GRID_Z)
    packed = LANES * len(upper_blocks(total))
    vmem = pl.BlockSpec(memory_space=pltpu.VMEM)
    hbm = pl.BlockSpec(memory_space=pl.ANY)
    order = pltpu.VMEM((size, size), jnp.bfloat16)
    field = pltpu.VMEM((levels + 2, planes * part, LANES), jnp.float32)
    triangle = pltpu.VMEM((packed, LANES), jnp.float32)
    square = pltpu.VMEM((total, total), jnp.float32)
    dma = pltpu.SemaphoreType.DMA
    most = max(2, doms, groups // 2)
    return pl.pallas_call(
        functools.partial(step_kernel, groups, cell_volume),
        out_shape=(
            jax.ShapeDtypeStruct((mine * doms, slab, width), jnp.bfloat16),
            jax.ShapeDtypeStruct((total, total), jnp.float32),
        ),
        in_specs=[pl.BlockSpec(memory_space=pltpu.SMEM), hbm, vmem],
        out_specs=(hbm, vmem),
        scratch_shapes=[
            pltpu.VMEM((slab + 1, total, lanes), jnp.bfloat16),
            pltpu.VMEM((total, LANES), jnp.bfloat16),
            pltpu.VMEM((slab, total, lanes), jnp.bfloat16),
            pltpu.VMEM((slab, lanes, total), jnp.bfloat16),
            pltpu.VMEM((lanes, lanes), jnp.bfloat16),
            pltpu.VMEM(sent.shape, jnp.bfloat16),
            pltpu.VMEM((doms, slab, width), jnp.float32),
            order,
            order,
            field,
            field,
            pltpu.VMEM((levels, planes * part, LANES), jnp.float32),
            pltpu.VMEM((planes + 1, mine, width), jnp.bfloat16),
            pltpu.VMEM((doms, mine, groups * LANES), jnp.bfloat16),
        ]
        + [triangle] * 6
        + [square] * 4
        + [
            pltpu.VMEM((lanes // LANES, total // 2 * slab, LANES), jnp.float32),
            pltpu.VMEM((total, slab, lanes), jnp.bfloat16),
            dma((chunks, doms)),
            dma((chunks, doms)),
            dma((doms,)),
            dma((doms,)),
            dma((chunks + 2, devices)),
            dma((chunks + 2, devices)),
        ]
        + [dma((2, 3, most))] * 4
        + [dma((groups,))] * 2,
        cost_estimate=pl.CostEstimate(flops=60 * total**3, bytes_accessed=8 << 20, transcendentals=0),
        compiler_params=pltpu.CompilerParams(vmem_limit_bytes=48 << 20, collective_id=2, has_side_effects=True),
    )(bounds, sent, potential)


def body_plain(orbitals, potential, bounds):
    bands, slab, width = orbitals.shape
    doms = lax.axis_size("dom")
    groups = lax.axis_size("band")
    devices = doms * groups
    total_bands = bands * groups
    mine = bands // doms
    everyone = ("dom", "band")
    half_width = (bounds[1] - bounds[0]) / 2.0
    centre = (bounds[1] + bounds[0]) / 2.0
    cell_volume = 1.0 / (slab * doms * width)

    sent = orbitals.reshape(doms, mine, slab, width).transpose(0, 2, 1, 3)
    cells = lax.all_to_all(sent, "dom", split_axis=0, concat_axis=0, tiled=True)
    cells = cells.reshape(doms * slab, mine, width)
    pot = lax.all_to_all(
        jnp.broadcast_to(potential, (doms, slab, width)), "dom", split_axis=0, concat_axis=0, tiled=True
    ).reshape(doms * slab, 1, width)
    filt, applied = filter_bands(cells, pot, jnp.stack([1.0 / half_width, centre]), devices)
    filt = lax.all_to_all(filt, everyone, split_axis=0, concat_axis=0, tiled=True)
    applied = lax.all_to_all(applied, everyone, split_axis=0, concat_axis=0, tiled=True)
    filt = filt.reshape(total_bands, -1)
    applied = applied.reshape(total_bands, -1)
    bits = exchange_bits(doms, groups)
    square = jax.ShapeDtypeStruct((total_bands, total_bands), jnp.float32)
    rotated, trans = sum_call(
        functools.partial(orthonormal_kernel, bits, cell_volume, (doms, groups, mine)),
        (filt,),
        (jax.ShapeDtypeStruct(filt.shape, jnp.bfloat16), square),
        3,
        bits,
        0,
        40 * total_bands**3,
    )
    out = lax.all_to_all(rotated, "band", split_axis=0, concat_axis=1, tiled=True)
    projected = sum_call(
        functools.partial(project_kernel, bits, cell_volume),
        (filt, applied, trans),
        square,
        0,
        bits,
        1,
        40 * total_bands**3,
    )
    return out.reshape(bands, slab, width), projected


def body(orbitals, potential, bounds):
    bands, slab, width = orbitals.shape
    doms = lax.axis_size("dom")
    groups = lax.axis_size("band")
    mine = bands // doms
    total = bands * groups
    blocks = len(upper_blocks(total))
    if mine % 8 or slab * GRID_Z != LANES or width % (groups * LANES) or total % (2 * LANES) or blocks * LANES % (8 * doms * groups):
        return body_plain(orbitals, potential, bounds)
    cell_volume = 1.0 / (slab * doms * width)
    sent = orbitals.reshape(doms, mine, slab, width).transpose(0, 2, 1, 3)
    return step_call(sent, potential, bounds, groups, cell_volume)


def solution(mesh):
    return jax.shard_map(
        body,
        mesh=mesh,
        in_specs=(P("band", "dom", None), P("dom", None), P()),
        out_specs=(P("band", "dom", None), P()),
        check_vma=False,
    )
```

```python
import functools

import jax
import jax.numpy as jnp
from jax import lax
from jax.experimental import pallas as pl
from jax.experimental.pallas import tpu as pltpu
from jax.sharding import PartitionSpec as P

GRID_Z = 32
DEG = 8
NS_STEPS = 8
LANES = 128
UNROLL = 8
PAUSE = 3
TILE_ROWS = 8


def filter_kernel(scal_ref, cells_ref, pot_ref, sums_ref, filt_ref, applied_ref, field, high, low, coef):
    planes, bands, width = cells_ref.shape
    rows = planes * bands
    blocks_per_plane = filt_ref.shape[0] // planes
    block = filt_ref.shape[2]
    tile = sums_ref.shape[1]
    inv_half = scal_ref[0]
    centre = scal_ref[1]

    for x in range(planes):
        mine = pl.ds(x * bands, bands)
        coef[mine, :] = jnp.broadcast_to(3.0 + pot_ref[x], (bands, width))
        start = cells_ref[x].astype(jnp.float32)
        field[0, mine, :] = start
    for c in range(width // tile):
        cols = pl.ds(c * tile, tile)
        start = field[0, :, cols]
        high[0, :, cols] = start.astype(jnp.bfloat16)
        low[0, :, cols] = jnp.zeros((rows, tile), jnp.bfloat16)

    def shifted(v, by):
        if bands % 8 == 0:
            return jnp.concatenate([v[by:], v[:by]], axis=0)
        return pltpu.roll(v, (rows - by) % rows, 0)

    def neighbours(slot, c, v):
        cols = pl.ds(pl.multiple_of(c * tile, tile), tile)
        left = pl.ds(pl.multiple_of(lax.rem(c * tile + width - LANES, width), LANES), LANES)
        right = pl.ds(pl.multiple_of(lax.rem(c * tile + tile, width), LANES), LANES)

        def part(ref):
            wide = jnp.concatenate([ref[slot, :, left], ref[slot, :, cols], ref[slot, :, right]], axis=1)
            return dot(wide, sums_ref[...])

        return part(high) + part(low) + (shifted(v, bands) + shifted(v, rows - bands))

    def sweep(slot, other, weight, diagonal, first):
        def run(c, carry):
            cols = pl.ds(pl.multiple_of(c * tile, tile), tile)
            v = field[slot, :, cols]
            fresh = weight * neighbours(slot, c, v) + (coef[:, cols] * diagonal[0] + diagonal[1]) * v
            if not first:
                fresh = fresh - field[other, :, cols]
            field[other, :, cols] = fresh
            top, rest = split(fresh)
            high[other, :, cols] = top
            low[other, :, cols] = rest
            return carry

        lax.fori_loop(0, width // tile, run, 0)

    sweep(0, 1, -0.5 * inv_half, (inv_half, -centre * inv_half), True)

    def middle(k, carry):
        slot = lax.rem(k, 2)
        sweep(slot, 1 - slot, -inv_half, (2.0 * inv_half, -2.0 * centre * inv_half), False)
        return carry

    lax.fori_loop(1, DEG, middle, 0)
    slot = DEG % 2
    for c in range(width // tile):
        cols = pl.ds(c * tile, tile)
        v = field[slot, :, cols]
        applied = coef[:, cols] * v - 0.5 * neighbours(slot, c, v)
        piece, inner = divmod(c * tile, block)
        for x in range(planes):
            where = (x * blocks_per_plane + piece, slice(None), pl.ds(inner, tile))
            filt_ref[where] = v[x * bands : (x + 1) * bands].astype(jnp.bfloat16)
            applied_ref[where] = applied[x * bands : (x + 1) * bands].astype(jnp.bfloat16)


def neighbour_sums(tile):
    source = lax.broadcasted_iota(jnp.int32, (tile + 2 * LANES, tile), 0) - LANES
    target = lax.broadcasted_iota(jnp.int32, (tile + 2 * LANES, tile), 1)
    step = source - target
    same_row = (source >= 0) & (source // GRID_Z == target // GRID_Z)
    apart = lax.rem(step + GRID_Z, GRID_Z)
    beside_z = same_row & ((apart == 1) | (apart == GRID_Z - 1))
    beside_y = (step == GRID_Z) | (step == -GRID_Z)
    return (beside_z | beside_y).astype(jnp.bfloat16)


def filter_bands(cells, potential, scalars, devices):
    planes, bands, width = cells.shape
    rows = planes * bands
    block = planes * width // devices
    out = jax.ShapeDtypeStruct((devices, bands, block), jnp.bfloat16)
    vmem = pl.BlockSpec(memory_space=pltpu.VMEM)
    return pl.pallas_call(
        filter_kernel,
        out_shape=(out, out),
        in_specs=[pl.BlockSpec(memory_space=pltpu.SMEM), vmem, vmem, vmem],
        out_specs=(vmem, vmem),
        scratch_shapes=[
            pltpu.VMEM((2, rows, width), jnp.float32),
            pltpu.VMEM((2, rows, width), jnp.bfloat16),
            pltpu.VMEM((2, rows, width), jnp.bfloat16),
            pltpu.VMEM((rows, width), jnp.float32),
        ],
        compiler_params=pltpu.CompilerParams(vmem_limit_bytes=48 << 20),
    )(scalars, cells, potential, neighbour_sums(min(256, block)))


def split(value):
    spread = value * 65537.0
    high = spread - (spread - value)
    return high.astype(jnp.bfloat16), (value - high).astype(jnp.bfloat16)


def dot(a, b):
    return jnp.dot(a, b, preferred_element_type=jnp.float32)


def dot3(a, b):
    (a_high, a_low), (b_high, b_low) = a, b
    return dot(a_high, b_high) + (dot(a_high, b_low) + dot(a_low, b_high))


def exchange_bits(doms, groups):
    dom = [("dom", 1 << i) for i in range(1, (doms - 1).bit_length())]
    band = [("band", 1 << i) for i in range((groups - 1).bit_length())]
    core = [("dom", 1)]
    return core + band[:1] + dom + band[1:], core + dom + band


def gram_sum(bits, cell_volume, filt_ref, other_ref, total, send, recv, gath, send_sem, recv_sem):
    size = filt_ref.shape[0] // 2
    index = {axis: lax.axis_index(axis) for axis in ("dom", "band")}

    def partner(axis, bit):
        mine = lax.rem(index[axis] // bit, 2)
        return mine, {axis: index[axis] + bit - 2 * bit * mine}

    barrier = pltpu.get_barrier_semaphore()
    for axis, bit in bits[0]:
        pl.semaphore_signal(
            barrier, inc=1, device_id=partner(axis, bit)[1], device_id_type=pl.DeviceIdType.MESH
        )

    pairs = (((1,), (1,)), ((), ()))
    for stream in range(2):
        total[stream] = cell_volume * lax.dot_general(
            filt_ref[pl.ds(stream * size, size), :],
            other_ref[...],
            pairs,
            preferred_element_type=jnp.float32,
        )
    pl.semaphore_wait(barrier, len(bits[0]))

    def copy(stream, number, source, target, device):
        made = pltpu.make_async_remote_copy(
            src_ref=source,
            dst_ref=target,
            send_sem=send_sem.at[stream, number],
            recv_sem=recv_sem.at[stream, number],
            device_id=device,
            device_id_type=pl.DeviceIdType.MESH,
        )
        made.start()
        return made

    stages = len(bits[0])
    start = [jnp.int32(0)] * 2
    halved = [[], []]
    length, offset = size, 0
    for stage in range(stages):
        halve = length >= 2 * TILE_ROWS
        count = length // 2 if halve else length
        space = pl.ds(offset, count)
        flight = []
        for stream in range(2):
            axis, bit = bits[stream][stage]
            mine, device = partner(axis, bit)
            give = start[stream] + (1 - mine) * count if halve else start[stream]
            keep = start[stream] + mine * count if halve else start[stream]
            give = pl.multiple_of(give, TILE_ROWS)
            send[stream, space, :] = total[stream, pl.ds(give, count), :]
            flight.append(
                copy(stream, stage, send.at[stream, space], recv.at[stream, space], device)
            )
            start[stream] = pl.multiple_of(keep, TILE_ROWS)
            if halve:
                halved[stream].append((stage, mine, device))
        for stream in range(2):
            flight[stream].wait()
            kept = pl.ds(start[stream], count)
            if halve:
                own = total[stream, kept, :]
            else:
                own = send[stream, space, :]
            total[stream, kept, :] = own + recv[stream, space, :]
        length = count
        offset += count

    for stream in range(2):
        kept = pl.ds(start[stream], length)
        gath[stream, kept, :] = total[stream, kept, :]
    for back in range(len(halved[0]) - 1, -1, -1):
        flight = []
        for stream in range(2):
            stage, mine, device = halved[stream][back]
            area = gath.at[stream, pl.ds(start[stream], length)]
            flight.append(copy(stream, stages + stage, area, area, device))
            start[stream] = pl.multiple_of(start[stream] - mine * length, TILE_ROWS)
        for made in flight:
            made.wait()
        length *= 2


def orthonormal_kernel(
    bits, cell_volume, groups, filt_ref, out_ref, trans_ref,
    total, send, recv, gath, y_ref, z_ref, t_ref, send_sem, recv_sem,
):
    gram_sum(bits, cell_volume, filt_ref, filt_ref, total, send, recv, gath, send_sem, recv_sem)
    size = filt_ref.shape[0]
    outer, inner, width = groups
    row = lax.broadcasted_iota(jnp.int32, (size, size), 0)
    col = lax.broadcasted_iota(jnp.int32, (size, size), 1)
    diag = jnp.where(row == col, 1.5, 0.0)
    corr = gath[...].reshape(size, size)
    scale = jnp.sqrt(jnp.sum(corr * corr) + 1e-06)
    scaled = corr / scale
    factor = diag - 0.5 * scaled
    z_ref[...] = factor
    y_ref[...] = dot3(split(factor), split(scaled))

    def step(k, carry):
        y = split(y_ref[...])
        z = split(z_ref[...])
        factor = split(diag - 0.5 * dot3(z, y))
        y_ref[...] = dot3(factor, y)
        z_ref[...] = dot3(factor, z)
        return carry

    lax.fori_loop(1, NS_STEPS - 1, step, 0)
    y = split(y_ref[...])
    z = split(z_ref[...])
    factor = split(diag - 0.5 * dot3(z, y))
    t_ref[...] = dot3(factor, z) / jnp.sqrt(scale)
    for i in range(outer):
        for j in range(inner):
            trans_ref[pl.ds((j * outer + i) * width, width), :] = t_ref[
                pl.ds((i * inner + j) * width, width), :
            ]
    trans = split(trans_ref[...])
    filt = filt_ref[...]
    out_ref[...] = (dot(trans[0], filt) + dot(trans[1], filt)).astype(jnp.bfloat16)


def project_kernel(
    bits, cell_volume, filt_ref, applied_ref, trans_ref, proj_ref,
    total, send, recv, gath, send_sem, recv_sem,
):
    gram_sum(bits, cell_volume, filt_ref, applied_ref, total, send, recv, gath, send_sem, recv_sem)
    size = filt_ref.shape[0]
    trans = split(trans_ref[...])
    half = split(dot3(trans, split(gath[...].reshape(size, size))))
    contract = (((1,), (1,)), ((), ()))

    def dot_t(a, b):
        return lax.dot_general(a, b, contract, preferred_element_type=jnp.float32)

    proj_ref[...] = dot_t(half[0], trans[0]) + (
        dot_t(half[0], trans[1]) + dot_t(half[1], trans[0])
    )


def sum_call(kernel, operands, out_shape, squares, bits, number, flops):
    size = operands[0].shape[0]
    vmem = pl.BlockSpec(memory_space=pltpu.VMEM)
    room = size // 2 + TILE_ROWS * len(bits[0])
    sems = pltpu.SemaphoreType.DMA((2, 2 * len(bits[0])))
    halves = pltpu.VMEM((2, size // 2, size), jnp.float32)
    stage = pltpu.VMEM((2, room, size), jnp.float32)
    return pl.pallas_call(
        kernel,
        out_shape=out_shape,
        in_specs=[vmem] * len(operands),
        out_specs=jax.tree.map(lambda _: vmem, out_shape),
        scratch_shapes=[halves, stage, stage, halves]
        + [pltpu.VMEM((size, size), jnp.float32)] * squares
        + [sems, sems],
        cost_estimate=pl.CostEstimate(flops=flops, bytes_accessed=8 << 20, transcendentals=0),
        compiler_params=pltpu.CompilerParams(
            vmem_limit_bytes=32 << 20, collective_id=number, has_side_effects=True
        ),
    )(*operands)


def peers(doms, groups):
    dom = lax.axis_index("dom")
    band = lax.axis_index("band")
    rows = [lax.rem(dom + r, doms) for r in range(doms)]
    columns = [lax.rem(band + r, groups) for r in range(groups)]
    return [{"dom": d, "band": b} for b in columns for d in rows]


def remote(source, target, send_sem, recv_sem, device):
    return pltpu.make_async_remote_copy(
        src_ref=source,
        dst_ref=target,
        send_sem=send_sem,
        recv_sem=recv_sem,
        device_id=device,
        device_id_type=pl.DeviceIdType.MESH,
    )


def greet(others):
    barrier = pltpu.get_barrier_semaphore()
    for other in others:
        pl.semaphore_signal(barrier, inc=1, device_id=other, device_id_type=pl.DeviceIdType.MESH)
    return barrier


def lane_orders(perm, back):
    size = perm.shape[0]
    high = size // LANES
    row = lax.broadcasted_iota(jnp.int32, (size, size), 0)
    col = lax.broadcasted_iota(jnp.int32, (size, size), 1)
    grouped = lax.rem(row // GRID_Z, high) * LANES + lax.rem(row, GRID_Z) * high + row // LANES
    perm[...] = jnp.where(grouped == col, 1.0, 0.0).astype(jnp.bfloat16)
    natural = lax.rem(row, high) * LANES + row // LANES * GRID_Z + lax.rem(row // high, GRID_Z)
    back[...] = jnp.where(natural == col, 1.0, 0.0).astype(jnp.bfloat16)


class BlockSum:
    def __init__(self, total, recv, gath, send_sem, recv_sem, levels):
        self.total, self.recv, self.gath = total, recv, gath
        self.send_sem, self.recv_sem, self.levels = send_sem, recv_sem, levels
        self.start, self.length = jnp.int32(0), total.shape[0]
        self.offset, self.copies = 0, []

    def steps(self):
        for level in range(len(self.levels)):
            yield functools.partial(self.scatter, level)
            yield functools.partial(self.add, level)
        for level in range(len(self.levels) - 1, -1, -1):
            yield functools.partial(self.gather, level)
            yield functools.partial(self.join, level)

    def scatter(self, level):
        at, size, device = self.levels[level]
        rows = self.length // size
        self.copies = []
        for r in range(1, size):
            to = lax.rem(at + r, size)
            source = pl.ds(pl.multiple_of(self.start + to * rows, TILE_ROWS), rows)
            place = pl.ds(self.offset + (r - 1) * rows, rows)
            self.copies.append(
                remote(
                    self.total.at[source], self.recv.at[place],
                    self.send_sem.at[0, level, r], self.recv_sem.at[0, level, r], device(to),
                )
            )
        for made in self.copies:
            made.start()

    def add(self, level):
        at, size, _ = self.levels[level]
        rows = self.length // size
        self.start = pl.multiple_of(self.start + at * rows, TILE_ROWS)
        self.length = rows
        kept = pl.ds(self.start, rows)
        for made in self.copies:
            made.wait()
        value = self.total[kept]
        for r in range(1, size):
            value = value + self.recv[pl.ds(self.offset + (r - 1) * rows, rows)]
        self.offset += (size - 1) * rows
        self.total[kept] = value
        if level == len(self.levels) - 1:
            self.gath[kept] = value

    def gather(self, level):
        at, size, device = self.levels[level]
        area = self.gath.at[pl.ds(self.start, self.length)]
        self.copies = [
            remote(area, area, self.send_sem.at[1, level, r], self.recv_sem.at[1, level, r], device(lax.rem(at + r, size)))
            for r in range(1, size)
        ]
        for made in self.copies:
            made.start()

    def join(self, level):
        at, size, _ = self.levels[level]
        for made in self.copies:
            made.wait()
        self.start = pl.multiple_of(self.start - at * self.length, TILE_ROWS)
        self.length *= size


def sum_levels(doms, groups):
    dom = lax.axis_index("dom")
    band = lax.axis_index("band")
    core, chip = lax.rem(dom, 2), dom // 2
    low, high = lax.rem(band, 2), band // 2
    return [
        (core, 2, lambda to: {"dom": chip * 2 + to}),
        (chip * 2 + low, doms, lambda to: {"dom": to // 2 * 2 + core, "band": high * 2 + lax.rem(to, 2)}),
        (high, groups // 2, lambda to: {"band": to * 2 + low}),
    ]


def upper_blocks(total):
    count = total // LANES
    return [(i, j) for i in range(count) for j in range(i, count)]


def next_cells(nexts):
    size = nexts.shape[0]
    row = lax.broadcasted_iota(jnp.int32, (size, size), 0)
    col = lax.broadcasted_iota(jnp.int32, (size, size), 1)
    ahead = col // GRID_Z * GRID_Z + lax.rem(col + 1, GRID_Z)
    nexts[...] = jnp.where((row == ahead) | (row == col + GRID_Z), 1.0, 0.0).astype(jnp.bfloat16)


def gram(factor, left, flipped, packed, halve):
    slab, lanes, total = flipped.shape
    size = 2 * LANES
    count = total // size
    product = {}
    for i in range(count):
        first = 0 if halve else i * size
        block = jnp.zeros((size, total - first), jnp.float32)
        for x in range(slab):
            block = block + dot(left[x, pl.ds(i * size, size), :], flipped[x, :, pl.ds(first, total - first)])
        for a in range(2):
            for j in range(first // LANES, total // LANES):
                column = j * LANES - first
                product[2 * i + a, j] = block[a * LANES : (a + 1) * LANES, column : column + LANES]
    for n, (i, j) in enumerate(upper_blocks(total)):
        value = product[i, j]
        if halve:
            value = 0.5 * (value + product[j, i].T)
        packed[pl.ds(n * LANES, LANES)] = value * factor


def unpack(packed, full):
    for n, (i, j) in enumerate(upper_blocks(full.shape[0])):
        block = packed[pl.ds(n * LANES, LANES)]
        full[pl.ds(i * LANES, LANES), pl.ds(j * LANES, LANES)] = block
        if i != j:
            full[pl.ds(j * LANES, LANES), pl.ds(i * LANES, LANES)] = block.T


def inverse_root(full, work, other, pause):
    size = full.shape[0]
    row = lax.broadcasted_iota(jnp.int32, (size, size), 0)
    col = lax.broadcasted_iota(jnp.int32, (size, size), 1)

    def diagonal(value):
        return jnp.where(row == col, value, 0.0)

    corr = full[...]
    scale = jnp.sqrt(jnp.sum(corr * corr) + 1e-06)
    work[...] = corr / scale
    for double in range(NS_STEPS // 2 - 1):
        held = split(work[...])
        square = dot(held[0], held[0])
        rest = dot(square.astype(jnp.bfloat16), (0.0625 * square - 0.5625 * work[...]).astype(jnp.bfloat16))
        factor = split(diagonal(2.25) - 2.4375 * work[...] + (1.6875 * square + rest))
        pause()
        if double == 0:
            full[...] = factor[0].astype(jnp.float32) + factor[1].astype(jnp.float32)
        else:
            full[...] = dot3(split(full[...]), factor)
            pause()
        other[...] = dot3(held, factor)
        pause()
        work[...] = dot3(factor, split(other[...]))
        pause()
    left = diagonal(1.0) - work[...]
    rounded = left.astype(jnp.bfloat16)
    square = dot(rounded, rounded)
    rest = 0.5 * left + 0.375 * square
    rest = rest + dot(square.astype(jnp.bfloat16), (0.3125 * left + 0.0625 * square).astype(jnp.bfloat16))
    pause()
    value = full[...]
    value = value + dot(value.astype(jnp.bfloat16), rest.astype(jnp.bfloat16))
    return value / jnp.sqrt(scale)


def step_kernel(
    groups, cell_volume, bounds_ref, sent_ref, pot_ref, out_ref, proj_ref,
    filt_ref, beyond, image_ref, flipped, nexts, stage, pots, perm, back, even, odd, diag, send_f, send_y,
    corr_sum, corr_recv, corr_gath, hamil_sum, hamil_recv, hamil_gath, full, work, other, turn, spread, turned,
    in_send, in_recv, pot_send, pot_recv, out_send, out_recv, corr_send, corr_arrive, hamil_send, hamil_arrive, back_send, back_recv,
):
    doms, slab, mine, width = stage.shape
    devices = doms * groups
    dom = lax.axis_index("dom")
    band = lax.axis_index("band")
    planes = doms * slab
    part = min(mine, 8)
    chunks = mine // part
    rows = planes * part
    lanes = width // groups
    levels = width // LANES
    high = LANES // GRID_Z
    spans = levels // high
    half_width = (bounds_ref[1] - bounds_ref[0]) / 2.0
    centre = (bounds_ref[1] + bounds_ref[0]) / 2.0
    inv_half = 1.0 / half_width

    everyone = peers(doms, groups)
    barrier = greet(everyone[1:])
    lane_orders(perm, back)
    pl.semaphore_wait(barrier, len(everyone) - 1)

    def incoming(c, r):
        peer = lax.rem(dom + r, doms)
        some = pl.ds(c * part, part)
        source, target = sent_ref.at[peer, :, some, :], stage.at[dom, :, some, :]
        if r == 0:
            return pltpu.make_async_copy(source, target, in_recv.at[c, r])
        return remote(source, target, in_send.at[c, r], in_recv.at[c, r], {"dom": peer})

    def potential(r):
        if r == 0:
            return pltpu.make_async_copy(pot_ref, pots.at[dom], pot_recv.at[r])
        return remote(pot_ref, pots.at[dom], pot_send.at[r], pot_recv.at[r], {"dom": lax.rem(dom + r, doms)})

    for r in range(doms):
        potential(r).start()
    for c in range(chunks):
        for r in range(doms):
            incoming(c, r).start()

    lane = lax.broadcasted_iota(jnp.int32, (rows, LANES), 1)
    row_of_lane = lax.broadcasted_iota(jnp.int32, (doms, part, LANES), 2) // GRID_Z
    first_high = lax.rem(lane, high) == 0
    last_high = lax.rem(lane, high) == high - 1

    for r in range(doms):
        potential(r).wait()
    for k in range(spans):
        pot = jnp.concatenate(
            [pots[:, :, pl.ds((h * spans + k) * LANES, LANES)].reshape(planes, LANES) for h in range(high)], axis=1
        )
        ordered = jnp.zeros(pot.shape, jnp.float32)
        for piece in range(3):
            top = pot.astype(jnp.bfloat16)
            ordered = ordered + dot(top, perm[...])
            pot = pot - top.astype(jnp.float32)
        scaled = (3.0 + ordered - centre) * (2.0 * inv_half)
        for b in range(high):
            line = scaled[:, b * LANES : (b + 1) * LANES]
            diag[k * high + b] = jnp.broadcast_to(line[:, None, :], (planes, part, LANES)).reshape(rows, LANES)

    def edges(field):
        top = field[levels]
        field[0] = jnp.where(first_high, pltpu.roll(top, LANES - (high - 1), 1), pltpu.roll(top, 1, 1))
        low = field[1]
        field[levels + 1] = jnp.where(last_high, pltpu.roll(low, high - 1, 1), pltpu.roll(low, LANES - 1, 1))

    def image(field, i):
        v = field[i]
        around = pltpu.roll(v, high, 1) + pltpu.roll(v, LANES - high, 1)
        around = around + (field[i - 1] + field[i + 1])
        around = around + (
            jnp.concatenate([v[part:], v[:part]], axis=0) + jnp.concatenate([v[rows - part :], v[: rows - part]], axis=0)
        )
        return diag[i - 1] * v - inv_half * around, v

    def sweep(source, target, first):
        def run(j, carry):
            for i in range(UNROLL):
                i = 1 + j * UNROLL + i
                fresh = image(source, i)[0]
                target[i] = 0.5 * fresh if first else fresh - target[i]
            return carry

        lax.fori_loop(0, levels // UNROLL, run, 0)
        edges(target)

    first_row = pl.multiple_of((band * doms + dom) * mine, part)

    def outgoing(pieces):
        copies = []
        for r, device in enumerate(everyone):
            for which, piece, place in pieces(device):
                recv = out_recv.at[which, r]
                if r == 0:
                    copies.append(pltpu.make_async_copy(piece, place, recv))
                else:
                    copies.append(remote(piece, place, out_send.at[which, r], recv, device))
        return copies

    def block(device):
        return pl.ds(pl.multiple_of(device["band"] * lanes, LANES), lanes)

    def main(c, device):
        source = send_f.at[pl.ds(device["dom"] * slab, slab), pl.ds(c * part, part), block(device)]
        return [(c, source, filt_ref.at[pl.ds(0, slab), pl.ds(first_row + c * part, part), :])]

    def halo(device):
        above = pl.ds(pl.multiple_of(lax.rem(device["band"] + 1, groups) * LANES, LANES), LANES)
        rows_here = pl.ds(first_row, mine)
        return [
            (chunks, send_f.at[device["dom"] * slab + slab, :, block(device)], filt_ref.at[slab, rows_here, :]),
            (chunks + 1, send_y.at[device["dom"], :, above], beyond.at[rows_here, :]),
        ]

    for c in range(chunks):
        for r in range(doms):
            incoming(c, r).wait()
        some = pl.ds(c * part, part)
        for k in range(spans):
            cells = jnp.concatenate(
                [
                    stage[:, :, some, pl.ds((h * spans + k) * LANES, LANES)].astype(jnp.float32).reshape(rows, LANES)
                    for h in range(high)
                ],
                axis=1,
            )
            ordered = dot(cells.astype(jnp.bfloat16), perm[...])
            for b in range(high):
                even[1 + k * high + b] = ordered[:, b * LANES : (b + 1) * LANES]
        edges(even)
        sweep(even, odd, True)

        def pair(k, carry):
            sweep(odd, even, False)
            sweep(even, odd, False)
            return carry

        lax.fori_loop(0, (DEG - 1) // 2, pair, 0)
        last = odd
        if DEG % 2 == 0:
            sweep(odd, even, False)
            last = even

        for k in range(spans):
            values = [last[1 + k * high + b] for b in range(high)]
            natural = dot(jnp.concatenate(values, axis=1).astype(jnp.bfloat16), back[...])
            for h in range(high):
                column = (h * spans + k) * LANES
                value = natural[:, h * LANES : (h + 1) * LANES].reshape(planes, part, LANES)
                send_f[pl.ds(0, planes), some, pl.ds(column, LANES)] = value.astype(jnp.bfloat16)
                send_f[planes, some, pl.ds(column, LANES)] = value[0].astype(jnp.bfloat16)
                if column % lanes == 0:
                    value = value.reshape(doms, slab * part, LANES)
                    edge = value[:, :part]
                    for x in range(1, slab):
                        moved = value[:, x * part : (x + 1) * part].reshape(doms * part, LANES)
                        moved = pltpu.roll(moved, x * GRID_Z, 1).reshape(doms, part, LANES)
                        edge = jnp.where(row_of_lane == x, moved, edge)
                    send_y[:, some, pl.ds(column // lanes * LANES, LANES)] = edge.astype(jnp.bfloat16)
        for copy in outgoing(functools.partial(main, c)):
            copy.start()
    for copy in outgoing(halo):
        copy.start()
    next_cells(nexts)
    for c in range(chunks):
        for copy in outgoing(functools.partial(main, c)):
            copy.wait()

    total = filt_ref.shape[1]
    for x in range(slab):
        flipped[x] = filt_ref[x].T
    gram(cell_volume, filt_ref, flipped, corr_sum, False)
    corr = BlockSum(corr_sum, corr_recv, corr_gath, corr_send, corr_arrive, sum_levels(doms, groups))
    steps = list(corr.steps())
    steps[0]()
    for copy in outgoing(halo):
        copy.wait()
    edge = lax.broadcasted_iota(jnp.int32, (total, LANES), 1) >= LANES - GRID_Z
    for x in range(slab):
        pot = 3.0 + pots[dom, pl.ds(x, 1), pl.ds(pl.multiple_of(band * lanes, LANES), lanes)]
        value = filt_ref[x].astype(jnp.float32) * pot - filt_ref[x + 1].astype(jnp.float32)
        value = value - dot(filt_ref[x], nexts[...])
        after = pltpu.roll(beyond[...].astype(jnp.float32), (LANES - GRID_Z - x * GRID_Z) % LANES, 1)
        image_ref[x, :, pl.ds(0, lanes - LANES)] = value[:, : lanes - LANES].astype(jnp.bfloat16)
        image_ref[x, :, pl.ds(lanes - LANES, LANES)] = (
            value[:, lanes - LANES :] - jnp.where(edge, after, 0.0)
        ).astype(jnp.bfloat16)
    for step in steps[1:3]:
        step()
    gram(cell_volume, image_ref, flipped, hamil_sum, True)
    hamil = BlockSum(hamil_sum, hamil_recv, hamil_gath, hamil_send, hamil_arrive, sum_levels(doms, groups))
    pending = list(hamil.steps())
    pending.pop(0)()
    steps = steps[3:]
    while steps:
        for _ in range(2):
            if steps:
                steps.pop(0)()
        for _ in range(2):
            if steps:
                pending.pop(0)()
    unpack(corr_gath, full)

    def pause():
        for _ in range(2):
            if len(pending) > 1:
                pending.pop(0)()

    calls = [0]

    def sometimes():
        calls[0] += 1
        if calls[0] % PAUSE == 0:
            pause()

    value = inverse_root(full, work, other, sometimes)
    turn[0], turn[1] = split(value)

    bands = out_ref.shape[0]
    half = total // 2
    side = groups // 2
    place = out_ref.at[:, :, pl.ds(pl.multiple_of(band * lanes, LANES), lanes)]
    returned = []
    for n in range(2):
        which = lax.rem(band // side + 1 + n, 2)
        rows_here = pl.ds(pl.multiple_of(which * half, half), half)
        for x in range(slab):
            points = filt_ref[x]
            product = dot(turn[0, rows_here, :], points) + dot(turn[1, rows_here, :], points)
            for t in range(lanes // LANES):
                spread[t, pl.ds(x, half, stride=slab), :] = product[:, t * LANES : (t + 1) * LANES]
        for t in range(lanes // LANES):
            turned[rows_here, :, pl.ds(t * LANES, LANES)] = spread[t].reshape(half, slab, LANES).astype(jnp.bfloat16)
        for q in range(side):
            to = which * side + lax.rem(band + q, side)
            source = turned.at[pl.ds(to * bands, bands)]
            recv = back_recv.at[n * side + q]
            if n == 1 and q == 0:
                copy = pltpu.make_async_copy(source, place, recv)
            else:
                copy = remote(source, place, back_send.at[n * side + q], recv, {"band": to})
            copy.start()
            returned.append(copy)

    while pending:
        pending.pop(0)()
    unpack(hamil_gath, full)
    halfway = split(dot3((turn[0], turn[1]), split(full[...])))
    proj_ref[...] = dot3(halfway, (turn[0], turn[1]))
    for copy in returned:
        copy.wait()


def step_call(sent, potential, bounds, groups, cell_volume):
    doms, slab, mine, width = sent.shape
    devices = doms * groups
    total = devices * mine
    planes = doms * slab
    part = min(mine, 8)
    chunks = mine // part
    levels = width // LANES
    lanes = width // groups
    size = LANES * (LANES // GRID_Z)
    packed = LANES * len(upper_blocks(total))
    vmem = pl.BlockSpec(memory_space=pltpu.VMEM)
    hbm = pl.BlockSpec(memory_space=pl.ANY)
    order = pltpu.VMEM((size, size), jnp.bfloat16)
    field = pltpu.VMEM((levels + 2, planes * part, LANES), jnp.float32)
    triangle = pltpu.VMEM((packed, LANES), jnp.float32)
    square = pltpu.VMEM((total, total), jnp.float32)
    dma = pltpu.SemaphoreType.DMA
    most = max(2, doms, groups // 2)
    return pl.pallas_call(
        functools.partial(step_kernel, groups, cell_volume),
        out_shape=(
            jax.ShapeDtypeStruct((mine * doms, slab, width), jnp.bfloat16),
            jax.ShapeDtypeStruct((total, total), jnp.float32),
        ),
        in_specs=[pl.BlockSpec(memory_space=pltpu.SMEM), hbm, hbm],
        out_specs=(hbm, vmem),
        scratch_shapes=[
            pltpu.VMEM((slab + 1, total, lanes), jnp.bfloat16),
            pltpu.VMEM((total, LANES), jnp.bfloat16),
            pltpu.VMEM((slab, total, lanes), jnp.bfloat16),
            pltpu.VMEM((slab, lanes, total), jnp.bfloat16),
            pltpu.VMEM((lanes, lanes), jnp.bfloat16),
            pltpu.VMEM(sent.shape, jnp.bfloat16),
            pltpu.VMEM((doms, slab, width), jnp.float32),
            order,
            order,
            field,
            field,
            pltpu.VMEM((levels, planes * part, LANES), jnp.float32),
            pltpu.VMEM((planes + 1, mine, width), jnp.bfloat16),
            pltpu.VMEM((doms, mine, groups * LANES), jnp.bfloat16),
        ]
        + [triangle] * 6
        + [square] * 3
        + [
            pltpu.VMEM((2, total, total), jnp.bfloat16),
            pltpu.VMEM((lanes // LANES, total // 2 * slab, LANES), jnp.float32),
            pltpu.VMEM((total, slab, lanes), jnp.bfloat16),
            dma((chunks, doms)),
            dma((chunks, doms)),
            dma((doms,)),
            dma((doms,)),
            dma((chunks + 2, devices)),
            dma((chunks + 2, devices)),
        ]
        + [dma((2, 3, most))] * 4
        + [dma((groups,))] * 2,
        cost_estimate=pl.CostEstimate(flops=60 * total**3, bytes_accessed=8 << 20, transcendentals=0),
        compiler_params=pltpu.CompilerParams(vmem_limit_bytes=48 << 20, collective_id=2, has_side_effects=True),
    )(bounds, sent, potential)


def body_plain(orbitals, potential, bounds):
    bands, slab, width = orbitals.shape
    doms = lax.axis_size("dom")
    groups = lax.axis_size("band")
    devices = doms * groups
    total_bands = bands * groups
    mine = bands // doms
    everyone = ("dom", "band")
    half_width = (bounds[1] - bounds[0]) / 2.0
    centre = (bounds[1] + bounds[0]) / 2.0
    cell_volume = 1.0 / (slab * doms * width)

    sent = orbitals.reshape(doms, mine, slab, width).transpose(0, 2, 1, 3)
    cells = lax.all_to_all(sent, "dom", split_axis=0, concat_axis=0, tiled=True)
    cells = cells.reshape(doms * slab, mine, width)
    pot = lax.all_to_all(
        jnp.broadcast_to(potential, (doms, slab, width)), "dom", split_axis=0, concat_axis=0, tiled=True
    ).reshape(doms * slab, 1, width)
    filt, applied = filter_bands(cells, pot, jnp.stack([1.0 / half_width, centre]), devices)
    filt = lax.all_to_all(filt, everyone, split_axis=0, concat_axis=0, tiled=True)
    applied = lax.all_to_all(applied, everyone, split_axis=0, concat_axis=0, tiled=True)
    filt = filt.reshape(total_bands, -1)
    applied = applied.reshape(total_bands, -1)
    bits = exchange_bits(doms, groups)
    square = jax.ShapeDtypeStruct((total_bands, total_bands), jnp.float32)
    rotated, trans = sum_call(
        functools.partial(orthonormal_kernel, bits, cell_volume, (doms, groups, mine)),
        (filt,),
        (jax.ShapeDtypeStruct(filt.shape, jnp.bfloat16), square),
        3,
        bits,
        0,
        40 * total_bands**3,
    )
    out = lax.all_to_all(rotated, "band", split_axis=0, concat_axis=1, tiled=True)
    projected = sum_call(
        functools.partial(project_kernel, bits, cell_volume),
        (filt, applied, trans),
        square,
        0,
        bits,
        1,
        40 * total_bands**3,
    )
    return out.reshape(bands, slab, width), projected


def body(orbitals, potential, bounds):
    bands, slab, width = orbitals.shape
    doms = lax.axis_size("dom")
    groups = lax.axis_size("band")
    mine = bands // doms
    total = bands * groups
    blocks = len(upper_blocks(total))
    if mine % 8 or slab * GRID_Z != LANES or width % (groups * LANES) or total % (2 * LANES) or blocks * LANES % (8 * doms * groups):
        return body_plain(orbitals, potential, bounds)
    cell_volume = 1.0 / (slab * doms * width)
    sent = orbitals.reshape(doms, mine, slab, width).transpose(0, 2, 1, 3)
    return step_call(sent, potential, bounds, groups, cell_volume)


def solution(mesh):
    return jax.shard_map(
        body,
        mesh=mesh,
        in_specs=(P("band", "dom", None), P("dom", None), P()),
        out_specs=(P("band", "dom", None), P()),
        check_vma=False,
    )
```

```python
import functools

import jax
import jax.numpy as jnp
from jax import lax
from jax.experimental import pallas as pl
from jax.experimental.pallas import tpu as pltpu
from jax.sharding import PartitionSpec as P

GRID_Z = 32
DEG = 8
NS_STEPS = 8
LANES = 128
UNROLL = 8
SHARE = 2
PAUSE = 3
TILE_ROWS = 8


def filter_kernel(scal_ref, cells_ref, pot_ref, sums_ref, filt_ref, applied_ref, field, high, low, coef):
    planes, bands, width = cells_ref.shape
    rows = planes * bands
    blocks_per_plane = filt_ref.shape[0] // planes
    block = filt_ref.shape[2]
    tile = sums_ref.shape[1]
    inv_half = scal_ref[0]
    centre = scal_ref[1]

    for x in range(planes):
        mine = pl.ds(x * bands, bands)
        coef[mine, :] = jnp.broadcast_to(3.0 + pot_ref[x], (bands, width))
        start = cells_ref[x].astype(jnp.float32)
        field[0, mine, :] = start
    for c in range(width // tile):
        cols = pl.ds(c * tile, tile)
        start = field[0, :, cols]
        high[0, :, cols] = start.astype(jnp.bfloat16)
        low[0, :, cols] = jnp.zeros((rows, tile), jnp.bfloat16)

    def shifted(v, by):
        if bands % 8 == 0:
            return jnp.concatenate([v[by:], v[:by]], axis=0)
        return pltpu.roll(v, (rows - by) % rows, 0)

    def neighbours(slot, c, v):
        cols = pl.ds(pl.multiple_of(c * tile, tile), tile)
        left = pl.ds(pl.multiple_of(lax.rem(c * tile + width - LANES, width), LANES), LANES)
        right = pl.ds(pl.multiple_of(lax.rem(c * tile + tile, width), LANES), LANES)

        def part(ref):
            wide = jnp.concatenate([ref[slot, :, left], ref[slot, :, cols], ref[slot, :, right]], axis=1)
            return dot(wide, sums_ref[...])

        return part(high) + part(low) + (shifted(v, bands) + shifted(v, rows - bands))

    def sweep(slot, other, weight, diagonal, first):
        def run(c, carry):
            cols = pl.ds(pl.multiple_of(c * tile, tile), tile)
            v = field[slot, :, cols]
            fresh = weight * neighbours(slot, c, v) + (coef[:, cols] * diagonal[0] + diagonal[1]) * v
            if not first:
                fresh = fresh - field[other, :, cols]
            field[other, :, cols] = fresh
            top, rest = split(fresh)
            high[other, :, cols] = top
            low[other, :, cols] = rest
            return carry

        lax.fori_loop(0, width // tile, run, 0)

    sweep(0, 1, -0.5 * inv_half, (inv_half, -centre * inv_half), True)

    def middle(k, carry):
        slot = lax.rem(k, 2)
        sweep(slot, 1 - slot, -inv_half, (2.0 * inv_half, -2.0 * centre * inv_half), False)
        return carry

    lax.fori_loop(1, DEG, middle, 0)
    slot = DEG % 2
    for c in range(width // tile):
        cols = pl.ds(c * tile, tile)
        v = field[slot, :, cols]
        applied = coef[:, cols] * v - 0.5 * neighbours(slot, c, v)
        piece, inner = divmod(c * tile, block)
        for x in range(planes):
            where = (x * blocks_per_plane + piece, slice(None), pl.ds(inner, tile))
            filt_ref[where] = v[x * bands : (x + 1) * bands].astype(jnp.bfloat16)
            applied_ref[where] = applied[x * bands : (x + 1) * bands].astype(jnp.bfloat16)


def neighbour_sums(tile):
    source = lax.broadcasted_iota(jnp.int32, (tile + 2 * LANES, tile), 0) - LANES
    target = lax.broadcasted_iota(jnp.int32, (tile + 2 * LANES, tile), 1)
    step = source - target
    same_row = (source >= 0) & (source // GRID_Z == target // GRID_Z)
    apart = lax.rem(step + GRID_Z, GRID_Z)
    beside_z = same_row & ((apart == 1) | (apart == GRID_Z - 1))
    beside_y = (step == GRID_Z) | (step == -GRID_Z)
    return (beside_z | beside_y).astype(jnp.bfloat16)


def filter_bands(cells, potential, scalars, devices):
    planes, bands, width = cells.shape
    rows = planes * bands
    block = planes * width // devices
    out = jax.ShapeDtypeStruct((devices, bands, block), jnp.bfloat16)
    vmem = pl.BlockSpec(memory_space=pltpu.VMEM)
    return pl.pallas_call(
        filter_kernel,
        out_shape=(out, out),
        in_specs=[pl.BlockSpec(memory_space=pltpu.SMEM), vmem, vmem, vmem],
        out_specs=(vmem, vmem),
        scratch_shapes=[
            pltpu.VMEM((2, rows, width), jnp.float32),
            pltpu.VMEM((2, rows, width), jnp.bfloat16),
            pltpu.VMEM((2, rows, width), jnp.bfloat16),
            pltpu.VMEM((rows, width), jnp.float32),
        ],
        compiler_params=pltpu.CompilerParams(vmem_limit_bytes=48 << 20),
    )(scalars, cells, potential, neighbour_sums(min(256, block)))


def split(value):
    spread = value * 65537.0
    high = spread - (spread - value)
    return high.astype(jnp.bfloat16), (value - high).astype(jnp.bfloat16)


def dot(a, b):
    return jnp.dot(a, b, preferred_element_type=jnp.float32)


def dot3(a, b):
    (a_high, a_low), (b_high, b_low) = a, b
    return dot(a_high, b_high) + (dot(a_high, b_low) + dot(a_low, b_high))


def exchange_bits(doms, groups):
    dom = [("dom", 1 << i) for i in range(1, (doms - 1).bit_length())]
    band = [("band", 1 << i) for i in range((groups - 1).bit_length())]
    core = [("dom", 1)]
    return core + band[:1] + dom + band[1:], core + dom + band


def gram_sum(bits, cell_volume, filt_ref, other_ref, total, send, recv, gath, send_sem, recv_sem):
    size = filt_ref.shape[0] // 2
    index = {axis: lax.axis_index(axis) for axis in ("dom", "band")}

    def partner(axis, bit):
        mine = lax.rem(index[axis] // bit, 2)
        return mine, {axis: index[axis] + bit - 2 * bit * mine}

    barrier = pltpu.get_barrier_semaphore()
    for axis, bit in bits[0]:
        pl.semaphore_signal(
            barrier, inc=1, device_id=partner(axis, bit)[1], device_id_type=pl.DeviceIdType.MESH
        )

    pairs = (((1,), (1,)), ((), ()))
    for stream in range(2):
        total[stream] = cell_volume * lax.dot_general(
            filt_ref[pl.ds(stream * size, size), :],
            other_ref[...],
            pairs,
            preferred_element_type=jnp.float32,
        )
    pl.semaphore_wait(barrier, len(bits[0]))

    def copy(stream, number, source, target, device):
        made = pltpu.make_async_remote_copy(
            src_ref=source,
            dst_ref=target,
            send_sem=send_sem.at[stream, number],
            recv_sem=recv_sem.at[stream, number],
            device_id=device,
            device_id_type=pl.DeviceIdType.MESH,
        )
        made.start()
        return made

    stages = len(bits[0])
    start = [jnp.int32(0)] * 2
    halved = [[], []]
    length, offset = size, 0
    for stage in range(stages):
        halve = length >= 2 * TILE_ROWS
        count = length // 2 if halve else length
        space = pl.ds(offset, count)
        flight = []
        for stream in range(2):
            axis, bit = bits[stream][stage]
            mine, device = partner(axis, bit)
            give = start[stream] + (1 - mine) * count if halve else start[stream]
            keep = start[stream] + mine * count if halve else start[stream]
            give = pl.multiple_of(give, TILE_ROWS)
            send[stream, space, :] = total[stream, pl.ds(give, count), :]
            flight.append(
                copy(stream, stage, send.at[stream, space], recv.at[stream, space], device)
            )
            start[stream] = pl.multiple_of(keep, TILE_ROWS)
            if halve:
                halved[stream].append((stage, mine, device))
        for stream in range(2):
            flight[stream].wait()
            kept = pl.ds(start[stream], count)
            if halve:
                own = total[stream, kept, :]
            else:
                own = send[stream, space, :]
            total[stream, kept, :] = own + recv[stream, space, :]
        length = count
        offset += count

    for stream in range(2):
        kept = pl.ds(start[stream], length)
        gath[stream, kept, :] = total[stream, kept, :]
    for back in range(len(halved[0]) - 1, -1, -1):
        flight = []
        for stream in range(2):
            stage, mine, device = halved[stream][back]
            area = gath.at[stream, pl.ds(start[stream], length)]
            flight.append(copy(stream, stages + stage, area, area, device))
            start[stream] = pl.multiple_of(start[stream] - mine * length, TILE_ROWS)
        for made in flight:
            made.wait()
        length *= 2


def orthonormal_kernel(
    bits, cell_volume, groups, filt_ref, out_ref, trans_ref,
    total, send, recv, gath, y_ref, z_ref, t_ref, send_sem, recv_sem,
):
    gram_sum(bits, cell_volume, filt_ref, filt_ref, total, send, recv, gath, send_sem, recv_sem)
    size = filt_ref.shape[0]
    outer, inner, width = groups
    row = lax.broadcasted_iota(jnp.int32, (size, size), 0)
    col = lax.broadcasted_iota(jnp.int32, (size, size), 1)
    diag = jnp.where(row == col, 1.5, 0.0)
    corr = gath[...].reshape(size, size)
    scale = jnp.sqrt(jnp.sum(corr * corr) + 1e-06)
    scaled = corr / scale
    factor = diag - 0.5 * scaled
    z_ref[...] = factor
    y_ref[...] = dot3(split(factor), split(scaled))

    def step(k, carry):
        y = split(y_ref[...])
        z = split(z_ref[...])
        factor = split(diag - 0.5 * dot3(z, y))
        y_ref[...] = dot3(factor, y)
        z_ref[...] = dot3(factor, z)
        return carry

    lax.fori_loop(1, NS_STEPS - 1, step, 0)
    y = split(y_ref[...])
    z = split(z_ref[...])
    factor = split(diag - 0.5 * dot3(z, y))
    t_ref[...] = dot3(factor, z) / jnp.sqrt(scale)
    for i in range(outer):
        for j in range(inner):
            trans_ref[pl.ds((j * outer + i) * width, width), :] = t_ref[
                pl.ds((i * inner + j) * width, width), :
            ]
    trans = split(trans_ref[...])
    filt = filt_ref[...]
    out_ref[...] = (dot(trans[0], filt) + dot(trans[1], filt)).astype(jnp.bfloat16)


def project_kernel(
    bits, cell_volume, filt_ref, applied_ref, trans_ref, proj_ref,
    total, send, recv, gath, send_sem, recv_sem,
):
    gram_sum(bits, cell_volume, filt_ref, applied_ref, total, send, recv, gath, send_sem, recv_sem)
    size = filt_ref.shape[0]
    trans = split(trans_ref[...])
    half = split(dot3(trans, split(gath[...].reshape(size, size))))
    contract = (((1,), (1,)), ((), ()))

    def dot_t(a, b):
        return lax.dot_general(a, b, contract, preferred_element_type=jnp.float32)

    proj_ref[...] = dot_t(half[0], trans[0]) + (
        dot_t(half[0], trans[1]) + dot_t(half[1], trans[0])
    )


def sum_call(kernel, operands, out_shape, squares, bits, number, flops):
    size = operands[0].shape[0]
    vmem = pl.BlockSpec(memory_space=pltpu.VMEM)
    room = size // 2 + TILE_ROWS * len(bits[0])
    sems = pltpu.SemaphoreType.DMA((2, 2 * len(bits[0])))
    halves = pltpu.VMEM((2, size // 2, size), jnp.float32)
    stage = pltpu.VMEM((2, room, size), jnp.float32)
    return pl.pallas_call(
        kernel,
        out_shape=out_shape,
        in_specs=[vmem] * len(operands),
        out_specs=jax.tree.map(lambda _: vmem, out_shape),
        scratch_shapes=[halves, stage, stage, halves]
        + [pltpu.VMEM((size, size), jnp.float32)] * squares
        + [sems, sems],
        cost_estimate=pl.CostEstimate(flops=flops, bytes_accessed=8 << 20, transcendentals=0),
        compiler_params=pltpu.CompilerParams(
            vmem_limit_bytes=32 << 20, collective_id=number, has_side_effects=True
        ),
    )(*operands)


def peers(doms, groups):
    dom = lax.axis_index("dom")
    band = lax.axis_index("band")
    rows = [lax.rem(dom + r, doms) for r in range(doms)]
    columns = [lax.rem(band + r, groups) for r in range(groups)]
    return [{"dom": d, "band": b} for b in columns for d in rows]


def remote(source, target, send_sem, recv_sem, device):
    return pltpu.make_async_remote_copy(
        src_ref=source,
        dst_ref=target,
        send_sem=send_sem,
        recv_sem=recv_sem,
        device_id=device,
        device_id_type=pl.DeviceIdType.MESH,
    )


def greet(others):
    barrier = pltpu.get_barrier_semaphore()
    for other in others:
        pl.semaphore_signal(barrier, inc=1, device_id=other, device_id_type=pl.DeviceIdType.MESH)
    return barrier


def lane_orders(perm, back):
    size = perm.shape[0]
    high = size // LANES
    row = lax.broadcasted_iota(jnp.int32, (size, size), 0)
    col = lax.broadcasted_iota(jnp.int32, (size, size), 1)
    grouped = lax.rem(row // GRID_Z, high) * LANES + lax.rem(row, GRID_Z) * high + row // LANES
    perm[...] = jnp.where(grouped == col, 1.0, 0.0).astype(jnp.bfloat16)
    natural = lax.rem(row, high) * LANES + row // LANES * GRID_Z + lax.rem(row // high, GRID_Z)
    back[...] = jnp.where(natural == col, 1.0, 0.0).astype(jnp.bfloat16)


class BlockSum:
    def __init__(self, total, recv, gath, send_sem, recv_sem, levels):
        self.total, self.recv, self.gath = total, recv, gath
        self.send_sem, self.recv_sem, self.levels = send_sem, recv_sem, levels
        self.start, self.length = jnp.int32(0), total.shape[0]
        self.offset, self.copies = 0, []

    def steps(self):
        for level in range(len(self.levels)):
            yield functools.partial(self.scatter, level)
            yield functools.partial(self.add, level)
        for level in range(len(self.levels) - 1, -1, -1):
            yield functools.partial(self.gather, level)
            yield functools.partial(self.join, level)

    def scatter(self, level):
        at, size, device = self.levels[level]
        rows = self.length // size
        self.copies = []
        for r in range(1, size):
            to = lax.rem(at + r, size)
            source = pl.ds(pl.multiple_of(self.start + to * rows, TILE_ROWS), rows)
            place = pl.ds(self.offset + (r - 1) * rows, rows)
            self.copies.append(
                remote(
                    self.total.at[source], self.recv.at[place],
                    self.send_sem.at[0, level, r], self.recv_sem.at[0, level, r], device(to),
                )
            )
        for made in self.copies:
            made.start()

    def add(self, level):
        at, size, _ = self.levels[level]
        rows = self.length // size
        self.start = pl.multiple_of(self.start + at * rows, TILE_ROWS)
        self.length = rows
        kept = pl.ds(self.start, rows)
        for made in self.copies:
            made.wait()
        value = self.total[kept]
        for r in range(1, size):
            value = value + self.recv[pl.ds(self.offset + (r - 1) * rows, rows)]
        self.offset += (size - 1) * rows
        self.total[kept] = value
        if level == len(self.levels) - 1:
            self.gath[kept] = value

    def gather(self, level):
        at, size, device = self.levels[level]
        area = self.gath.at[pl.ds(self.start, self.length)]
        self.copies = [
            remote(area, area, self.send_sem.at[1, level, r], self.recv_sem.at[1, level, r], device(lax.rem(at + r, size)))
            for r in range(1, size)
        ]
        for made in self.copies:
            made.start()

    def join(self, level):
        at, size, _ = self.levels[level]
        for made in self.copies:
            made.wait()
        self.start = pl.multiple_of(self.start - at * self.length, TILE_ROWS)
        self.length *= size


def sum_levels(doms, groups):
    dom = lax.axis_index("dom")
    band = lax.axis_index("band")
    core, chip = lax.rem(dom, 2), dom // 2
    low, high = lax.rem(band, 2), band // 2
    return [
        (core, 2, lambda to: {"dom": chip * 2 + to}),
        (chip * 2 + low, doms, lambda to: {"dom": to // 2 * 2 + core, "band": high * 2 + lax.rem(to, 2)}),
        (high, groups // 2, lambda to: {"band": to * 2 + low}),
    ]


def upper_blocks(total):
    count = total // LANES
    return [(i, j) for i in range(count) for j in range(i, count)]


def next_rings(ring, high):
    row = lax.rem(lax.broadcasted_iota(jnp.int32, ring.shape, 0), LANES)
    apart = lax.rem(row - lax.broadcasted_iota(jnp.int32, ring.shape, 1) + LANES, LANES)
    ring[...] = jnp.where((apart == high) | (apart == LANES - high), 1.0, 0.0).astype(jnp.bfloat16)


def next_cells(nexts):
    size = nexts.shape[0]
    row = lax.broadcasted_iota(jnp.int32, (size, size), 0)
    col = lax.broadcasted_iota(jnp.int32, (size, size), 1)
    ahead = col // GRID_Z * GRID_Z + lax.rem(col + 1, GRID_Z)
    nexts[...] = jnp.where((row == ahead) | (row == col + GRID_Z), 1.0, 0.0).astype(jnp.bfloat16)


def gram(factor, left, flipped, packed, halve):
    slab, lanes, total = flipped.shape
    size = 2 * LANES
    count = total // size
    product = {}
    for i in range(count):
        first = 0 if halve else i * size
        block = jnp.zeros((size, total - first), jnp.float32)
        for x in range(slab):
            block = block + dot(left[x, pl.ds(i * size, size), :], flipped[x, :, pl.ds(first, total - first)])
        for a in range(2):
            for j in range(first // LANES, total // LANES):
                column = j * LANES - first
                product[2 * i + a, j] = block[a * LANES : (a + 1) * LANES, column : column + LANES]
    for n, (i, j) in enumerate(upper_blocks(total)):
        value = product[i, j]
        if halve:
            value = 0.5 * (value + product[j, i].T)
        packed[pl.ds(n * LANES, LANES)] = value * factor


def unpack(packed, full):
    for n, (i, j) in enumerate(upper_blocks(full.shape[0])):
        block = packed[pl.ds(n * LANES, LANES)]
        full[pl.ds(i * LANES, LANES), pl.ds(j * LANES, LANES)] = block
        if i != j:
            full[pl.ds(j * LANES, LANES), pl.ds(i * LANES, LANES)] = block.T


def inverse_root(full, work, other, pause):
    size = full.shape[0]
    row = lax.broadcasted_iota(jnp.int32, (size, size), 0)
    col = lax.broadcasted_iota(jnp.int32, (size, size), 1)

    def diagonal(value):
        return jnp.where(row == col, value, 0.0)

    corr = full[...]
    scale = jnp.sqrt(jnp.sum(corr * corr) + 1e-06)
    work[...] = corr / scale
    for double in range(NS_STEPS // 2 - 1):
        held = split(work[...])
        square = dot(held[0], held[0])
        rest = dot(square.astype(jnp.bfloat16), (0.0625 * square - 0.5625 * work[...]).astype(jnp.bfloat16))
        factor = split(diagonal(2.25) - 2.4375 * work[...] + (1.6875 * square + rest))
        pause()
        if double == 0:
            full[...] = factor[0].astype(jnp.float32) + factor[1].astype(jnp.float32)
        else:
            full[...] = dot3(split(full[...]), factor)
            pause()
        other[...] = dot3(held, factor)
        pause()
        work[...] = dot3(factor, split(other[...]))
        pause()
    left = diagonal(1.0) - work[...]
    rounded = left.astype(jnp.bfloat16)
    square = dot(rounded, rounded)
    rest = 0.5 * left + 0.375 * square
    rest = rest + dot(square.astype(jnp.bfloat16), (0.3125 * left + 0.0625 * square).astype(jnp.bfloat16))
    pause()
    value = full[...]
    value = value + dot(value.astype(jnp.bfloat16), rest.astype(jnp.bfloat16))
    return value / jnp.sqrt(scale)


def step_kernel(
    groups, cell_volume, bounds_ref, sent_ref, pot_ref, out_ref, proj_ref,
    filt_ref, beyond, image_ref, flipped, nexts, stage, pots, perm, back, ring, even, odd, diag, send_f, send_y,
    corr_sum, corr_recv, corr_gath, hamil_sum, hamil_recv, hamil_gath, full, work, other, turn, spread, turned,
    in_send, in_recv, pot_send, pot_recv, out_send, out_recv, corr_send, corr_arrive, hamil_send, hamil_arrive, back_send, back_recv,
):
    doms, slab, mine, width = stage.shape
    devices = doms * groups
    dom = lax.axis_index("dom")
    band = lax.axis_index("band")
    planes = doms * slab
    part = min(mine, 8)
    chunks = mine // part
    rows = planes * part
    lanes = width // groups
    levels = width // LANES
    high = LANES // GRID_Z
    spans = levels // high
    half_width = (bounds_ref[1] - bounds_ref[0]) / 2.0
    centre = (bounds_ref[1] + bounds_ref[0]) / 2.0
    inv_half = 1.0 / half_width

    everyone = peers(doms, groups)
    barrier = greet(everyone[1:])
    lane_orders(perm, back)
    next_rings(ring, high)
    pl.semaphore_wait(barrier, len(everyone) - 1)

    def incoming(c, r):
        peer = lax.rem(dom + r, doms)
        some = pl.ds(c * part, part)
        source, target = sent_ref.at[peer, :, some, :], stage.at[dom, :, some, :]
        if r == 0:
            return pltpu.make_async_copy(source, target, in_recv.at[c, r])
        return remote(source, target, in_send.at[c, r], in_recv.at[c, r], {"dom": peer})

    def potential(r):
        if r == 0:
            return pltpu.make_async_copy(pot_ref, pots.at[dom], pot_recv.at[r])
        return remote(pot_ref, pots.at[dom], pot_send.at[r], pot_recv.at[r], {"dom": lax.rem(dom + r, doms)})

    for r in range(doms):
        potential(r).start()
    for c in range(chunks):
        for r in range(doms):
            incoming(c, r).start()

    lane = lax.broadcasted_iota(jnp.int32, (rows, LANES), 1)
    row_of_lane = lax.broadcasted_iota(jnp.int32, (doms, part, LANES), 2) // GRID_Z
    first_high = lax.rem(lane, high) == 0
    last_high = lax.rem(lane, high) == high - 1

    for r in range(doms):
        potential(r).wait()
    for k in range(spans):
        pot = jnp.concatenate(
            [pots[:, :, pl.ds((h * spans + k) * LANES, LANES)].reshape(planes, LANES) for h in range(high)], axis=1
        )
        ordered = jnp.zeros(pot.shape, jnp.float32)
        for piece in range(3):
            top = pot.astype(jnp.bfloat16)
            ordered = ordered + dot(top, perm[...])
            pot = pot - top.astype(jnp.float32)
        scaled = (3.0 + ordered - centre) * (2.0 * inv_half)
        for b in range(high):
            line = scaled[:, b * LANES : (b + 1) * LANES]
            diag[k * high + b] = jnp.broadcast_to(line[:, None, :], (planes, part, LANES)).reshape(rows, LANES)

    def edges(field):
        top = field[levels]
        field[0] = jnp.where(first_high, pltpu.roll(top, LANES - (high - 1), 1), pltpu.roll(top, 1, 1))
        low = field[1]
        field[levels + 1] = jnp.where(last_high, pltpu.roll(low, high - 1, 1), pltpu.roll(low, LANES - 1, 1))

    cut = rows // SHARE if SHARE else 0

    def sums_z(values):
        if not cut:
            return None
        top = split(jnp.concatenate([v[:cut] for v in values], axis=0))
        return dot(jnp.concatenate(top, axis=1), ring[...])

    def image(v, field, i, sums):
        rest = v[cut:]
        around = pltpu.roll(rest, high, 1) + pltpu.roll(rest, LANES - high, 1)
        if cut:
            around = jnp.concatenate([sums, around], axis=0)
        around = around + (field[i - 1] + field[i + 1])
        around = around + (
            jnp.concatenate([v[part:], v[:part]], axis=0) + jnp.concatenate([v[rows - part :], v[: rows - part]], axis=0)
        )
        return diag[i - 1] * v - inv_half * around

    def sweep(source, target, first):
        def run(j, carry):
            start = 1 + j * UNROLL
            values = [source[start + i] for i in range(UNROLL)]
            sums = sums_z(values)
            for i in range(UNROLL):
                fresh = image(values[i], source, start + i, sums[i * cut : (i + 1) * cut] if cut else None)
                target[start + i] = 0.5 * fresh if first else fresh - target[start + i]
            return carry

        lax.fori_loop(0, levels // UNROLL, run, 0)
        edges(target)

    first_row = pl.multiple_of((band * doms + dom) * mine, part)

    def outgoing(pieces):
        copies = []
        for r, device in enumerate(everyone):
            for which, piece, place in pieces(device):
                recv = out_recv.at[which, r]
                if r == 0:
                    copies.append(pltpu.make_async_copy(piece, place, recv))
                else:
                    copies.append(remote(piece, place, out_send.at[which, r], recv, device))
        return copies

    def block(device):
        return pl.ds(pl.multiple_of(device["band"] * lanes, LANES), lanes)

    def main(c, device):
        source = send_f.at[pl.ds(device["dom"] * slab, slab), pl.ds(c * part, part), block(device)]
        return [(c, source, filt_ref.at[pl.ds(0, slab), pl.ds(first_row + c * part, part), :])]

    def halo(device):
        above = pl.ds(pl.multiple_of(lax.rem(device["band"] + 1, groups) * LANES, LANES), LANES)
        rows_here = pl.ds(first_row, mine)
        return [
            (chunks, send_f.at[device["dom"] * slab + slab, :, block(device)], filt_ref.at[slab, rows_here, :]),
            (chunks + 1, send_y.at[device["dom"], :, above], beyond.at[rows_here, :]),
        ]

    for c in range(chunks):
        for r in range(doms):
            incoming(c, r).wait()
        some = pl.ds(c * part, part)
        for k in range(spans):
            cells = jnp.concatenate(
                [
                    stage[:, :, some, pl.ds((h * spans + k) * LANES, LANES)].astype(jnp.float32).reshape(rows, LANES)
                    for h in range(high)
                ],
                axis=1,
            )
            ordered = dot(cells.astype(jnp.bfloat16), perm[...])
            for b in range(high):
                even[1 + k * high + b] = ordered[:, b * LANES : (b + 1) * LANES]
        edges(even)
        sweep(even, odd, True)

        def pair(k, carry):
            sweep(odd, even, False)
            sweep(even, odd, False)
            return carry

        lax.fori_loop(0, (DEG - 1) // 2, pair, 0)
        last = odd
        if DEG % 2 == 0:
            sweep(odd, even, False)
            last = even

        for k in range(spans):
            values = [last[1 + k * high + b] for b in range(high)]
            natural = dot(jnp.concatenate(values, axis=1).astype(jnp.bfloat16), back[...])
            for h in range(high):
                column = (h * spans + k) * LANES
                value = natural[:, h * LANES : (h + 1) * LANES].reshape(planes, part, LANES)
                send_f[pl.ds(0, planes), some, pl.ds(column, LANES)] = value.astype(jnp.bfloat16)
                send_f[planes, some, pl.ds(column, LANES)] = value[0].astype(jnp.bfloat16)
                if column % lanes == 0:
                    value = value.reshape(doms, slab * part, LANES)
                    edge = value[:, :part]
                    for x in range(1, slab):
                        moved = value[:, x * part : (x + 1) * part].reshape(doms * part, LANES)
                        moved = pltpu.roll(moved, x * GRID_Z, 1).reshape(doms, part, LANES)
                        edge = jnp.where(row_of_lane == x, moved, edge)
                    send_y[:, some, pl.ds(column // lanes * LANES, LANES)] = edge.astype(jnp.bfloat16)
        for copy in outgoing(functools.partial(main, c)):
            copy.start()
    for copy in outgoing(halo):
        copy.start()
    next_cells(nexts)
    for c in range(chunks):
        for copy in outgoing(functools.partial(main, c)):
            copy.wait()

    total = filt_ref.shape[1]
    for x in range(slab):
        flipped[x] = filt_ref[x].T
    gram(cell_volume, filt_ref, flipped, corr_sum, False)
    corr = BlockSum(corr_sum, corr_recv, corr_gath, corr_send, corr_arrive, sum_levels(doms, groups))
    steps = list(corr.steps())
    steps[0]()
    for copy in outgoing(halo):
        copy.wait()
    edge = lax.broadcasted_iota(jnp.int32, (total, LANES), 1) >= LANES - GRID_Z
    for x in range(slab):
        pot = 3.0 + pots[dom, pl.ds(x, 1), pl.ds(pl.multiple_of(band * lanes, LANES), lanes)]
        value = filt_ref[x].astype(jnp.float32) * pot - filt_ref[x + 1].astype(jnp.float32)
        value = value - dot(filt_ref[x], nexts[...])
        after = pltpu.roll(beyond[...].astype(jnp.float32), (LANES - GRID_Z - x * GRID_Z) % LANES, 1)
        image_ref[x, :, pl.ds(0, lanes - LANES)] = value[:, : lanes - LANES].astype(jnp.bfloat16)
        image_ref[x, :, pl.ds(lanes - LANES, LANES)] = (
            value[:, lanes - LANES :] - jnp.where(edge, after, 0.0)
        ).astype(jnp.bfloat16)
    for step in steps[1:3]:
        step()
    gram(cell_volume, image_ref, flipped, hamil_sum, True)
    hamil = BlockSum(hamil_sum, hamil_recv, hamil_gath, hamil_send, hamil_arrive, sum_levels(doms, groups))
    pending = list(hamil.steps())
    pending.pop(0)()
    steps = steps[3:]
    while steps:
        for _ in range(2):
            if steps:
                steps.pop(0)()
        for _ in range(2):
            if steps:
                pending.pop(0)()
    unpack(corr_gath, full)

    def pause():
        for _ in range(2):
            if len(pending) > 1:
                pending.pop(0)()

    calls = [0]

    def sometimes():
        calls[0] += 1
        if calls[0] % PAUSE == 0:
            pause()

    value = inverse_root(full, work, other, sometimes)
    turn[0], turn[1] = split(value)

    bands = out_ref.shape[0]
    parts = groups // 2
    size = total // parts
    place = out_ref.at[:, :, pl.ds(pl.multiple_of(band * lanes, LANES), lanes)]
    returned = []
    for n, shift in enumerate(sorted(range(parts), key=lambda r: -min(r, parts - r))):
        which = lax.rem(band // 2 + shift, parts)
        rows_here = pl.ds(pl.multiple_of(which * size, size), size)
        for x in range(slab):
            points = filt_ref[x]
            product = dot(turn[0, rows_here, :], points) + dot(turn[1, rows_here, :], points)
            for t in range(lanes // LANES):
                spread[t, pl.ds(x, size, stride=slab), :] = product[:, t * LANES : (t + 1) * LANES]
        for t in range(lanes // LANES):
            turned[rows_here, :, pl.ds(t * LANES, LANES)] = spread[t].reshape(size, slab, LANES).astype(jnp.bfloat16)
        for q in (1, 0):
            to = which * 2 + lax.rem(band + q, 2)
            source = turned.at[pl.ds(to * bands, bands)]
            recv = back_recv.at[n * 2 + q]
            if shift == 0 and q == 0:
                copy = pltpu.make_async_copy(source, place, recv)
            else:
                copy = remote(source, place, back_send.at[n * 2 + q], recv, {"band": to})
            copy.start()
            returned.append(copy)

    while pending:
        pending.pop(0)()
    unpack(hamil_gath, full)
    halfway = split(dot3((turn[0], turn[1]), split(full[...])))
    proj_ref[...] = dot3(halfway, (turn[0], turn[1]))
    for copy in returned:
        copy.wait()


def step_call(sent, potential, bounds, groups, cell_volume):
    doms, slab, mine, width = sent.shape
    devices = doms * groups
    total = devices * mine
    planes = doms * slab
    part = min(mine, 8)
    chunks = mine // part
    levels = width // LANES
    lanes = width // groups
    size = LANES * (LANES // GRID_Z)
    packed = LANES * len(upper_blocks(total))
    vmem = pl.BlockSpec(memory_space=pltpu.VMEM)
    hbm = pl.BlockSpec(memory_space=pl.ANY)
    order = pltpu.VMEM((size, size), jnp.bfloat16)
    field = pltpu.VMEM((levels + 2, planes * part, LANES), jnp.float32)
    triangle = pltpu.VMEM((packed, LANES), jnp.float32)
    square = pltpu.VMEM((total, total), jnp.float32)
    dma = pltpu.SemaphoreType.DMA
    most = max(2, doms, groups // 2)
    return pl.pallas_call(
        functools.partial(step_kernel, groups, cell_volume),
        out_shape=(
            jax.ShapeDtypeStruct((mine * doms, slab, width), jnp.bfloat16),
            jax.ShapeDtypeStruct((total, total), jnp.float32),
        ),
        in_specs=[pl.BlockSpec(memory_space=pltpu.SMEM), hbm, hbm],
        out_specs=(hbm, vmem),
        scratch_shapes=[
            pltpu.VMEM((slab + 1, total, lanes), jnp.bfloat16),
            pltpu.VMEM((total, LANES), jnp.bfloat16),
            pltpu.VMEM((slab, total, lanes), jnp.bfloat16),
            pltpu.VMEM((slab, lanes, total), jnp.bfloat16),
            pltpu.VMEM((lanes, lanes), jnp.bfloat16),
            pltpu.VMEM(sent.shape, jnp.bfloat16),
            pltpu.VMEM((doms, slab, width), jnp.float32),
            order,
            order,
            pltpu.VMEM((2 * LANES, LANES), jnp.bfloat16),
            field,
            field,
            pltpu.VMEM((levels, planes * part, LANES), jnp.float32),
            pltpu.VMEM((planes + 1, mine, width), jnp.bfloat16),
            pltpu.VMEM((doms, mine, groups * LANES), jnp.bfloat16),
        ]
        + [triangle] * 6
        + [square] * 3
        + [
            pltpu.VMEM((2, total, total), jnp.bfloat16),
            pltpu.VMEM((lanes // LANES, total // (groups // 2) * slab, LANES), jnp.float32),
            pltpu.VMEM((total, slab, lanes), jnp.bfloat16),
            dma((chunks, doms)),
            dma((chunks, doms)),
            dma((doms,)),
            dma((doms,)),
            dma((chunks + 2, devices)),
            dma((chunks + 2, devices)),
        ]
        + [dma((2, 3, most))] * 4
        + [dma((groups,))] * 2,
        cost_estimate=pl.CostEstimate(flops=60 * total**3, bytes_accessed=8 << 20, transcendentals=0),
        compiler_params=pltpu.CompilerParams(vmem_limit_bytes=48 << 20, collective_id=2, has_side_effects=True),
    )(bounds, sent, potential)


def body_plain(orbitals, potential, bounds):
    bands, slab, width = orbitals.shape
    doms = lax.axis_size("dom")
    groups = lax.axis_size("band")
    devices = doms * groups
    total_bands = bands * groups
    mine = bands // doms
    everyone = ("dom", "band")
    half_width = (bounds[1] - bounds[0]) / 2.0
    centre = (bounds[1] + bounds[0]) / 2.0
    cell_volume = 1.0 / (slab * doms * width)

    sent = orbitals.reshape(doms, mine, slab, width).transpose(0, 2, 1, 3)
    cells = lax.all_to_all(sent, "dom", split_axis=0, concat_axis=0, tiled=True)
    cells = cells.reshape(doms * slab, mine, width)
    pot = lax.all_to_all(
        jnp.broadcast_to(potential, (doms, slab, width)), "dom", split_axis=0, concat_axis=0, tiled=True
    ).reshape(doms * slab, 1, width)
    filt, applied = filter_bands(cells, pot, jnp.stack([1.0 / half_width, centre]), devices)
    filt = lax.all_to_all(filt, everyone, split_axis=0, concat_axis=0, tiled=True)
    applied = lax.all_to_all(applied, everyone, split_axis=0, concat_axis=0, tiled=True)
    filt = filt.reshape(total_bands, -1)
    applied = applied.reshape(total_bands, -1)
    bits = exchange_bits(doms, groups)
    square = jax.ShapeDtypeStruct((total_bands, total_bands), jnp.float32)
    rotated, trans = sum_call(
        functools.partial(orthonormal_kernel, bits, cell_volume, (doms, groups, mine)),
        (filt,),
        (jax.ShapeDtypeStruct(filt.shape, jnp.bfloat16), square),
        3,
        bits,
        0,
        40 * total_bands**3,
    )
    out = lax.all_to_all(rotated, "band", split_axis=0, concat_axis=1, tiled=True)
    projected = sum_call(
        functools.partial(project_kernel, bits, cell_volume),
        (filt, applied, trans),
        square,
        0,
        bits,
        1,
        40 * total_bands**3,
    )
    return out.reshape(bands, slab, width), projected


def body(orbitals, potential, bounds):
    bands, slab, width = orbitals.shape
    doms = lax.axis_size("dom")
    groups = lax.axis_size("band")
    mine = bands // doms
    total = bands * groups
    blocks = len(upper_blocks(total))
    if mine % 8 or slab * GRID_Z != LANES or width % (groups * LANES) or total % (2 * LANES) or blocks * LANES % (8 * doms * groups):
        return body_plain(orbitals, potential, bounds)
    cell_volume = 1.0 / (slab * doms * width)
    sent = orbitals.reshape(doms, mine, slab, width).transpose(0, 2, 1, 3)
    return step_call(sent, potential, bounds, groups, cell_volume)


def solution(mesh):
    return jax.shard_map(
        body,
        mesh=mesh,
        in_specs=(P("band", "dom", None), P("dom", None), P()),
        out_specs=(P("band", "dom", None), P()),
        check_vma=False,
    )
```

```python
import functools

import jax
import jax.numpy as jnp
from jax import lax
from jax.experimental import pallas as pl
from jax.experimental.pallas import tpu as pltpu
from jax.sharding import PartitionSpec as P

GRID_Z = 32
DEG = 8
NS_STEPS = 8
LANES = 128
UNROLL = 8
SHARE = 2
PAUSE = 1
TILE_ROWS = 8


def filter_kernel(scal_ref, cells_ref, pot_ref, sums_ref, filt_ref, applied_ref, field, high, low, coef):
    planes, bands, width = cells_ref.shape
    rows = planes * bands
    blocks_per_plane = filt_ref.shape[0] // planes
    block = filt_ref.shape[2]
    tile = sums_ref.shape[1]
    inv_half = scal_ref[0]
    centre = scal_ref[1]

    for x in range(planes):
        mine = pl.ds(x * bands, bands)
        coef[mine, :] = jnp.broadcast_to(3.0 + pot_ref[x], (bands, width))
        start = cells_ref[x].astype(jnp.float32)
        field[0, mine, :] = start
    for c in range(width // tile):
        cols = pl.ds(c * tile, tile)
        start = field[0, :, cols]
        high[0, :, cols] = start.astype(jnp.bfloat16)
        low[0, :, cols] = jnp.zeros((rows, tile), jnp.bfloat16)

    def shifted(v, by):
        if bands % 8 == 0:
            return jnp.concatenate([v[by:], v[:by]], axis=0)
        return pltpu.roll(v, (rows - by) % rows, 0)

    def neighbours(slot, c, v):
        cols = pl.ds(pl.multiple_of(c * tile, tile), tile)
        left = pl.ds(pl.multiple_of(lax.rem(c * tile + width - LANES, width), LANES), LANES)
        right = pl.ds(pl.multiple_of(lax.rem(c * tile + tile, width), LANES), LANES)

        def part(ref):
            wide = jnp.concatenate([ref[slot, :, left], ref[slot, :, cols], ref[slot, :, right]], axis=1)
            return dot(wide, sums_ref[...])

        return part(high) + part(low) + (shifted(v, bands) + shifted(v, rows - bands))

    def sweep(slot, other, weight, diagonal, first):
        def run(c, carry):
            cols = pl.ds(pl.multiple_of(c * tile, tile), tile)
            v = field[slot, :, cols]
            fresh = weight * neighbours(slot, c, v) + (coef[:, cols] * diagonal[0] + diagonal[1]) * v
            if not first:
                fresh = fresh - field[other, :, cols]
            field[other, :, cols] = fresh
            top, rest = split(fresh)
            high[other, :, cols] = top
            low[other, :, cols] = rest
            return carry

        lax.fori_loop(0, width // tile, run, 0)

    sweep(0, 1, -0.5 * inv_half, (inv_half, -centre * inv_half), True)

    def middle(k, carry):
        slot = lax.rem(k, 2)
        sweep(slot, 1 - slot, -inv_half, (2.0 * inv_half, -2.0 * centre * inv_half), False)
        return carry

    lax.fori_loop(1, DEG, middle, 0)
    slot = DEG % 2
    for c in range(width // tile):
        cols = pl.ds(c * tile, tile)
        v = field[slot, :, cols]
        applied = coef[:, cols] * v - 0.5 * neighbours(slot, c, v)
        piece, inner = divmod(c * tile, block)
        for x in range(planes):
            where = (x * blocks_per_plane + piece, slice(None), pl.ds(inner, tile))
            filt_ref[where] = v[x * bands : (x + 1) * bands].astype(jnp.bfloat16)
            applied_ref[where] = applied[x * bands : (x + 1) * bands].astype(jnp.bfloat16)


def neighbour_sums(tile):
    source = lax.broadcasted_iota(jnp.int32, (tile + 2 * LANES, tile), 0) - LANES
    target = lax.broadcasted_iota(jnp.int32, (tile + 2 * LANES, tile), 1)
    step = source - target
    same_row = (source >= 0) & (source // GRID_Z == target // GRID_Z)
    apart = lax.rem(step + GRID_Z, GRID_Z)
    beside_z = same_row & ((apart == 1) | (apart == GRID_Z - 1))
    beside_y = (step == GRID_Z) | (step == -GRID_Z)
    return (beside_z | beside_y).astype(jnp.bfloat16)


def filter_bands(cells, potential, scalars, devices):
    planes, bands, width = cells.shape
    rows = planes * bands
    block = planes * width // devices
    out = jax.ShapeDtypeStruct((devices, bands, block), jnp.bfloat16)
    vmem = pl.BlockSpec(memory_space=pltpu.VMEM)
    return pl.pallas_call(
        filter_kernel,
        out_shape=(out, out),
        in_specs=[pl.BlockSpec(memory_space=pltpu.SMEM), vmem, vmem, vmem],
        out_specs=(vmem, vmem),
        scratch_shapes=[
            pltpu.VMEM((2, rows, width), jnp.float32),
            pltpu.VMEM((2, rows, width), jnp.bfloat16),
            pltpu.VMEM((2, rows, width), jnp.bfloat16),
            pltpu.VMEM((rows, width), jnp.float32),
        ],
        compiler_params=pltpu.CompilerParams(vmem_limit_bytes=48 << 20),
    )(scalars, cells, potential, neighbour_sums(min(256, block)))


def split(value):
    spread = value * 65537.0
    high = spread - (spread - value)
    return high.astype(jnp.bfloat16), (value - high).astype(jnp.bfloat16)


def dot(a, b):
    return jnp.dot(a, b, preferred_element_type=jnp.float32)


def dot3(a, b):
    (a_high, a_low), (b_high, b_low) = a, b
    return dot(a_high, b_high) + (dot(a_high, b_low) + dot(a_low, b_high))


def exchange_bits(doms, groups):
    dom = [("dom", 1 << i) for i in range(1, (doms - 1).bit_length())]
    band = [("band", 1 << i) for i in range((groups - 1).bit_length())]
    core = [("dom", 1)]
    return core + band[:1] + dom + band[1:], core + dom + band


def gram_sum(bits, cell_volume, filt_ref, other_ref, total, send, recv, gath, send_sem, recv_sem):
    size = filt_ref.shape[0] // 2
    index = {axis: lax.axis_index(axis) for axis in ("dom", "band")}

    def partner(axis, bit):
        mine = lax.rem(index[axis] // bit, 2)
        return mine, {axis: index[axis] + bit - 2 * bit * mine}

    barrier = pltpu.get_barrier_semaphore()
    for axis, bit in bits[0]:
        pl.semaphore_signal(
            barrier, inc=1, device_id=partner(axis, bit)[1], device_id_type=pl.DeviceIdType.MESH
        )

    pairs = (((1,), (1,)), ((), ()))
    for stream in range(2):
        total[stream] = cell_volume * lax.dot_general(
            filt_ref[pl.ds(stream * size, size), :],
            other_ref[...],
            pairs,
            preferred_element_type=jnp.float32,
        )
    pl.semaphore_wait(barrier, len(bits[0]))

    def copy(stream, number, source, target, device):
        made = pltpu.make_async_remote_copy(
            src_ref=source,
            dst_ref=target,
            send_sem=send_sem.at[stream, number],
            recv_sem=recv_sem.at[stream, number],
            device_id=device,
            device_id_type=pl.DeviceIdType.MESH,
        )
        made.start()
        return made

    stages = len(bits[0])
    start = [jnp.int32(0)] * 2
    halved = [[], []]
    length, offset = size, 0
    for stage in range(stages):
        halve = length >= 2 * TILE_ROWS
        count = length // 2 if halve else length
        space = pl.ds(offset, count)
        flight = []
        for stream in range(2):
            axis, bit = bits[stream][stage]
            mine, device = partner(axis, bit)
            give = start[stream] + (1 - mine) * count if halve else start[stream]
            keep = start[stream] + mine * count if halve else start[stream]
            give = pl.multiple_of(give, TILE_ROWS)
            send[stream, space, :] = total[stream, pl.ds(give, count), :]
            flight.append(
                copy(stream, stage, send.at[stream, space], recv.at[stream, space], device)
            )
            start[stream] = pl.multiple_of(keep, TILE_ROWS)
            if halve:
                halved[stream].append((stage, mine, device))
        for stream in range(2):
            flight[stream].wait()
            kept = pl.ds(start[stream], count)
            if halve:
                own = total[stream, kept, :]
            else:
                own = send[stream, space, :]
            total[stream, kept, :] = own + recv[stream, space, :]
        length = count
        offset += count

    for stream in range(2):
        kept = pl.ds(start[stream], length)
        gath[stream, kept, :] = total[stream, kept, :]
    for back in range(len(halved[0]) - 1, -1, -1):
        flight = []
        for stream in range(2):
            stage, mine, device = halved[stream][back]
            area = gath.at[stream, pl.ds(start[stream], length)]
            flight.append(copy(stream, stages + stage, area, area, device))
            start[stream] = pl.multiple_of(start[stream] - mine * length, TILE_ROWS)
        for made in flight:
            made.wait()
        length *= 2


def orthonormal_kernel(
    bits, cell_volume, groups, filt_ref, out_ref, trans_ref,
    total, send, recv, gath, y_ref, z_ref, t_ref, send_sem, recv_sem,
):
    gram_sum(bits, cell_volume, filt_ref, filt_ref, total, send, recv, gath, send_sem, recv_sem)
    size = filt_ref.shape[0]
    outer, inner, width = groups
    row = lax.broadcasted_iota(jnp.int32, (size, size), 0)
    col = lax.broadcasted_iota(jnp.int32, (size, size), 1)
    diag = jnp.where(row == col, 1.5, 0.0)
    corr = gath[...].reshape(size, size)
    scale = jnp.sqrt(jnp.sum(corr * corr) + 1e-06)
    scaled = corr / scale
    factor = diag - 0.5 * scaled
    z_ref[...] = factor
    y_ref[...] = dot3(split(factor), split(scaled))

    def step(k, carry):
        y = split(y_ref[...])
        z = split(z_ref[...])
        factor = split(diag - 0.5 * dot3(z, y))
        y_ref[...] = dot3(factor, y)
        z_ref[...] = dot3(factor, z)
        return carry

    lax.fori_loop(1, NS_STEPS - 1, step, 0)
    y = split(y_ref[...])
    z = split(z_ref[...])
    factor = split(diag - 0.5 * dot3(z, y))
    t_ref[...] = dot3(factor, z) / jnp.sqrt(scale)
    for i in range(outer):
        for j in range(inner):
            trans_ref[pl.ds((j * outer + i) * width, width), :] = t_ref[
                pl.ds((i * inner + j) * width, width), :
            ]
    trans = split(trans_ref[...])
    filt = filt_ref[...]
    out_ref[...] = (dot(trans[0], filt) + dot(trans[1], filt)).astype(jnp.bfloat16)


def project_kernel(
    bits, cell_volume, filt_ref, applied_ref, trans_ref, proj_ref,
    total, send, recv, gath, send_sem, recv_sem,
):
    gram_sum(bits, cell_volume, filt_ref, applied_ref, total, send, recv, gath, send_sem, recv_sem)
    size = filt_ref.shape[0]
    trans = split(trans_ref[...])
    half = split(dot3(trans, split(gath[...].reshape(size, size))))
    contract = (((1,), (1,)), ((), ()))

    def dot_t(a, b):
        return lax.dot_general(a, b, contract, preferred_element_type=jnp.float32)

    proj_ref[...] = dot_t(half[0], trans[0]) + (
        dot_t(half[0], trans[1]) + dot_t(half[1], trans[0])
    )


def sum_call(kernel, operands, out_shape, squares, bits, number, flops):
    size = operands[0].shape[0]
    vmem = pl.BlockSpec(memory_space=pltpu.VMEM)
    room = size // 2 + TILE_ROWS * len(bits[0])
    sems = pltpu.SemaphoreType.DMA((2, 2 * len(bits[0])))
    halves = pltpu.VMEM((2, size // 2, size), jnp.float32)
    stage = pltpu.VMEM((2, room, size), jnp.float32)
    return pl.pallas_call(
        kernel,
        out_shape=out_shape,
        in_specs=[vmem] * len(operands),
        out_specs=jax.tree.map(lambda _: vmem, out_shape),
        scratch_shapes=[halves, stage, stage, halves]
        + [pltpu.VMEM((size, size), jnp.float32)] * squares
        + [sems, sems],
        cost_estimate=pl.CostEstimate(flops=flops, bytes_accessed=8 << 20, transcendentals=0),
        compiler_params=pltpu.CompilerParams(
            vmem_limit_bytes=32 << 20, collective_id=number, has_side_effects=True
        ),
    )(*operands)


def peers(doms, groups):
    dom = lax.axis_index("dom")
    band = lax.axis_index("band")
    rows = [lax.rem(dom + r, doms) for r in range(doms)]
    columns = [lax.rem(band + r, groups) for r in sorted(range(groups), key=lambda r: -min(r, groups - r))]
    others = [{"dom": d, "band": b} for b in columns for d in rows if b is not columns[-1] or d is not rows[0]]
    return [{"dom": dom, "band": band}] + others


def remote(source, target, send_sem, recv_sem, device):
    return pltpu.make_async_remote_copy(
        src_ref=source,
        dst_ref=target,
        send_sem=send_sem,
        recv_sem=recv_sem,
        device_id=device,
        device_id_type=pl.DeviceIdType.MESH,
    )


def greet(others):
    barrier = pltpu.get_barrier_semaphore()
    for other in others:
        pl.semaphore_signal(barrier, inc=1, device_id=other, device_id_type=pl.DeviceIdType.MESH)
    return barrier


def lane_orders(perm, back):
    size = perm.shape[0]
    high = size // LANES
    row = lax.broadcasted_iota(jnp.int32, (size, size), 0)
    col = lax.broadcasted_iota(jnp.int32, (size, size), 1)
    grouped = lax.rem(row // GRID_Z, high) * LANES + lax.rem(row, GRID_Z) * high + row // LANES
    perm[...] = jnp.where(grouped == col, 1.0, 0.0).astype(jnp.bfloat16)
    natural = lax.rem(row, high) * LANES + row // LANES * GRID_Z + lax.rem(row // high, GRID_Z)
    back[...] = jnp.where(natural == col, 1.0, 0.0).astype(jnp.bfloat16)


class BlockSum:
    def __init__(self, total, recv, gath, send_sem, recv_sem, levels):
        self.total, self.recv, self.gath = total, recv, gath
        self.send_sem, self.recv_sem, self.levels = send_sem, recv_sem, levels
        self.start, self.length = jnp.int32(0), total.shape[0]
        self.offset, self.copies = 0, []

    def steps(self):
        for level in range(len(self.levels)):
            yield functools.partial(self.scatter, level)
            yield functools.partial(self.add, level)
        for level in range(len(self.levels) - 1, -1, -1):
            yield functools.partial(self.gather, level)
            yield functools.partial(self.join, level)

    def scatter(self, level):
        at, size, device = self.levels[level]
        rows = self.length // size
        self.copies = []
        for r in range(1, size):
            to = lax.rem(at + r, size)
            source = pl.ds(pl.multiple_of(self.start + to * rows, TILE_ROWS), rows)
            place = pl.ds(self.offset + (r - 1) * rows, rows)
            self.copies.append(
                remote(
                    self.total.at[source], self.recv.at[place],
                    self.send_sem.at[0, level, r], self.recv_sem.at[0, level, r], device(to),
                )
            )
        for made in self.copies:
            made.start()

    def add(self, level):
        at, size, _ = self.levels[level]
        rows = self.length // size
        self.start = pl.multiple_of(self.start + at * rows, TILE_ROWS)
        self.length = rows
        kept = pl.ds(self.start, rows)
        for made in self.copies:
            made.wait()
        value = self.total[kept]
        for r in range(1, size):
            value = value + self.recv[pl.ds(self.offset + (r - 1) * rows, rows)]
        self.offset += (size - 1) * rows
        self.total[kept] = value
        if level == len(self.levels) - 1:
            self.gath[kept] = value

    def gather(self, level):
        at, size, device = self.levels[level]
        area = self.gath.at[pl.ds(self.start, self.length)]
        self.copies = [
            remote(area, area, self.send_sem.at[1, level, r], self.recv_sem.at[1, level, r], device(lax.rem(at + r, size)))
            for r in range(1, size)
        ]
        for made in self.copies:
            made.start()

    def join(self, level):
        at, size, _ = self.levels[level]
        for made in self.copies:
            made.wait()
        self.start = pl.multiple_of(self.start - at * self.length, TILE_ROWS)
        self.length *= size


def sum_levels(doms, groups):
    dom = lax.axis_index("dom")
    band = lax.axis_index("band")
    core, chip = lax.rem(dom, 2), dom // 2
    low, high = lax.rem(band, 2), band // 2
    return [
        (core, 2, lambda to: {"dom": chip * 2 + to}),
        (chip * 2 + low, doms, lambda to: {"dom": to // 2 * 2 + core, "band": high * 2 + lax.rem(to, 2)}),
        (high, groups // 2, lambda to: {"band": to * 2 + low}),
    ]


def upper_blocks(total):
    count = total // LANES
    return [(i, j) for i in range(count) for j in range(i, count)]


def next_rings(ring, high):
    row = lax.rem(lax.broadcasted_iota(jnp.int32, ring.shape, 0), LANES)
    apart = lax.rem(row - lax.broadcasted_iota(jnp.int32, ring.shape, 1) + LANES, LANES)
    ring[...] = jnp.where((apart == high) | (apart == LANES - high), 1.0, 0.0).astype(jnp.bfloat16)


def next_cells(nexts):
    size = nexts.shape[0]
    row = lax.broadcasted_iota(jnp.int32, (size, size), 0)
    col = lax.broadcasted_iota(jnp.int32, (size, size), 1)
    ahead = col // GRID_Z * GRID_Z + lax.rem(col + 1, GRID_Z)
    nexts[...] = jnp.where((row == ahead) | (row == col + GRID_Z), 1.0, 0.0).astype(jnp.bfloat16)


def gram(factor, left, flipped, packed, halve):
    slab, lanes, total = flipped.shape
    size = 2 * LANES
    count = total // size
    product = {}
    for i in range(count):
        first = 0 if halve else i * size
        block = jnp.zeros((size, total - first), jnp.float32)
        for x in range(slab):
            block = block + dot(left[x, pl.ds(i * size, size), :], flipped[x, :, pl.ds(first, total - first)])
        for a in range(2):
            for j in range(first // LANES, total // LANES):
                column = j * LANES - first
                product[2 * i + a, j] = block[a * LANES : (a + 1) * LANES, column : column + LANES]
    for n, (i, j) in enumerate(upper_blocks(total)):
        value = product[i, j]
        if halve:
            value = 0.5 * (value + product[j, i].T)
        packed[pl.ds(n * LANES, LANES)] = value * factor


def unpack(packed, full):
    for n, (i, j) in enumerate(upper_blocks(full.shape[0])):
        block = packed[pl.ds(n * LANES, LANES)]
        full[pl.ds(i * LANES, LANES), pl.ds(j * LANES, LANES)] = block
        if i != j:
            full[pl.ds(j * LANES, LANES), pl.ds(i * LANES, LANES)] = block.T


def inverse_root(full, work, other, pause):
    size = full.shape[0]
    row = lax.broadcasted_iota(jnp.int32, (size, size), 0)
    col = lax.broadcasted_iota(jnp.int32, (size, size), 1)

    def diagonal(value):
        return jnp.where(row == col, value, 0.0)

    corr = full[...]
    scale = jnp.sqrt(jnp.sum(corr * corr) + 1e-06)
    work[...] = corr / scale
    for double in range(NS_STEPS // 2 - 1):
        held = split(work[...])
        square = dot(held[0], held[0])
        rest = dot(square.astype(jnp.bfloat16), (0.0625 * square - 0.5625 * work[...]).astype(jnp.bfloat16))
        factor = split(diagonal(2.25) - 2.4375 * work[...] + (1.6875 * square + rest))
        pause()
        if double == 0:
            full[...] = factor[0].astype(jnp.float32) + factor[1].astype(jnp.float32)
        else:
            full[...] = dot3(split(full[...]), factor)
            pause()
        other[...] = dot3(held, factor)
        pause()
        work[...] = dot3(factor, split(other[...]))
        pause()
    left = diagonal(1.0) - work[...]
    rounded = left.astype(jnp.bfloat16)
    square = dot(rounded, rounded)
    rest = 0.5 * left + 0.375 * square
    rest = rest + dot(square.astype(jnp.bfloat16), (0.3125 * left + 0.0625 * square).astype(jnp.bfloat16))
    pause()
    value = full[...]
    value = value + dot(value.astype(jnp.bfloat16), rest.astype(jnp.bfloat16))
    return value / jnp.sqrt(scale)


def step_kernel(
    groups, cell_volume, bounds_ref, sent_ref, pot_ref, out_ref, proj_ref,
    filt_ref, beyond, image_ref, flipped, nexts, stage, pots, perm, back, ring, even, odd, diag, send_f, send_y,
    corr_sum, corr_recv, corr_gath, hamil_sum, hamil_recv, hamil_gath, full, work, other, turn, spread, turned,
    in_send, in_recv, pot_send, pot_recv, out_send, out_recv, corr_send, corr_arrive, hamil_send, hamil_arrive, back_send, back_recv,
):
    doms, slab, mine, width = stage.shape
    devices = doms * groups
    dom = lax.axis_index("dom")
    band = lax.axis_index("band")
    planes = doms * slab
    part = min(mine, 8)
    chunks = mine // part
    rows = planes * part
    lanes = width // groups
    levels = width // LANES
    high = LANES // GRID_Z
    spans = levels // high
    half_width = (bounds_ref[1] - bounds_ref[0]) / 2.0
    centre = (bounds_ref[1] + bounds_ref[0]) / 2.0
    inv_half = 1.0 / half_width

    everyone = peers(doms, groups)
    barrier = greet(everyone[1:])
    lane_orders(perm, back)
    next_rings(ring, high)
    pl.semaphore_wait(barrier, len(everyone) - 1)

    def incoming(c, r):
        peer = lax.rem(dom + r, doms)
        some = pl.ds(c * part, part)
        source, target = sent_ref.at[peer, :, some, :], stage.at[dom, :, some, :]
        if r == 0:
            return pltpu.make_async_copy(source, target, in_recv.at[c, r])
        return remote(source, target, in_send.at[c, r], in_recv.at[c, r], {"dom": peer})

    def potential(r):
        if r == 0:
            return pltpu.make_async_copy(pot_ref, pots.at[dom], pot_recv.at[r])
        return remote(pot_ref, pots.at[dom], pot_send.at[r], pot_recv.at[r], {"dom": lax.rem(dom + r, doms)})

    for r in range(doms):
        potential(r).start()
    for c in range(chunks):
        for r in range(doms):
            incoming(c, r).start()

    lane = lax.broadcasted_iota(jnp.int32, (rows, LANES), 1)
    row_of_lane = lax.broadcasted_iota(jnp.int32, (doms, part, LANES), 2) // GRID_Z
    first_high = lax.rem(lane, high) == 0
    last_high = lax.rem(lane, high) == high - 1

    for r in range(doms):
        potential(r).wait()
    for k in range(spans):
        pot = jnp.concatenate(
            [pots[:, :, pl.ds((h * spans + k) * LANES, LANES)].reshape(planes, LANES) for h in range(high)], axis=1
        )
        ordered = jnp.zeros(pot.shape, jnp.float32)
        for piece in range(3):
            top = pot.astype(jnp.bfloat16)
            ordered = ordered + dot(top, perm[...])
            pot = pot - top.astype(jnp.float32)
        scaled = (3.0 + ordered - centre) * (2.0 * inv_half)
        for b in range(high):
            line = scaled[:, b * LANES : (b + 1) * LANES]
            diag[k * high + b] = jnp.broadcast_to(line[:, None, :], (planes, part, LANES)).reshape(rows, LANES)

    def edges(field):
        top = field[levels]
        field[0] = jnp.where(first_high, pltpu.roll(top, LANES - (high - 1), 1), pltpu.roll(top, 1, 1))
        low = field[1]
        field[levels + 1] = jnp.where(last_high, pltpu.roll(low, high - 1, 1), pltpu.roll(low, LANES - 1, 1))

    cut = rows // SHARE if SHARE else 0

    def sums_z(values):
        if not cut:
            return None
        top = split(jnp.concatenate([v[:cut] for v in values], axis=0))
        return dot(jnp.concatenate(top, axis=1), ring[...])

    def image(v, field, i, sums):
        rest = v[cut:]
        around = pltpu.roll(rest, high, 1) + pltpu.roll(rest, LANES - high, 1)
        if cut:
            around = jnp.concatenate([sums, around], axis=0)
        around = around + (field[i - 1] + field[i + 1])
        around = around + (
            jnp.concatenate([v[part:], v[:part]], axis=0) + jnp.concatenate([v[rows - part :], v[: rows - part]], axis=0)
        )
        return diag[i - 1] * v - inv_half * around

    def sweep(source, target, first):
        def run(j, carry):
            start = 1 + j * UNROLL
            values = [source[start + i] for i in range(UNROLL)]
            sums = sums_z(values)
            for i in range(UNROLL):
                fresh = image(values[i], source, start + i, sums[i * cut : (i + 1) * cut] if cut else None)
                target[start + i] = 0.5 * fresh if first else fresh - target[start + i]
            return carry

        lax.fori_loop(0, levels // UNROLL, run, 0)
        edges(target)

    first_row = pl.multiple_of((band * doms + dom) * mine, part)

    def outgoing(pieces):
        copies = []
        for r, device in enumerate(everyone):
            for which, piece, place in pieces(device):
                recv = out_recv.at[which, r]
                if r == 0:
                    copies.append(pltpu.make_async_copy(piece, place, recv))
                else:
                    copies.append(remote(piece, place, out_send.at[which, r], recv, device))
        return copies

    def block(device):
        return pl.ds(pl.multiple_of(device["band"] * lanes, LANES), lanes)

    def main(c, device):
        source = send_f.at[pl.ds(device["dom"] * slab, slab), pl.ds(c * part, part), block(device)]
        return [(c, source, filt_ref.at[pl.ds(0, slab), pl.ds(first_row + c * part, part), :])]

    def halo(device):
        above = pl.ds(pl.multiple_of(lax.rem(device["band"] + 1, groups) * LANES, LANES), LANES)
        rows_here = pl.ds(first_row, mine)
        return [
            (chunks, send_f.at[device["dom"] * slab + slab, :, block(device)], filt_ref.at[slab, rows_here, :]),
            (chunks + 1, send_y.at[device["dom"], :, above], beyond.at[rows_here, :]),
        ]

    for c in range(chunks):
        for r in range(doms):
            incoming(c, r).wait()
        some = pl.ds(c * part, part)
        for k in range(spans):
            cells = jnp.concatenate(
                [
                    stage[:, :, some, pl.ds((h * spans + k) * LANES, LANES)].astype(jnp.float32).reshape(rows, LANES)
                    for h in range(high)
                ],
                axis=1,
            )
            ordered = dot(cells.astype(jnp.bfloat16), perm[...])
            for b in range(high):
                even[1 + k * high + b] = ordered[:, b * LANES : (b + 1) * LANES]
        edges(even)
        sweep(even, odd, True)

        def pair(k, carry):
            sweep(odd, even, False)
            sweep(even, odd, False)
            return carry

        lax.fori_loop(0, (DEG - 1) // 2, pair, 0)
        last = odd
        if DEG % 2 == 0:
            sweep(odd, even, False)
            last = even

        for k in range(spans):
            values = [last[1 + k * high + b] for b in range(high)]
            natural = dot(jnp.concatenate(values, axis=1).astype(jnp.bfloat16), back[...])
            for h in range(high):
                column = (h * spans + k) * LANES
                value = natural[:, h * LANES : (h + 1) * LANES].reshape(planes, part, LANES)
                send_f[pl.ds(0, planes), some, pl.ds(column, LANES)] = value.astype(jnp.bfloat16)
                send_f[planes, some, pl.ds(column, LANES)] = value[0].astype(jnp.bfloat16)
                if column % lanes == 0:
                    value = value.reshape(doms, slab * part, LANES)
                    edge = value[:, :part]
                    for x in range(1, slab):
                        moved = value[:, x * part : (x + 1) * part].reshape(doms * part, LANES)
                        moved = pltpu.roll(moved, x * GRID_Z, 1).reshape(doms, part, LANES)
                        edge = jnp.where(row_of_lane == x, moved, edge)
                    send_y[:, some, pl.ds(column // lanes * LANES, LANES)] = edge.astype(jnp.bfloat16)
        for copy in outgoing(functools.partial(main, c)):
            copy.start()
    for copy in outgoing(halo):
        copy.start()
    next_cells(nexts)
    for c in range(chunks):
        for copy in outgoing(functools.partial(main, c)):
            copy.wait()

    total = filt_ref.shape[1]
    for x in range(slab):
        flipped[x] = filt_ref[x].T
    gram(cell_volume, filt_ref, flipped, corr_sum, False)
    corr = BlockSum(corr_sum, corr_recv, corr_gath, corr_send, corr_arrive, sum_levels(doms, groups))
    steps = list(corr.steps())
    for step in steps[:3]:
        step()
    for copy in outgoing(halo):
        copy.wait()
    edge = lax.broadcasted_iota(jnp.int32, (total, LANES), 1) >= LANES - GRID_Z
    for x in range(slab):
        pot = 3.0 + pots[dom, pl.ds(x, 1), pl.ds(pl.multiple_of(band * lanes, LANES), lanes)]
        value = filt_ref[x].astype(jnp.float32) * pot - filt_ref[x + 1].astype(jnp.float32)
        value = value - dot(filt_ref[x], nexts[...])
        after = pltpu.roll(beyond[...].astype(jnp.float32), (LANES - GRID_Z - x * GRID_Z) % LANES, 1)
        image_ref[x, :, pl.ds(0, lanes - LANES)] = value[:, : lanes - LANES].astype(jnp.bfloat16)
        image_ref[x, :, pl.ds(lanes - LANES, LANES)] = (
            value[:, lanes - LANES :] - jnp.where(edge, after, 0.0)
        ).astype(jnp.bfloat16)
    gram(cell_volume, image_ref, flipped, hamil_sum, True)
    hamil = BlockSum(hamil_sum, hamil_recv, hamil_gath, hamil_send, hamil_arrive, sum_levels(doms, groups))
    pending = list(hamil.steps())
    pending.pop(0)()
    steps = steps[3:]
    while steps:
        for _ in range(2):
            if steps:
                steps.pop(0)()
        for _ in range(2):
            if steps:
                pending.pop(0)()
    unpack(corr_gath, full)

    def pause():
        for _ in range(2):
            if len(pending) > 1:
                pending.pop(0)()

    calls = [0]

    def sometimes():
        calls[0] += 1
        if calls[0] % PAUSE == 0:
            pause()

    value = inverse_root(full, work, other, sometimes)
    turn[0], turn[1] = split(value)

    bands = out_ref.shape[0]
    parts = groups // 2
    size = total // parts
    place = out_ref.at[:, :, pl.ds(pl.multiple_of(band * lanes, LANES), lanes)]
    returned = []
    for n, shift in enumerate(sorted(range(parts), key=lambda r: -min(r, parts - r))):
        which = lax.rem(band // 2 + shift, parts)
        rows_here = pl.ds(pl.multiple_of(which * size, size), size)
        for x in range(slab):
            points = filt_ref[x]
            product = dot(turn[0, rows_here, :], points) + dot(turn[1, rows_here, :], points)
            for t in range(lanes // LANES):
                spread[t, pl.ds(x, size, stride=slab), :] = product[:, t * LANES : (t + 1) * LANES]
        for t in range(lanes // LANES):
            turned[rows_here, :, pl.ds(t * LANES, LANES)] = spread[t].reshape(size, slab, LANES).astype(jnp.bfloat16)
        for q in (1, 0):
            to = which * 2 + lax.rem(band + q, 2)
            source = turned.at[pl.ds(to * bands, bands)]
            recv = back_recv.at[n * 2 + q]
            if shift == 0 and q == 0:
                copy = pltpu.make_async_copy(source, place, recv)
            else:
                copy = remote(source, place, back_send.at[n * 2 + q], recv, {"band": to})
            copy.start()
            returned.append(copy)

    while pending:
        pending.pop(0)()
    unpack(hamil_gath, full)
    halfway = split(dot3((turn[0], turn[1]), split(full[...])))
    proj_ref[...] = dot3(halfway, (turn[0], turn[1]))
    for copy in returned:
        copy.wait()


def step_call(sent, potential, bounds, groups, cell_volume):
    doms, slab, mine, width = sent.shape
    devices = doms * groups
    total = devices * mine
    planes = doms * slab
    part = min(mine, 8)
    chunks = mine // part
    levels = width // LANES
    lanes = width // groups
    size = LANES * (LANES // GRID_Z)
    packed = LANES * len(upper_blocks(total))
    vmem = pl.BlockSpec(memory_space=pltpu.VMEM)
    hbm = pl.BlockSpec(memory_space=pl.ANY)
    order = pltpu.VMEM((size, size), jnp.bfloat16)
    field = pltpu.VMEM((levels + 2, planes * part, LANES), jnp.float32)
    triangle = pltpu.VMEM((packed, LANES), jnp.float32)
    square = pltpu.VMEM((total, total), jnp.float32)
    dma = pltpu.SemaphoreType.DMA
    most = max(2, doms, groups // 2)
    return pl.pallas_call(
        functools.partial(step_kernel, groups, cell_volume),
        out_shape=(
            jax.ShapeDtypeStruct((mine * doms, slab, width), jnp.bfloat16),
            jax.ShapeDtypeStruct((total, total), jnp.float32),
        ),
        in_specs=[pl.BlockSpec(memory_space=pltpu.SMEM), hbm, hbm],
        out_specs=(hbm, vmem),
        scratch_shapes=[
            pltpu.VMEM((slab + 1, total, lanes), jnp.bfloat16),
            pltpu.VMEM((total, LANES), jnp.bfloat16),
            pltpu.VMEM((slab, total, lanes), jnp.bfloat16),
            pltpu.VMEM((slab, lanes, total), jnp.bfloat16),
            pltpu.VMEM((lanes, lanes), jnp.bfloat16),
            pltpu.VMEM(sent.shape, jnp.bfloat16),
            pltpu.VMEM((doms, slab, width), jnp.float32),
            order,
            order,
            pltpu.VMEM((2 * LANES, LANES), jnp.bfloat16),
            field,
            field,
            pltpu.VMEM((levels, planes * part, LANES), jnp.float32),
            pltpu.VMEM((planes + 1, mine, width), jnp.bfloat16),
            pltpu.VMEM((doms, mine, groups * LANES), jnp.bfloat16),
        ]
        + [triangle] * 6
        + [square] * 3
        + [
            pltpu.VMEM((2, total, total), jnp.bfloat16),
            pltpu.VMEM((lanes // LANES, total // (groups // 2) * slab, LANES), jnp.float32),
            pltpu.VMEM((total, slab, lanes), jnp.bfloat16),
            dma((chunks, doms)),
            dma((chunks, doms)),
            dma((doms,)),
            dma((doms,)),
            dma((chunks + 2, devices)),
            dma((chunks + 2, devices)),
        ]
        + [dma((2, 3, most))] * 4
        + [dma((groups,))] * 2,
        cost_estimate=pl.CostEstimate(flops=60 * total**3, bytes_accessed=8 << 20, transcendentals=0),
        compiler_params=pltpu.CompilerParams(vmem_limit_bytes=48 << 20, collective_id=2, has_side_effects=True),
    )(bounds, sent, potential)


def body_plain(orbitals, potential, bounds):
    bands, slab, width = orbitals.shape
    doms = lax.axis_size("dom")
    groups = lax.axis_size("band")
    devices = doms * groups
    total_bands = bands * groups
    mine = bands // doms
    everyone = ("dom", "band")
    half_width = (bounds[1] - bounds[0]) / 2.0
    centre = (bounds[1] + bounds[0]) / 2.0
    cell_volume = 1.0 / (slab * doms * width)

    sent = orbitals.reshape(doms, mine, slab, width).transpose(0, 2, 1, 3)
    cells = lax.all_to_all(sent, "dom", split_axis=0, concat_axis=0, tiled=True)
    cells = cells.reshape(doms * slab, mine, width)
    pot = lax.all_to_all(
        jnp.broadcast_to(potential, (doms, slab, width)), "dom", split_axis=0, concat_axis=0, tiled=True
    ).reshape(doms * slab, 1, width)
    filt, applied = filter_bands(cells, pot, jnp.stack([1.0 / half_width, centre]), devices)
    filt = lax.all_to_all(filt, everyone, split_axis=0, concat_axis=0, tiled=True)
    applied = lax.all_to_all(applied, everyone, split_axis=0, concat_axis=0, tiled=True)
    filt = filt.reshape(total_bands, -1)
    applied = applied.reshape(total_bands, -1)
    bits = exchange_bits(doms, groups)
    square = jax.ShapeDtypeStruct((total_bands, total_bands), jnp.float32)
    rotated, trans = sum_call(
        functools.partial(orthonormal_kernel, bits, cell_volume, (doms, groups, mine)),
        (filt,),
        (jax.ShapeDtypeStruct(filt.shape, jnp.bfloat16), square),
        3,
        bits,
        0,
        40 * total_bands**3,
    )
    out = lax.all_to_all(rotated, "band", split_axis=0, concat_axis=1, tiled=True)
    projected = sum_call(
        functools.partial(project_kernel, bits, cell_volume),
        (filt, applied, trans),
        square,
        0,
        bits,
        1,
        40 * total_bands**3,
    )
    return out.reshape(bands, slab, width), projected


def body(orbitals, potential, bounds):
    bands, slab, width = orbitals.shape
    doms = lax.axis_size("dom")
    groups = lax.axis_size("band")
    mine = bands // doms
    total = bands * groups
    blocks = len(upper_blocks(total))
    if mine % 8 or slab * GRID_Z != LANES or width % (groups * LANES) or total % (2 * LANES) or blocks * LANES % (8 * doms * groups):
        return body_plain(orbitals, potential, bounds)
    cell_volume = 1.0 / (slab * doms * width)
    sent = orbitals.reshape(doms, mine, slab, width).transpose(0, 2, 1, 3)
    return step_call(sent, potential, bounds, groups, cell_volume)


def solution(mesh):
    return jax.shard_map(
        body,
        mesh=mesh,
        in_specs=(P("band", "dom", None), P("dom", None), P()),
        out_specs=(P("band", "dom", None), P()),
        check_vma=False,
    )
```

```python
import functools

import jax
import jax.numpy as jnp
from jax import lax
from jax.experimental import pallas as pl
from jax.experimental.pallas import tpu as pltpu
from jax.sharding import PartitionSpec as P

GRID_Z = 32
DEG = 8
NS_STEPS = 8
LANES = 128
UNROLL = 16
SHARE = 2
PAUSE = 1
TILE_ROWS = 8


def filter_kernel(scal_ref, cells_ref, pot_ref, sums_ref, filt_ref, applied_ref, field, high, low, coef):
    planes, bands, width = cells_ref.shape
    rows = planes * bands
    blocks_per_plane = filt_ref.shape[0] // planes
    block = filt_ref.shape[2]
    tile = sums_ref.shape[1]
    inv_half = scal_ref[0]
    centre = scal_ref[1]

    for x in range(planes):
        mine = pl.ds(x * bands, bands)
        coef[mine, :] = jnp.broadcast_to(3.0 + pot_ref[x], (bands, width))
        start = cells_ref[x].astype(jnp.float32)
        field[0, mine, :] = start
    for c in range(width // tile):
        cols = pl.ds(c * tile, tile)
        start = field[0, :, cols]
        high[0, :, cols] = start.astype(jnp.bfloat16)
        low[0, :, cols] = jnp.zeros((rows, tile), jnp.bfloat16)

    def shifted(v, by):
        if bands % 8 == 0:
            return jnp.concatenate([v[by:], v[:by]], axis=0)
        return pltpu.roll(v, (rows - by) % rows, 0)

    def neighbours(slot, c, v):
        cols = pl.ds(pl.multiple_of(c * tile, tile), tile)
        left = pl.ds(pl.multiple_of(lax.rem(c * tile + width - LANES, width), LANES), LANES)
        right = pl.ds(pl.multiple_of(lax.rem(c * tile + tile, width), LANES), LANES)

        def part(ref):
            wide = jnp.concatenate([ref[slot, :, left], ref[slot, :, cols], ref[slot, :, right]], axis=1)
            return dot(wide, sums_ref[...])

        return part(high) + part(low) + (shifted(v, bands) + shifted(v, rows - bands))

    def sweep(slot, other, weight, diagonal, first):
        def run(c, carry):
            cols = pl.ds(pl.multiple_of(c * tile, tile), tile)
            v = field[slot, :, cols]
            fresh = weight * neighbours(slot, c, v) + (coef[:, cols] * diagonal[0] + diagonal[1]) * v
            if not first:
                fresh = fresh - field[other, :, cols]
            field[other, :, cols] = fresh
            top, rest = split(fresh)
            high[other, :, cols] = top
            low[other, :, cols] = rest
            return carry

        lax.fori_loop(0, width // tile, run, 0)

    sweep(0, 1, -0.5 * inv_half, (inv_half, -centre * inv_half), True)

    def middle(k, carry):
        slot = lax.rem(k, 2)
        sweep(slot, 1 - slot, -inv_half, (2.0 * inv_half, -2.0 * centre * inv_half), False)
        return carry

    lax.fori_loop(1, DEG, middle, 0)
    slot = DEG % 2
    for c in range(width // tile):
        cols = pl.ds(c * tile, tile)
        v = field[slot, :, cols]
        applied = coef[:, cols] * v - 0.5 * neighbours(slot, c, v)
        piece, inner = divmod(c * tile, block)
        for x in range(planes):
            where = (x * blocks_per_plane + piece, slice(None), pl.ds(inner, tile))
            filt_ref[where] = v[x * bands : (x + 1) * bands].astype(jnp.bfloat16)
            applied_ref[where] = applied[x * bands : (x + 1) * bands].astype(jnp.bfloat16)


def neighbour_sums(tile):
    source = lax.broadcasted_iota(jnp.int32, (tile + 2 * LANES, tile), 0) - LANES
    target = lax.broadcasted_iota(jnp.int32, (tile + 2 * LANES, tile), 1)
    step = source - target
    same_row = (source >= 0) & (source // GRID_Z == target // GRID_Z)
    apart = lax.rem(step + GRID_Z, GRID_Z)
    beside_z = same_row & ((apart == 1) | (apart == GRID_Z - 1))
    beside_y = (step == GRID_Z) | (step == -GRID_Z)
    return (beside_z | beside_y).astype(jnp.bfloat16)


def filter_bands(cells, potential, scalars, devices):
    planes, bands, width = cells.shape
    rows = planes * bands
    block = planes * width // devices
    out = jax.ShapeDtypeStruct((devices, bands, block), jnp.bfloat16)
    vmem = pl.BlockSpec(memory_space=pltpu.VMEM)
    return pl.pallas_call(
        filter_kernel,
        out_shape=(out, out),
        in_specs=[pl.BlockSpec(memory_space=pltpu.SMEM), vmem, vmem, vmem],
        out_specs=(vmem, vmem),
        scratch_shapes=[
            pltpu.VMEM((2, rows, width), jnp.float32),
            pltpu.VMEM((2, rows, width), jnp.bfloat16),
            pltpu.VMEM((2, rows, width), jnp.bfloat16),
            pltpu.VMEM((rows, width), jnp.float32),
        ],
        compiler_params=pltpu.CompilerParams(vmem_limit_bytes=48 << 20),
    )(scalars, cells, potential, neighbour_sums(min(256, block)))


def split(value):
    spread = value * 65537.0
    high = spread - (spread - value)
    return high.astype(jnp.bfloat16), (value - high).astype(jnp.bfloat16)


def dot(a, b):
    return jnp.dot(a, b, preferred_element_type=jnp.float32)


def dot3(a, b):
    (a_high, a_low), (b_high, b_low) = a, b
    return dot(a_high, b_high) + (dot(a_high, b_low) + dot(a_low, b_high))


def exchange_bits(doms, groups):
    dom = [("dom", 1 << i) for i in range(1, (doms - 1).bit_length())]
    band = [("band", 1 << i) for i in range((groups - 1).bit_length())]
    core = [("dom", 1)]
    return core + band[:1] + dom + band[1:], core + dom + band


def gram_sum(bits, cell_volume, filt_ref, other_ref, total, send, recv, gath, send_sem, recv_sem):
    size = filt_ref.shape[0] // 2
    index = {axis: lax.axis_index(axis) for axis in ("dom", "band")}

    def partner(axis, bit):
        mine = lax.rem(index[axis] // bit, 2)
        return mine, {axis: index[axis] + bit - 2 * bit * mine}

    barrier = pltpu.get_barrier_semaphore()
    for axis, bit in bits[0]:
        pl.semaphore_signal(
            barrier, inc=1, device_id=partner(axis, bit)[1], device_id_type=pl.DeviceIdType.MESH
        )

    pairs = (((1,), (1,)), ((), ()))
    for stream in range(2):
        total[stream] = cell_volume * lax.dot_general(
            filt_ref[pl.ds(stream * size, size), :],
            other_ref[...],
            pairs,
            preferred_element_type=jnp.float32,
        )
    pl.semaphore_wait(barrier, len(bits[0]))

    def copy(stream, number, source, target, device):
        made = pltpu.make_async_remote_copy(
            src_ref=source,
            dst_ref=target,
            send_sem=send_sem.at[stream, number],
            recv_sem=recv_sem.at[stream, number],
            device_id=device,
            device_id_type=pl.DeviceIdType.MESH,
        )
        made.start()
        return made

    stages = len(bits[0])
    start = [jnp.int32(0)] * 2
    halved = [[], []]
    length, offset = size, 0
    for stage in range(stages):
        halve = length >= 2 * TILE_ROWS
        count = length // 2 if halve else length
        space = pl.ds(offset, count)
        flight = []
        for stream in range(2):
            axis, bit = bits[stream][stage]
            mine, device = partner(axis, bit)
            give = start[stream] + (1 - mine) * count if halve else start[stream]
            keep = start[stream] + mine * count if halve else start[stream]
            give = pl.multiple_of(give, TILE_ROWS)
            send[stream, space, :] = total[stream, pl.ds(give, count), :]
            flight.append(
                copy(stream, stage, send.at[stream, space], recv.at[stream, space], device)
            )
            start[stream] = pl.multiple_of(keep, TILE_ROWS)
            if halve:
                halved[stream].append((stage, mine, device))
        for stream in range(2):
            flight[stream].wait()
            kept = pl.ds(start[stream], count)
            if halve:
                own = total[stream, kept, :]
            else:
                own = send[stream, space, :]
            total[stream, kept, :] = own + recv[stream, space, :]
        length = count
        offset += count

    for stream in range(2):
        kept = pl.ds(start[stream], length)
        gath[stream, kept, :] = total[stream, kept, :]
    for back in range(len(halved[0]) - 1, -1, -1):
        flight = []
        for stream in range(2):
            stage, mine, device = halved[stream][back]
            area = gath.at[stream, pl.ds(start[stream], length)]
            flight.append(copy(stream, stages + stage, area, area, device))
            start[stream] = pl.multiple_of(start[stream] - mine * length, TILE_ROWS)
        for made in flight:
            made.wait()
        length *= 2


def orthonormal_kernel(
    bits, cell_volume, groups, filt_ref, out_ref, trans_ref,
    total, send, recv, gath, y_ref, z_ref, t_ref, send_sem, recv_sem,
):
    gram_sum(bits, cell_volume, filt_ref, filt_ref, total, send, recv, gath, send_sem, recv_sem)
    size = filt_ref.shape[0]
    outer, inner, width = groups
    row = lax.broadcasted_iota(jnp.int32, (size, size), 0)
    col = lax.broadcasted_iota(jnp.int32, (size, size), 1)
    diag = jnp.where(row == col, 1.5, 0.0)
    corr = gath[...].reshape(size, size)
    scale = jnp.sqrt(jnp.sum(corr * corr) + 1e-06)
    scaled = corr / scale
    factor = diag - 0.5 * scaled
    z_ref[...] = factor
    y_ref[...] = dot3(split(factor), split(scaled))

    def step(k, carry):
        y = split(y_ref[...])
        z = split(z_ref[...])
        factor = split(diag - 0.5 * dot3(z, y))
        y_ref[...] = dot3(factor, y)
        z_ref[...] = dot3(factor, z)
        return carry

    lax.fori_loop(1, NS_STEPS - 1, step, 0)
    y = split(y_ref[...])
    z = split(z_ref[...])
    factor = split(diag - 0.5 * dot3(z, y))
    t_ref[...] = dot3(factor, z) / jnp.sqrt(scale)
    for i in range(outer):
        for j in range(inner):
            trans_ref[pl.ds((j * outer + i) * width, width), :] = t_ref[
                pl.ds((i * inner + j) * width, width), :
            ]
    trans = split(trans_ref[...])
    filt = filt_ref[...]
    out_ref[...] = (dot(trans[0], filt) + dot(trans[1], filt)).astype(jnp.bfloat16)


def project_kernel(
    bits, cell_volume, filt_ref, applied_ref, trans_ref, proj_ref,
    total, send, recv, gath, send_sem, recv_sem,
):
    gram_sum(bits, cell_volume, filt_ref, applied_ref, total, send, recv, gath, send_sem, recv_sem)
    size = filt_ref.shape[0]
    trans = split(trans_ref[...])
    half = split(dot3(trans, split(gath[...].reshape(size, size))))
    contract = (((1,), (1,)), ((), ()))

    def dot_t(a, b):
        return lax.dot_general(a, b, contract, preferred_element_type=jnp.float32)

    proj_ref[...] = dot_t(half[0], trans[0]) + (
        dot_t(half[0], trans[1]) + dot_t(half[1], trans[0])
    )


def sum_call(kernel, operands, out_shape, squares, bits, number, flops):
    size = operands[0].shape[0]
    vmem = pl.BlockSpec(memory_space=pltpu.VMEM)
    room = size // 2 + TILE_ROWS * len(bits[0])
    sems = pltpu.SemaphoreType.DMA((2, 2 * len(bits[0])))
    halves = pltpu.VMEM((2, size // 2, size), jnp.float32)
    stage = pltpu.VMEM((2, room, size), jnp.float32)
    return pl.pallas_call(
        kernel,
        out_shape=out_shape,
        in_specs=[vmem] * len(operands),
        out_specs=jax.tree.map(lambda _: vmem, out_shape),
        scratch_shapes=[halves, stage, stage, halves]
        + [pltpu.VMEM((size, size), jnp.float32)] * squares
        + [sems, sems],
        cost_estimate=pl.CostEstimate(flops=flops, bytes_accessed=8 << 20, transcendentals=0),
        compiler_params=pltpu.CompilerParams(
            vmem_limit_bytes=32 << 20, collective_id=number, has_side_effects=True
        ),
    )(*operands)


def peers(doms, groups):
    dom = lax.axis_index("dom")
    band = lax.axis_index("band")
    rows = [lax.rem(dom + r, doms) for r in range(doms)]
    columns = [lax.rem(band + r, groups) for r in sorted(range(groups), key=lambda r: -min(r, groups - r))]
    others = [{"dom": d, "band": b} for b in columns for d in rows if b is not columns[-1] or d is not rows[0]]
    return [{"dom": dom, "band": band}] + others


def remote(source, target, send_sem, recv_sem, device):
    return pltpu.make_async_remote_copy(
        src_ref=source,
        dst_ref=target,
        send_sem=send_sem,
        recv_sem=recv_sem,
        device_id=device,
        device_id_type=pl.DeviceIdType.MESH,
    )


def greet(others):
    barrier = pltpu.get_barrier_semaphore()
    for other in others:
        pl.semaphore_signal(barrier, inc=1, device_id=other, device_id_type=pl.DeviceIdType.MESH)
    return barrier


def lane_orders(perm, back):
    size = perm.shape[0]
    high = size // LANES
    row = lax.broadcasted_iota(jnp.int32, (size, size), 0)
    col = lax.broadcasted_iota(jnp.int32, (size, size), 1)
    grouped = lax.rem(row // GRID_Z, high) * LANES + lax.rem(row, GRID_Z) * high + row // LANES
    perm[...] = jnp.where(grouped == col, 1.0, 0.0).astype(jnp.bfloat16)
    natural = lax.rem(row, high) * LANES + row // LANES * GRID_Z + lax.rem(row // high, GRID_Z)
    back[...] = jnp.where(natural == col, 1.0, 0.0).astype(jnp.bfloat16)


class BlockSum:
    def __init__(self, total, recv, gath, send_sem, recv_sem, levels):
        self.total, self.recv, self.gath = total, recv, gath
        self.send_sem, self.recv_sem, self.levels = send_sem, recv_sem, levels
        self.start, self.length = jnp.int32(0), total.shape[0]
        self.offset, self.copies = 0, []

    def steps(self):
        for level in range(len(self.levels)):
            yield functools.partial(self.scatter, level)
            yield functools.partial(self.add, level)
        for level in range(len(self.levels) - 1, -1, -1):
            yield functools.partial(self.gather, level)
            yield functools.partial(self.join, level)

    def scatter(self, level):
        at, size, device = self.levels[level]
        rows = self.length // size
        self.copies = []
        for r in range(1, size):
            to = lax.rem(at + r, size)
            source = pl.ds(pl.multiple_of(self.start + to * rows, TILE_ROWS), rows)
            place = pl.ds(self.offset + (r - 1) * rows, rows)
            self.copies.append(
                remote(
                    self.total.at[source], self.recv.at[place],
                    self.send_sem.at[0, level, r], self.recv_sem.at[0, level, r], device(to),
                )
            )
        for made in self.copies:
            made.start()

    def add(self, level):
        at, size, _ = self.levels[level]
        rows = self.length // size
        self.start = pl.multiple_of(self.start + at * rows, TILE_ROWS)
        self.length = rows
        kept = pl.ds(self.start, rows)
        for made in self.copies:
            made.wait()
        value = self.total[kept]
        for r in range(1, size):
            value = value + self.recv[pl.ds(self.offset + (r - 1) * rows, rows)]
        self.offset += (size - 1) * rows
        self.total[kept] = value
        if level == len(self.levels) - 1:
            self.gath[kept] = value

    def gather(self, level):
        at, size, device = self.levels[level]
        area = self.gath.at[pl.ds(self.start, self.length)]
        self.copies = [
            remote(area, area, self.send_sem.at[1, level, r], self.recv_sem.at[1, level, r], device(lax.rem(at + r, size)))
            for r in range(1, size)
        ]
        for made in self.copies:
            made.start()

    def join(self, level):
        at, size, _ = self.levels[level]
        for made in self.copies:
            made.wait()
        self.start = pl.multiple_of(self.start - at * self.length, TILE_ROWS)
        self.length *= size


def sum_levels(doms, groups):
    dom = lax.axis_index("dom")
    band = lax.axis_index("band")
    core, chip = lax.rem(dom, 2), dom // 2
    low, high = lax.rem(band, 2), band // 2
    return [
        (core, 2, lambda to: {"dom": chip * 2 + to}),
        (chip * 2 + low, doms, lambda to: {"dom": to // 2 * 2 + core, "band": high * 2 + lax.rem(to, 2)}),
        (high, groups // 2, lambda to: {"band": to * 2 + low}),
    ]


def upper_blocks(total):
    count = total // LANES
    return [(i, j) for i in range(count) for j in range(i, count)]


def next_rings(ring, high):
    row = lax.rem(lax.broadcasted_iota(jnp.int32, ring.shape, 0), LANES)
    apart = lax.rem(row - lax.broadcasted_iota(jnp.int32, ring.shape, 1) + LANES, LANES)
    ring[...] = jnp.where((apart == high) | (apart == LANES - high), 1.0, 0.0).astype(jnp.bfloat16)


def next_cells(nexts):
    size = nexts.shape[0]
    row = lax.broadcasted_iota(jnp.int32, (size, size), 0)
    col = lax.broadcasted_iota(jnp.int32, (size, size), 1)
    ahead = col // GRID_Z * GRID_Z + lax.rem(col + 1, GRID_Z)
    nexts[...] = jnp.where((row == ahead) | (row == col + GRID_Z), 1.0, 0.0).astype(jnp.bfloat16)


def gram(factor, left, flipped, packed, halve):
    slab, lanes, total = flipped.shape
    size = 2 * LANES
    count = total // size
    product = {}
    for i in range(count):
        first = 0 if halve else i * size
        block = jnp.zeros((size, total - first), jnp.float32)
        for x in range(slab):
            block = block + dot(left[x, pl.ds(i * size, size), :], flipped[x, :, pl.ds(first, total - first)])
        for a in range(2):
            for j in range(first // LANES, total // LANES):
                column = j * LANES - first
                product[2 * i + a, j] = block[a * LANES : (a + 1) * LANES, column : column + LANES]
    for n, (i, j) in enumerate(upper_blocks(total)):
        value = product[i, j]
        if halve:
            value = 0.5 * (value + product[j, i].T)
        packed[pl.ds(n * LANES, LANES)] = value * factor


def unpack(packed, full):
    for n, (i, j) in enumerate(upper_blocks(full.shape[0])):
        block = packed[pl.ds(n * LANES, LANES)]
        full[pl.ds(i * LANES, LANES), pl.ds(j * LANES, LANES)] = block
        if i != j:
            full[pl.ds(j * LANES, LANES), pl.ds(i * LANES, LANES)] = block.T


def inverse_root(full, work, other, pause):
    size = full.shape[0]
    row = lax.broadcasted_iota(jnp.int32, (size, size), 0)
    col = lax.broadcasted_iota(jnp.int32, (size, size), 1)

    def diagonal(value):
        return jnp.where(row == col, value, 0.0)

    corr = full[...]
    scale = jnp.sqrt(jnp.sum(corr * corr) + 1e-06)
    work[...] = corr / scale
    for double in range(NS_STEPS // 2 - 1):
        held = split(work[...])
        square = dot(held[0], held[0])
        rest = dot(square.astype(jnp.bfloat16), (0.0625 * square - 0.5625 * work[...]).astype(jnp.bfloat16))
        factor = split(diagonal(2.25) - 2.4375 * work[...] + (1.6875 * square + rest))
        pause()
        if double == 0:
            full[...] = factor[0].astype(jnp.float32) + factor[1].astype(jnp.float32)
        else:
            full[...] = dot3(split(full[...]), factor)
            pause()
        other[...] = dot3(held, factor)
        pause()
        work[...] = dot3(factor, split(other[...]))
        pause()
    left = diagonal(1.0) - work[...]
    rounded = left.astype(jnp.bfloat16)
    square = dot(rounded, rounded)
    rest = 0.5 * left + 0.375 * square
    rest = rest + dot(square.astype(jnp.bfloat16), (0.3125 * left + 0.0625 * square).astype(jnp.bfloat16))
    pause()
    value = full[...]
    value = value + dot(value.astype(jnp.bfloat16), rest.astype(jnp.bfloat16))
    return value / jnp.sqrt(scale)


def step_kernel(
    groups, cell_volume, bounds_ref, sent_ref, pot_ref, out_ref, proj_ref,
    filt_ref, beyond, image_ref, flipped, nexts, stage, pots, perm, back, ring, even, odd, diag, send_f, send_y,
    corr_sum, corr_recv, corr_gath, hamil_sum, hamil_recv, hamil_gath, full, work, other, turn, spread, turned,
    in_send, in_recv, pot_send, pot_recv, out_send, out_recv, corr_send, corr_arrive, hamil_send, hamil_arrive, back_send, back_recv,
):
    doms, slab, mine, width = stage.shape
    devices = doms * groups
    dom = lax.axis_index("dom")
    band = lax.axis_index("band")
    planes = doms * slab
    part = min(mine, 8)
    chunks = mine // part
    rows = planes * part
    lanes = width // groups
    levels = width // LANES
    high = LANES // GRID_Z
    spans = levels // high
    half_width = (bounds_ref[1] - bounds_ref[0]) / 2.0
    centre = (bounds_ref[1] + bounds_ref[0]) / 2.0
    inv_half = 1.0 / half_width

    everyone = peers(doms, groups)
    barrier = greet(everyone[1:])
    lane_orders(perm, back)
    next_rings(ring, high)
    pl.semaphore_wait(barrier, len(everyone) - 1)

    def incoming(c, r):
        peer = lax.rem(dom + r, doms)
        some = pl.ds(c * part, part)
        source, target = sent_ref.at[peer, :, some, :], stage.at[dom, :, some, :]
        if r == 0:
            return pltpu.make_async_copy(source, target, in_recv.at[c, r])
        return remote(source, target, in_send.at[c, r], in_recv.at[c, r], {"dom": peer})

    def potential(r):
        if r == 0:
            return pltpu.make_async_copy(pot_ref, pots.at[dom], pot_recv.at[r])
        return remote(pot_ref, pots.at[dom], pot_send.at[r], pot_recv.at[r], {"dom": lax.rem(dom + r, doms)})

    for r in range(doms):
        potential(r).start()
    for c in range(chunks):
        for r in range(doms):
            incoming(c, r).start()

    lane = lax.broadcasted_iota(jnp.int32, (rows, LANES), 1)
    row_of_lane = lax.broadcasted_iota(jnp.int32, (doms, part, LANES), 2) // GRID_Z
    first_high = lax.rem(lane, high) == 0
    last_high = lax.rem(lane, high) == high - 1

    for r in range(doms):
        potential(r).wait()
    for k in range(spans):
        pot = jnp.concatenate(
            [pots[:, :, pl.ds((h * spans + k) * LANES, LANES)].reshape(planes, LANES) for h in range(high)], axis=1
        )
        ordered = jnp.zeros(pot.shape, jnp.float32)
        for piece in range(3):
            top = pot.astype(jnp.bfloat16)
            ordered = ordered + dot(top, perm[...])
            pot = pot - top.astype(jnp.float32)
        scaled = (3.0 + ordered - centre) * (2.0 * inv_half)
        for b in range(high):
            line = scaled[:, b * LANES : (b + 1) * LANES]
            diag[k * high + b] = jnp.broadcast_to(line[:, None, :], (planes, part, LANES)).reshape(rows, LANES)

    def edges(field):
        top = field[levels]
        field[0] = jnp.where(first_high, pltpu.roll(top, LANES - (high - 1), 1), pltpu.roll(top, 1, 1))
        low = field[1]
        field[levels + 1] = jnp.where(last_high, pltpu.roll(low, high - 1, 1), pltpu.roll(low, LANES - 1, 1))

    cut = rows // SHARE if SHARE else 0

    def sums_z(values):
        if not cut:
            return None
        top = split(jnp.concatenate([v[:cut] for v in values], axis=0))
        return dot(jnp.concatenate(top, axis=1), ring[...])

    def image(v, field, i, sums):
        rest = v[cut:]
        around = pltpu.roll(rest, high, 1) + pltpu.roll(rest, LANES - high, 1)
        if cut:
            around = jnp.concatenate([sums, around], axis=0)
        around = around + (field[i - 1] + field[i + 1])
        around = around + (
            jnp.concatenate([v[part:], v[:part]], axis=0) + jnp.concatenate([v[rows - part :], v[: rows - part]], axis=0)
        )
        return diag[i - 1] * v - inv_half * around

    def sweep(source, target, first):
        def run(j, carry):
            start = 1 + j * UNROLL
            values = [source[start + i] for i in range(UNROLL)]
            sums = sums_z(values)
            for i in range(UNROLL):
                fresh = image(values[i], source, start + i, sums[i * cut : (i + 1) * cut] if cut else None)
                target[start + i] = 0.5 * fresh if first else fresh - target[start + i]
            return carry

        lax.fori_loop(0, levels // UNROLL, run, 0)
        edges(target)

    first_row = pl.multiple_of((band * doms + dom) * mine, part)

    def outgoing(pieces):
        copies = []
        for r, device in enumerate(everyone):
            for which, piece, place in pieces(device):
                recv = out_recv.at[which, r]
                if r == 0:
                    copies.append(pltpu.make_async_copy(piece, place, recv))
                else:
                    copies.append(remote(piece, place, out_send.at[which, r], recv, device))
        return copies

    def block(device):
        return pl.ds(pl.multiple_of(device["band"] * lanes, LANES), lanes)

    def main(c, device):
        source = send_f.at[pl.ds(device["dom"] * slab, slab), pl.ds(c * part, part), block(device)]
        return [(c, source, filt_ref.at[pl.ds(0, slab), pl.ds(first_row + c * part, part), :])]

    def halo(device):
        above = pl.ds(pl.multiple_of(lax.rem(device["band"] + 1, groups) * LANES, LANES), LANES)
        rows_here = pl.ds(first_row, mine)
        return [
            (chunks, send_f.at[device["dom"] * slab + slab, :, block(device)], filt_ref.at[slab, rows_here, :]),
            (chunks + 1, send_y.at[device["dom"], :, above], beyond.at[rows_here, :]),
        ]

    for c in range(chunks):
        for r in range(doms):
            incoming(c, r).wait()
        some = pl.ds(c * part, part)
        for k in range(spans):
            cells = jnp.concatenate(
                [
                    stage[:, :, some, pl.ds((h * spans + k) * LANES, LANES)].astype(jnp.float32).reshape(rows, LANES)
                    for h in range(high)
                ],
                axis=1,
            )
            ordered = dot(cells.astype(jnp.bfloat16), perm[...])
            for b in range(high):
                even[1 + k * high + b] = ordered[:, b * LANES : (b + 1) * LANES]
        edges(even)
        sweep(even, odd, True)

        def pair(k, carry):
            sweep(odd, even, False)
            sweep(even, odd, False)
            return carry

        lax.fori_loop(0, (DEG - 1) // 2, pair, 0)
        last = odd
        if DEG % 2 == 0:
            sweep(odd, even, False)
            last = even

        for k in range(spans):
            values = [last[1 + k * high + b] for b in range(high)]
            natural = dot(jnp.concatenate(values, axis=1).astype(jnp.bfloat16), back[...])
            for h in range(high):
                column = (h * spans + k) * LANES
                value = natural[:, h * LANES : (h + 1) * LANES].reshape(planes, part, LANES)
                send_f[pl.ds(0, planes), some, pl.ds(column, LANES)] = value.astype(jnp.bfloat16)
                send_f[planes, some, pl.ds(column, LANES)] = value[0].astype(jnp.bfloat16)
                if column % lanes == 0:
                    value = value.reshape(doms, slab * part, LANES)
                    edge = value[:, :part]
                    for x in range(1, slab):
                        moved = value[:, x * part : (x + 1) * part].reshape(doms * part, LANES)
                        moved = pltpu.roll(moved, x * GRID_Z, 1).reshape(doms, part, LANES)
                        edge = jnp.where(row_of_lane == x, moved, edge)
                    send_y[:, some, pl.ds(column // lanes * LANES, LANES)] = edge.astype(jnp.bfloat16)
        for copy in outgoing(functools.partial(main, c)):
            copy.start()
    for copy in outgoing(halo):
        copy.start()
    next_cells(nexts)
    for c in range(chunks):
        for copy in outgoing(functools.partial(main, c)):
            copy.wait()

    total = filt_ref.shape[1]
    for x in range(slab):
        flipped[x] = filt_ref[x].T
    gram(cell_volume, filt_ref, flipped, corr_sum, False)
    corr = BlockSum(corr_sum, corr_recv, corr_gath, corr_send, corr_arrive, sum_levels(doms, groups))
    steps = list(corr.steps())
    for step in steps[:3]:
        step()
    for copy in outgoing(halo):
        copy.wait()
    edge = lax.broadcasted_iota(jnp.int32, (total, LANES), 1) >= LANES - GRID_Z
    for x in range(slab):
        pot = 3.0 + pots[dom, pl.ds(x, 1), pl.ds(pl.multiple_of(band * lanes, LANES), lanes)]
        value = filt_ref[x].astype(jnp.float32) * pot - filt_ref[x + 1].astype(jnp.float32)
        value = value - dot(filt_ref[x], nexts[...])
        after = pltpu.roll(beyond[...].astype(jnp.float32), (LANES - GRID_Z - x * GRID_Z) % LANES, 1)
        image_ref[x, :, pl.ds(0, lanes - LANES)] = value[:, : lanes - LANES].astype(jnp.bfloat16)
        image_ref[x, :, pl.ds(lanes - LANES, LANES)] = (
            value[:, lanes - LANES :] - jnp.where(edge, after, 0.0)
        ).astype(jnp.bfloat16)
    gram(cell_volume, image_ref, flipped, hamil_sum, True)
    hamil = BlockSum(hamil_sum, hamil_recv, hamil_gath, hamil_send, hamil_arrive, sum_levels(doms, groups))
    pending = list(hamil.steps())
    pending.pop(0)()
    steps = steps[3:]
    while steps:
        for _ in range(2):
            if steps:
                steps.pop(0)()
        for _ in range(2):
            if steps:
                pending.pop(0)()
    unpack(corr_gath, full)

    def pause():
        for _ in range(2):
            if len(pending) > 1:
                pending.pop(0)()

    calls = [0]

    def sometimes():
        calls[0] += 1
        if calls[0] % PAUSE == 0:
            pause()

    value = inverse_root(full, work, other, sometimes)
    turn[0], turn[1] = split(value)

    bands = out_ref.shape[0]
    parts = groups // 2
    size = total // parts
    place = out_ref.at[:, :, pl.ds(pl.multiple_of(band * lanes, LANES), lanes)]
    returned = []
    for n, shift in enumerate(sorted(range(parts), key=lambda r: -min(r, parts - r))):
        which = lax.rem(band // 2 + shift, parts)
        rows_here = pl.ds(pl.multiple_of(which * size, size), size)
        for x in range(slab):
            points = filt_ref[x]
            product = dot(turn[0, rows_here, :], points) + dot(turn[1, rows_here, :], points)
            for t in range(lanes // LANES):
                spread[t, pl.ds(x, size, stride=slab), :] = product[:, t * LANES : (t + 1) * LANES]
        for t in range(lanes // LANES):
            turned[rows_here, :, pl.ds(t * LANES, LANES)] = spread[t].reshape(size, slab, LANES).astype(jnp.bfloat16)
        for q in (1, 0):
            to = which * 2 + lax.rem(band + q, 2)
            source = turned.at[pl.ds(to * bands, bands)]
            recv = back_recv.at[n * 2 + q]
            if shift == 0 and q == 0:
                copy = pltpu.make_async_copy(source, place, recv)
            else:
                copy = remote(source, place, back_send.at[n * 2 + q], recv, {"band": to})
            copy.start()
            returned.append(copy)

    while pending:
        pending.pop(0)()
    unpack(hamil_gath, full)
    halfway = split(dot3((turn[0], turn[1]), split(full[...])))
    proj_ref[...] = dot3(halfway, (turn[0], turn[1]))
    for copy in returned:
        copy.wait()


def step_call(sent, potential, bounds, groups, cell_volume):
    doms, slab, mine, width = sent.shape
    devices = doms * groups
    total = devices * mine
    planes = doms * slab
    part = min(mine, 8)
    chunks = mine // part
    levels = width // LANES
    lanes = width // groups
    size = LANES * (LANES // GRID_Z)
    packed = LANES * len(upper_blocks(total))
    vmem = pl.BlockSpec(memory_space=pltpu.VMEM)
    hbm = pl.BlockSpec(memory_space=pl.ANY)
    order = pltpu.VMEM((size, size), jnp.bfloat16)
    field = pltpu.VMEM((levels + 2, planes * part, LANES), jnp.float32)
    triangle = pltpu.VMEM((packed, LANES), jnp.float32)
    square = pltpu.VMEM((total, total), jnp.float32)
    dma = pltpu.SemaphoreType.DMA
    most = max(2, doms, groups // 2)
    return pl.pallas_call(
        functools.partial(step_kernel, groups, cell_volume),
        out_shape=(
            jax.ShapeDtypeStruct((mine * doms, slab, width), jnp.bfloat16),
            jax.ShapeDtypeStruct((total, total), jnp.float32),
        ),
        in_specs=[pl.BlockSpec(memory_space=pltpu.SMEM), hbm, hbm],
        out_specs=(hbm, vmem),
        scratch_shapes=[
            pltpu.VMEM((slab + 1, total, lanes), jnp.bfloat16),
            pltpu.VMEM((total, LANES), jnp.bfloat16),
            pltpu.VMEM((slab, total, lanes), jnp.bfloat16),
            pltpu.VMEM((slab, lanes, total), jnp.bfloat16),
            pltpu.VMEM((lanes, lanes), jnp.bfloat16),
            pltpu.VMEM(sent.shape, jnp.bfloat16),
            pltpu.VMEM((doms, slab, width), jnp.float32),
            order,
            order,
            pltpu.VMEM((2 * LANES, LANES), jnp.bfloat16),
            field,
            field,
            pltpu.VMEM((levels, planes * part, LANES), jnp.float32),
            pltpu.VMEM((planes + 1, mine, width), jnp.bfloat16),
            pltpu.VMEM((doms, mine, groups * LANES), jnp.bfloat16),
        ]
        + [triangle] * 6
        + [square] * 3
        + [
            pltpu.VMEM((2, total, total), jnp.bfloat16),
            pltpu.VMEM((lanes // LANES, total // (groups // 2) * slab, LANES), jnp.float32),
            pltpu.VMEM((total, slab, lanes), jnp.bfloat16),
            dma((chunks, doms)),
            dma((chunks, doms)),
            dma((doms,)),
            dma((doms,)),
            dma((chunks + 2, devices)),
            dma((chunks + 2, devices)),
        ]
        + [dma((2, 3, most))] * 4
        + [dma((groups,))] * 2,
        cost_estimate=pl.CostEstimate(flops=60 * total**3, bytes_accessed=8 << 20, transcendentals=0),
        compiler_params=pltpu.CompilerParams(vmem_limit_bytes=48 << 20, collective_id=2, has_side_effects=True),
    )(bounds, sent, potential)


def body_plain(orbitals, potential, bounds):
    bands, slab, width = orbitals.shape
    doms = lax.axis_size("dom")
    groups = lax.axis_size("band")
    devices = doms * groups
    total_bands = bands * groups
    mine = bands // doms
    everyone = ("dom", "band")
    half_width = (bounds[1] - bounds[0]) / 2.0
    centre = (bounds[1] + bounds[0]) / 2.0
    cell_volume = 1.0 / (slab * doms * width)

    sent = orbitals.reshape(doms, mine, slab, width).transpose(0, 2, 1, 3)
    cells = lax.all_to_all(sent, "dom", split_axis=0, concat_axis=0, tiled=True)
    cells = cells.reshape(doms * slab, mine, width)
    pot = lax.all_to_all(
        jnp.broadcast_to(potential, (doms, slab, width)), "dom", split_axis=0, concat_axis=0, tiled=True
    ).reshape(doms * slab, 1, width)
    filt, applied = filter_bands(cells, pot, jnp.stack([1.0 / half_width, centre]), devices)
    filt = lax.all_to_all(filt, everyone, split_axis=0, concat_axis=0, tiled=True)
    applied = lax.all_to_all(applied, everyone, split_axis=0, concat_axis=0, tiled=True)
    filt = filt.reshape(total_bands, -1)
    applied = applied.reshape(total_bands, -1)
    bits = exchange_bits(doms, groups)
    square = jax.ShapeDtypeStruct((total_bands, total_bands), jnp.float32)
    rotated, trans = sum_call(
        functools.partial(orthonormal_kernel, bits, cell_volume, (doms, groups, mine)),
        (filt,),
        (jax.ShapeDtypeStruct(filt.shape, jnp.bfloat16), square),
        3,
        bits,
        0,
        40 * total_bands**3,
    )
    out = lax.all_to_all(rotated, "band", split_axis=0, concat_axis=1, tiled=True)
    projected = sum_call(
        functools.partial(project_kernel, bits, cell_volume),
        (filt, applied, trans),
        square,
        0,
        bits,
        1,
        40 * total_bands**3,
    )
    return out.reshape(bands, slab, width), projected


def body(orbitals, potential, bounds):
    bands, slab, width = orbitals.shape
    doms = lax.axis_size("dom")
    groups = lax.axis_size("band")
    mine = bands // doms
    total = bands * groups
    blocks = len(upper_blocks(total))
    if mine % 8 or slab * GRID_Z != LANES or width % (groups * LANES) or total % (2 * LANES) or blocks * LANES % (8 * doms * groups):
        return body_plain(orbitals, potential, bounds)
    cell_volume = 1.0 / (slab * doms * width)
    sent = orbitals.reshape(doms, mine, slab, width).transpose(0, 2, 1, 3)
    return step_call(sent, potential, bounds, groups, cell_volume)


def solution(mesh):
    return jax.shard_map(
        body,
        mesh=mesh,
        in_specs=(P("band", "dom", None), P("dom", None), P()),
        out_specs=(P("band", "dom", None), P()),
        check_vma=False,
    )
```

```python
import functools

import jax
import jax.numpy as jnp
from jax import lax
from jax.experimental import pallas as pl
from jax.experimental.pallas import tpu as pltpu
from jax.sharding import PartitionSpec as P

GRID_Z = 32
DEG = 8
NS_STEPS = 8
LANES = 128
UNROLL = 16
SHARE = 5
PAUSE = 1
TILE_ROWS = 8


def filter_kernel(scal_ref, cells_ref, pot_ref, sums_ref, filt_ref, applied_ref, field, high, low, coef):
    planes, bands, width = cells_ref.shape
    rows = planes * bands
    blocks_per_plane = filt_ref.shape[0] // planes
    block = filt_ref.shape[2]
    tile = sums_ref.shape[1]
    inv_half = scal_ref[0]
    centre = scal_ref[1]

    for x in range(planes):
        mine = pl.ds(x * bands, bands)
        coef[mine, :] = jnp.broadcast_to(3.0 + pot_ref[x], (bands, width))
        start = cells_ref[x].astype(jnp.float32)
        field[0, mine, :] = start
    for c in range(width // tile):
        cols = pl.ds(c * tile, tile)
        start = field[0, :, cols]
        high[0, :, cols] = start.astype(jnp.bfloat16)
        low[0, :, cols] = jnp.zeros((rows, tile), jnp.bfloat16)

    def shifted(v, by):
        if bands % 8 == 0:
            return jnp.concatenate([v[by:], v[:by]], axis=0)
        return pltpu.roll(v, (rows - by) % rows, 0)

    def neighbours(slot, c, v):
        cols = pl.ds(pl.multiple_of(c * tile, tile), tile)
        left = pl.ds(pl.multiple_of(lax.rem(c * tile + width - LANES, width), LANES), LANES)
        right = pl.ds(pl.multiple_of(lax.rem(c * tile + tile, width), LANES), LANES)

        def part(ref):
            wide = jnp.concatenate([ref[slot, :, left], ref[slot, :, cols], ref[slot, :, right]], axis=1)
            return dot(wide, sums_ref[...])

        return part(high) + part(low) + (shifted(v, bands) + shifted(v, rows - bands))

    def sweep(slot, other, weight, diagonal, first):
        def run(c, carry):
            cols = pl.ds(pl.multiple_of(c * tile, tile), tile)
            v = field[slot, :, cols]
            fresh = weight * neighbours(slot, c, v) + (coef[:, cols] * diagonal[0] + diagonal[1]) * v
            if not first:
                fresh = fresh - field[other, :, cols]
            field[other, :, cols] = fresh
            top, rest = split(fresh)
            high[other, :, cols] = top
            low[other, :, cols] = rest
            return carry

        lax.fori_loop(0, width // tile, run, 0)

    sweep(0, 1, -0.5 * inv_half, (inv_half, -centre * inv_half), True)

    def middle(k, carry):
        slot = lax.rem(k, 2)
        sweep(slot, 1 - slot, -inv_half, (2.0 * inv_half, -2.0 * centre * inv_half), False)
        return carry

    lax.fori_loop(1, DEG, middle, 0)
    slot = DEG % 2
    for c in range(width // tile):
        cols = pl.ds(c * tile, tile)
        v = field[slot, :, cols]
        applied = coef[:, cols] * v - 0.5 * neighbours(slot, c, v)
        piece, inner = divmod(c * tile, block)
        for x in range(planes):
            where = (x * blocks_per_plane + piece, slice(None), pl.ds(inner, tile))
            filt_ref[where] = v[x * bands : (x + 1) * bands].astype(jnp.bfloat16)
            applied_ref[where] = applied[x * bands : (x + 1) * bands].astype(jnp.bfloat16)


def neighbour_sums(tile):
    source = lax.broadcasted_iota(jnp.int32, (tile + 2 * LANES, tile), 0) - LANES
    target = lax.broadcasted_iota(jnp.int32, (tile + 2 * LANES, tile), 1)
    step = source - target
    same_row = (source >= 0) & (source // GRID_Z == target // GRID_Z)
    apart = lax.rem(step + GRID_Z, GRID_Z)
    beside_z = same_row & ((apart == 1) | (apart == GRID_Z - 1))
    beside_y = (step == GRID_Z) | (step == -GRID_Z)
    return (beside_z | beside_y).astype(jnp.bfloat16)


def filter_bands(cells, potential, scalars, devices):
    planes, bands, width = cells.shape
    rows = planes * bands
    block = planes * width // devices
    out = jax.ShapeDtypeStruct((devices, bands, block), jnp.bfloat16)
    vmem = pl.BlockSpec(memory_space=pltpu.VMEM)
    return pl.pallas_call(
        filter_kernel,
        out_shape=(out, out),
        in_specs=[pl.BlockSpec(memory_space=pltpu.SMEM), vmem, vmem, vmem],
        out_specs=(vmem, vmem),
        scratch_shapes=[
            pltpu.VMEM((2, rows, width), jnp.float32),
            pltpu.VMEM((2, rows, width), jnp.bfloat16),
            pltpu.VMEM((2, rows, width), jnp.bfloat16),
            pltpu.VMEM((rows, width), jnp.float32),
        ],
        compiler_params=pltpu.CompilerParams(vmem_limit_bytes=48 << 20),
    )(scalars, cells, potential, neighbour_sums(min(256, block)))


def split(value):
    spread = value * 65537.0
    high = spread - (spread - value)
    return high.astype(jnp.bfloat16), (value - high).astype(jnp.bfloat16)


def dot(a, b):
    return jnp.dot(a, b, preferred_element_type=jnp.float32)


def dot3(a, b):
    (a_high, a_low), (b_high, b_low) = a, b
    return dot(a_high, b_high) + (dot(a_high, b_low) + dot(a_low, b_high))


def exchange_bits(doms, groups):
    dom = [("dom", 1 << i) for i in range(1, (doms - 1).bit_length())]
    band = [("band", 1 << i) for i in range((groups - 1).bit_length())]
    core = [("dom", 1)]
    return core + band[:1] + dom + band[1:], core + dom + band


def gram_sum(bits, cell_volume, filt_ref, other_ref, total, send, recv, gath, send_sem, recv_sem):
    size = filt_ref.shape[0] // 2
    index = {axis: lax.axis_index(axis) for axis in ("dom", "band")}

    def partner(axis, bit):
        mine = lax.rem(index[axis] // bit, 2)
        return mine, {axis: index[axis] + bit - 2 * bit * mine}

    barrier = pltpu.get_barrier_semaphore()
    for axis, bit in bits[0]:
        pl.semaphore_signal(
            barrier, inc=1, device_id=partner(axis, bit)[1], device_id_type=pl.DeviceIdType.MESH
        )

    pairs = (((1,), (1,)), ((), ()))
    for stream in range(2):
        total[stream] = cell_volume * lax.dot_general(
            filt_ref[pl.ds(stream * size, size), :],
            other_ref[...],
            pairs,
            preferred_element_type=jnp.float32,
        )
    pl.semaphore_wait(barrier, len(bits[0]))

    def copy(stream, number, source, target, device):
        made = pltpu.make_async_remote_copy(
            src_ref=source,
            dst_ref=target,
            send_sem=send_sem.at[stream, number],
            recv_sem=recv_sem.at[stream, number],
            device_id=device,
            device_id_type=pl.DeviceIdType.MESH,
        )
        made.start()
        return made

    stages = len(bits[0])
    start = [jnp.int32(0)] * 2
    halved = [[], []]
    length, offset = size, 0
    for stage in range(stages):
        halve = length >= 2 * TILE_ROWS
        count = length // 2 if halve else length
        space = pl.ds(offset, count)
        flight = []
        for stream in range(2):
            axis, bit = bits[stream][stage]
            mine, device = partner(axis, bit)
            give = start[stream] + (1 - mine) * count if halve else start[stream]
            keep = start[stream] + mine * count if halve else start[stream]
            give = pl.multiple_of(give, TILE_ROWS)
            send[stream, space, :] = total[stream, pl.ds(give, count), :]
            flight.append(
                copy(stream, stage, send.at[stream, space], recv.at[stream, space], device)
            )
            start[stream] = pl.multiple_of(keep, TILE_ROWS)
            if halve:
                halved[stream].append((stage, mine, device))
        for stream in range(2):
            flight[stream].wait()
            kept = pl.ds(start[stream], count)
            if halve:
                own = total[stream, kept, :]
            else:
                own = send[stream, space, :]
            total[stream, kept, :] = own + recv[stream, space, :]
        length = count
        offset += count

    for stream in range(2):
        kept = pl.ds(start[stream], length)
        gath[stream, kept, :] = total[stream, kept, :]
    for back in range(len(halved[0]) - 1, -1, -1):
        flight = []
        for stream in range(2):
            stage, mine, device = halved[stream][back]
            area = gath.at[stream, pl.ds(start[stream], length)]
            flight.append(copy(stream, stages + stage, area, area, device))
            start[stream] = pl.multiple_of(start[stream] - mine * length, TILE_ROWS)
        for made in flight:
            made.wait()
        length *= 2


def orthonormal_kernel(
    bits, cell_volume, groups, filt_ref, out_ref, trans_ref,
    total, send, recv, gath, y_ref, z_ref, t_ref, send_sem, recv_sem,
):
    gram_sum(bits, cell_volume, filt_ref, filt_ref, total, send, recv, gath, send_sem, recv_sem)
    size = filt_ref.shape[0]
    outer, inner, width = groups
    row = lax.broadcasted_iota(jnp.int32, (size, size), 0)
    col = lax.broadcasted_iota(jnp.int32, (size, size), 1)
    diag = jnp.where(row == col, 1.5, 0.0)
    corr = gath[...].reshape(size, size)
    scale = jnp.sqrt(jnp.sum(corr * corr) + 1e-06)
    scaled = corr / scale
    factor = diag - 0.5 * scaled
    z_ref[...] = factor
    y_ref[...] = dot3(split(factor), split(scaled))

    def step(k, carry):
        y = split(y_ref[...])
        z = split(z_ref[...])
        factor = split(diag - 0.5 * dot3(z, y))
        y_ref[...] = dot3(factor, y)
        z_ref[...] = dot3(factor, z)
        return carry

    lax.fori_loop(1, NS_STEPS - 1, step, 0)
    y = split(y_ref[...])
    z = split(z_ref[...])
    factor = split(diag - 0.5 * dot3(z, y))
    t_ref[...] = dot3(factor, z) / jnp.sqrt(scale)
    for i in range(outer):
        for j in range(inner):
            trans_ref[pl.ds((j * outer + i) * width, width), :] = t_ref[
                pl.ds((i * inner + j) * width, width), :
            ]
    trans = split(trans_ref[...])
    filt = filt_ref[...]
    out_ref[...] = (dot(trans[0], filt) + dot(trans[1], filt)).astype(jnp.bfloat16)


def project_kernel(
    bits, cell_volume, filt_ref, applied_ref, trans_ref, proj_ref,
    total, send, recv, gath, send_sem, recv_sem,
):
    gram_sum(bits, cell_volume, filt_ref, applied_ref, total, send, recv, gath, send_sem, recv_sem)
    size = filt_ref.shape[0]
    trans = split(trans_ref[...])
    half = split(dot3(trans, split(gath[...].reshape(size, size))))
    contract = (((1,), (1,)), ((), ()))

    def dot_t(a, b):
        return lax.dot_general(a, b, contract, preferred_element_type=jnp.float32)

    proj_ref[...] = dot_t(half[0], trans[0]) + (
        dot_t(half[0], trans[1]) + dot_t(half[1], trans[0])
    )


def sum_call(kernel, operands, out_shape, squares, bits, number, flops):
    size = operands[0].shape[0]
    vmem = pl.BlockSpec(memory_space=pltpu.VMEM)
    room = size // 2 + TILE_ROWS * len(bits[0])
    sems = pltpu.SemaphoreType.DMA((2, 2 * len(bits[0])))
    halves = pltpu.VMEM((2, size // 2, size), jnp.float32)
    stage = pltpu.VMEM((2, room, size), jnp.float32)
    return pl.pallas_call(
        kernel,
        out_shape=out_shape,
        in_specs=[vmem] * len(operands),
        out_specs=jax.tree.map(lambda _: vmem, out_shape),
        scratch_shapes=[halves, stage, stage, halves]
        + [pltpu.VMEM((size, size), jnp.float32)] * squares
        + [sems, sems],
        cost_estimate=pl.CostEstimate(flops=flops, bytes_accessed=8 << 20, transcendentals=0),
        compiler_params=pltpu.CompilerParams(
            vmem_limit_bytes=32 << 20, collective_id=number, has_side_effects=True
        ),
    )(*operands)


def peers(doms, groups):
    dom = lax.axis_index("dom")
    band = lax.axis_index("band")
    rows = [lax.rem(dom + r, doms) for r in range(doms)]
    columns = [lax.rem(band + r, groups) for r in sorted(range(groups), key=lambda r: -min(r, groups - r))]
    others = [{"dom": d, "band": b} for b in columns for d in rows if b is not columns[-1] or d is not rows[0]]
    return [{"dom": dom, "band": band}] + others


def remote(source, target, send_sem, recv_sem, device):
    return pltpu.make_async_remote_copy(
        src_ref=source,
        dst_ref=target,
        send_sem=send_sem,
        recv_sem=recv_sem,
        device_id=device,
        device_id_type=pl.DeviceIdType.MESH,
    )


def greet(others):
    barrier = pltpu.get_barrier_semaphore()
    for other in others:
        pl.semaphore_signal(barrier, inc=1, device_id=other, device_id_type=pl.DeviceIdType.MESH)
    return barrier


def lane_orders(perm, back):
    size = perm.shape[0]
    high = size // LANES
    row = lax.broadcasted_iota(jnp.int32, (size, size), 0)
    col = lax.broadcasted_iota(jnp.int32, (size, size), 1)
    grouped = lax.rem(row // GRID_Z, high) * LANES + lax.rem(row, GRID_Z) * high + row // LANES
    perm[...] = jnp.where(grouped == col, 1.0, 0.0).astype(jnp.bfloat16)
    natural = lax.rem(row, high) * LANES + row // LANES * GRID_Z + lax.rem(row // high, GRID_Z)
    back[...] = jnp.where(natural == col, 1.0, 0.0).astype(jnp.bfloat16)


class BlockSum:
    def __init__(self, total, recv, gath, send_sem, recv_sem, levels):
        self.total, self.recv, self.gath = total, recv, gath
        self.send_sem, self.recv_sem, self.levels = send_sem, recv_sem, levels
        self.start, self.length = jnp.int32(0), total.shape[0]
        self.offset, self.copies = 0, []

    def steps(self):
        for level in range(len(self.levels)):
            yield functools.partial(self.scatter, level)
            yield functools.partial(self.add, level)
        for level in range(len(self.levels) - 1, -1, -1):
            yield functools.partial(self.gather, level)
            yield functools.partial(self.join, level)

    def scatter(self, level):
        at, size, device = self.levels[level]
        rows = self.length // size
        self.copies = []
        for r in range(1, size):
            to = lax.rem(at + r, size)
            source = pl.ds(pl.multiple_of(self.start + to * rows, TILE_ROWS), rows)
            place = pl.ds(self.offset + (r - 1) * rows, rows)
            self.copies.append(
                remote(
                    self.total.at[source], self.recv.at[place],
                    self.send_sem.at[0, level, r], self.recv_sem.at[0, level, r], device(to),
                )
            )
        for made in self.copies:
            made.start()

    def add(self, level):
        at, size, _ = self.levels[level]
        rows = self.length // size
        self.start = pl.multiple_of(self.start + at * rows, TILE_ROWS)
        self.length = rows
        kept = pl.ds(self.start, rows)
        for made in self.copies:
            made.wait()
        value = self.total[kept]
        for r in range(1, size):
            value = value + self.recv[pl.ds(self.offset + (r - 1) * rows, rows)]
        self.offset += (size - 1) * rows
        self.total[kept] = value
        if level == len(self.levels) - 1:
            self.gath[kept] = value

    def gather(self, level):
        at, size, device = self.levels[level]
        area = self.gath.at[pl.ds(self.start, self.length)]
        self.copies = [
            remote(area, area, self.send_sem.at[1, level, r], self.recv_sem.at[1, level, r], device(lax.rem(at + r, size)))
            for r in range(1, size)
        ]
        for made in self.copies:
            made.start()

    def join(self, level):
        at, size, _ = self.levels[level]
        for made in self.copies:
            made.wait()
        self.start = pl.multiple_of(self.start - at * self.length, TILE_ROWS)
        self.length *= size


def sum_levels(doms, groups):
    dom = lax.axis_index("dom")
    band = lax.axis_index("band")
    core, chip = lax.rem(dom, 2), dom // 2
    low, high = lax.rem(band, 2), band // 2
    return [
        (core, 2, lambda to: {"dom": chip * 2 + to}),
        (chip * 2 + low, doms, lambda to: {"dom": to // 2 * 2 + core, "band": high * 2 + lax.rem(to, 2)}),
        (high, groups // 2, lambda to: {"band": to * 2 + low}),
    ]


def upper_blocks(total):
    count = total // LANES
    return [(i, j) for i in range(count) for j in range(i, count)]


def next_rings(ring, high):
    row = lax.rem(lax.broadcasted_iota(jnp.int32, ring.shape, 0), LANES)
    apart = lax.rem(row - lax.broadcasted_iota(jnp.int32, ring.shape, 1) + LANES, LANES)
    ring[...] = jnp.where((apart == high) | (apart == LANES - high), 1.0, 0.0).astype(jnp.bfloat16)


def next_cells(nexts):
    size = nexts.shape[0]
    row = lax.broadcasted_iota(jnp.int32, (size, size), 0)
    col = lax.broadcasted_iota(jnp.int32, (size, size), 1)
    ahead = col // GRID_Z * GRID_Z + lax.rem(col + 1, GRID_Z)
    nexts[...] = jnp.where((row == ahead) | (row == col + GRID_Z), 1.0, 0.0).astype(jnp.bfloat16)


def gram(factor, left, flipped, packed, halve):
    slab, lanes, total = flipped.shape
    size = 2 * LANES
    count = total // size
    product = {}
    for i in range(count):
        first = 0 if halve else i * size
        block = jnp.zeros((size, total - first), jnp.float32)
        for x in range(slab):
            block = block + dot(left[x, pl.ds(i * size, size), :], flipped[x, :, pl.ds(first, total - first)])
        for a in range(2):
            for j in range(first // LANES, total // LANES):
                column = j * LANES - first
                product[2 * i + a, j] = block[a * LANES : (a + 1) * LANES, column : column + LANES]
    for n, (i, j) in enumerate(upper_blocks(total)):
        value = product[i, j]
        if halve:
            value = 0.5 * (value + product[j, i].T)
        packed[pl.ds(n * LANES, LANES)] = value * factor


def unpack(packed, full):
    for n, (i, j) in enumerate(upper_blocks(full.shape[0])):
        block = packed[pl.ds(n * LANES, LANES)]
        full[pl.ds(i * LANES, LANES), pl.ds(j * LANES, LANES)] = block
        if i != j:
            full[pl.ds(j * LANES, LANES), pl.ds(i * LANES, LANES)] = block.T


def inverse_root(full, work, other, pause):
    size = full.shape[0]
    row = lax.broadcasted_iota(jnp.int32, (size, size), 0)
    col = lax.broadcasted_iota(jnp.int32, (size, size), 1)

    def diagonal(value):
        return jnp.where(row == col, value, 0.0)

    corr = full[...]
    scale = jnp.sqrt(jnp.sum(corr * corr) + 1e-06)
    work[...] = corr / scale
    for double in range(NS_STEPS // 2 - 1):
        held = split(work[...])
        square = dot(held[0], held[0])
        rest = dot(square.astype(jnp.bfloat16), (0.0625 * square - 0.5625 * work[...]).astype(jnp.bfloat16))
        factor = split(diagonal(2.25) - 2.4375 * work[...] + (1.6875 * square + rest))
        pause()
        if double == 0:
            full[...] = factor[0].astype(jnp.float32) + factor[1].astype(jnp.float32)
        else:
            full[...] = dot3(split(full[...]), factor)
            pause()
        other[...] = dot3(held, factor)
        pause()
        work[...] = dot3(factor, split(other[...]))
        pause()
    left = diagonal(1.0) - work[...]
    rounded = left.astype(jnp.bfloat16)
    square = dot(rounded, rounded)
    rest = 0.5 * left + 0.375 * square
    rest = rest + dot(square.astype(jnp.bfloat16), (0.3125 * left + 0.0625 * square).astype(jnp.bfloat16))
    pause()
    value = full[...]
    value = value + dot(value.astype(jnp.bfloat16), rest.astype(jnp.bfloat16))
    return value / jnp.sqrt(scale)


def step_kernel(
    groups, cell_volume, bounds_ref, sent_ref, pot_ref, out_ref, proj_ref,
    filt_ref, beyond, image_ref, flipped, nexts, stage, pots, perm, back, ring, even, odd, diag, send_f, send_y,
    corr_sum, corr_recv, corr_gath, hamil_sum, hamil_recv, hamil_gath, full, work, other, turn, spread, turned,
    in_send, in_recv, pot_send, pot_recv, out_send, out_recv, corr_send, corr_arrive, hamil_send, hamil_arrive, back_send, back_recv,
):
    doms, slab, mine, width = stage.shape
    devices = doms * groups
    dom = lax.axis_index("dom")
    band = lax.axis_index("band")
    planes = doms * slab
    part = min(mine, 8)
    chunks = mine // part
    rows = planes * part
    lanes = width // groups
    levels = width // LANES
    high = LANES // GRID_Z
    spans = levels // high
    half_width = (bounds_ref[1] - bounds_ref[0]) / 2.0
    centre = (bounds_ref[1] + bounds_ref[0]) / 2.0
    inv_half = 1.0 / half_width

    everyone = peers(doms, groups)
    barrier = greet(everyone[1:])
    lane_orders(perm, back)
    next_rings(ring, high)
    pl.semaphore_wait(barrier, len(everyone) - 1)

    def incoming(c, r):
        peer = lax.rem(dom + r, doms)
        some = pl.ds(c * part, part)
        source, target = sent_ref.at[peer, :, some, :], stage.at[dom, :, some, :]
        if r == 0:
            return pltpu.make_async_copy(source, target, in_recv.at[c, r])
        return remote(source, target, in_send.at[c, r], in_recv.at[c, r], {"dom": peer})

    def potential(r):
        if r == 0:
            return pltpu.make_async_copy(pot_ref, pots.at[dom], pot_recv.at[r])
        return remote(pot_ref, pots.at[dom], pot_send.at[r], pot_recv.at[r], {"dom": lax.rem(dom + r, doms)})

    for r in range(doms):
        potential(r).start()
    for c in range(chunks):
        for r in range(doms):
            incoming(c, r).start()

    lane = lax.broadcasted_iota(jnp.int32, (rows, LANES), 1)
    row_of_lane = lax.broadcasted_iota(jnp.int32, (doms, part, LANES), 2) // GRID_Z
    first_high = lax.rem(lane, high) == 0
    last_high = lax.rem(lane, high) == high - 1

    for r in range(doms):
        potential(r).wait()
    for k in range(spans):
        pot = jnp.concatenate(
            [pots[:, :, pl.ds((h * spans + k) * LANES, LANES)].reshape(planes, LANES) for h in range(high)], axis=1
        )
        ordered = jnp.zeros(pot.shape, jnp.float32)
        for piece in range(3):
            top = pot.astype(jnp.bfloat16)
            ordered = ordered + dot(top, perm[...])
            pot = pot - top.astype(jnp.float32)
        scaled = (3.0 + ordered - centre) * (2.0 * inv_half)
        for b in range(high):
            line = scaled[:, b * LANES : (b + 1) * LANES]
            diag[k * high + b] = jnp.broadcast_to(line[:, None, :], (planes, part, LANES)).reshape(rows, LANES)

    def edges(field):
        top = field[levels]
        field[0] = jnp.where(first_high, pltpu.roll(top, LANES - (high - 1), 1), pltpu.roll(top, 1, 1))
        low = field[1]
        field[levels + 1] = jnp.where(last_high, pltpu.roll(low, high - 1, 1), pltpu.roll(low, LANES - 1, 1))

    cut = rows * SHARE // 8

    def sums_z(values):
        if not cut:
            return None
        top = split(jnp.concatenate([v[:cut] for v in values], axis=0))
        return dot(jnp.concatenate(top, axis=1), ring[...])

    def image(v, field, i, sums):
        rest = v[cut:]
        around = pltpu.roll(rest, high, 1) + pltpu.roll(rest, LANES - high, 1)
        if cut:
            around = jnp.concatenate([sums, around], axis=0)
        around = around + (field[i - 1] + field[i + 1])
        around = around + (
            jnp.concatenate([v[part:], v[:part]], axis=0) + jnp.concatenate([v[rows - part :], v[: rows - part]], axis=0)
        )
        return diag[i - 1] * v - inv_half * around

    def sweep(source, target, first):
        def run(j, carry):
            start = 1 + j * UNROLL
            values = [source[start + i] for i in range(UNROLL)]
            sums = sums_z(values)
            for i in range(UNROLL):
                fresh = image(values[i], source, start + i, sums[i * cut : (i + 1) * cut] if cut else None)
                target[start + i] = 0.5 * fresh if first else fresh - target[start + i]
            return carry

        lax.fori_loop(0, levels // UNROLL, run, 0)
        edges(target)

    first_row = pl.multiple_of((band * doms + dom) * mine, part)

    def outgoing(pieces):
        copies = []
        for r, device in enumerate(everyone):
            for which, piece, place in pieces(device):
                recv = out_recv.at[which, r]
                if r == 0:
                    copies.append(pltpu.make_async_copy(piece, place, recv))
                else:
                    copies.append(remote(piece, place, out_send.at[which, r], recv, device))
        return copies

    def block(device):
        return pl.ds(pl.multiple_of(device["band"] * lanes, LANES), lanes)

    def main(c, device):
        source = send_f.at[pl.ds(device["dom"] * slab, slab), pl.ds(c * part, part), block(device)]
        return [(c, source, filt_ref.at[pl.ds(0, slab), pl.ds(first_row + c * part, part), :])]

    def halo(device):
        above = pl.ds(pl.multiple_of(lax.rem(device["band"] + 1, groups) * LANES, LANES), LANES)
        rows_here = pl.ds(first_row, mine)
        return [
            (chunks, send_f.at[device["dom"] * slab + slab, :, block(device)], filt_ref.at[slab, rows_here, :]),
            (chunks + 1, send_y.at[device["dom"], :, above], beyond.at[rows_here, :]),
        ]

    for c in range(chunks):
        for r in range(doms):
            incoming(c, r).wait()
        some = pl.ds(c * part, part)
        for k in range(spans):
            cells = jnp.concatenate(
                [
                    stage[:, :, some, pl.ds((h * spans + k) * LANES, LANES)].astype(jnp.float32).reshape(rows, LANES)
                    for h in range(high)
                ],
                axis=1,
            )
            ordered = dot(cells.astype(jnp.bfloat16), perm[...])
            for b in range(high):
                even[1 + k * high + b] = ordered[:, b * LANES : (b + 1) * LANES]
        edges(even)
        sweep(even, odd, True)

        def pair(k, carry):
            sweep(odd, even, False)
            sweep(even, odd, False)
            return carry

        lax.fori_loop(0, (DEG - 1) // 2, pair, 0)
        last = odd
        if DEG % 2 == 0:
            sweep(odd, even, False)
            last = even

        for k in range(spans):
            values = [last[1 + k * high + b] for b in range(high)]
            natural = dot(jnp.concatenate(values, axis=1).astype(jnp.bfloat16), back[...])
            for h in range(high):
                column = (h * spans + k) * LANES
                value = natural[:, h * LANES : (h + 1) * LANES].reshape(planes, part, LANES)
                send_f[pl.ds(0, planes), some, pl.ds(column, LANES)] = value.astype(jnp.bfloat16)
                send_f[planes, some, pl.ds(column, LANES)] = value[0].astype(jnp.bfloat16)
                if column % lanes == 0:
                    value = value.reshape(doms, slab * part, LANES)
                    edge = value[:, :part]
                    for x in range(1, slab):
                        moved = value[:, x * part : (x + 1) * part].reshape(doms * part, LANES)
                        moved = pltpu.roll(moved, x * GRID_Z, 1).reshape(doms, part, LANES)
                        edge = jnp.where(row_of_lane == x, moved, edge)
                    send_y[:, some, pl.ds(column // lanes * LANES, LANES)] = edge.astype(jnp.bfloat16)
        for copy in outgoing(functools.partial(main, c)):
            copy.start()
    for copy in outgoing(halo):
        copy.start()
    next_cells(nexts)
    for c in range(chunks):
        for copy in outgoing(functools.partial(main, c)):
            copy.wait()

    total = filt_ref.shape[1]
    for x in range(slab):
        flipped[x] = filt_ref[x].T
    gram(cell_volume, filt_ref, flipped, corr_sum, False)
    corr = BlockSum(corr_sum, corr_recv, corr_gath, corr_send, corr_arrive, sum_levels(doms, groups))
    steps = list(corr.steps())
    for step in steps[:3]:
        step()
    for copy in outgoing(halo):
        copy.wait()
    edge = lax.broadcasted_iota(jnp.int32, (total, LANES), 1) >= LANES - GRID_Z
    for x in range(slab):
        pot = 3.0 + pots[dom, pl.ds(x, 1), pl.ds(pl.multiple_of(band * lanes, LANES), lanes)]
        value = filt_ref[x].astype(jnp.float32) * pot - filt_ref[x + 1].astype(jnp.float32)
        value = value - dot(filt_ref[x], nexts[...])
        after = pltpu.roll(beyond[...].astype(jnp.float32), (LANES - GRID_Z - x * GRID_Z) % LANES, 1)
        image_ref[x, :, pl.ds(0, lanes - LANES)] = value[:, : lanes - LANES].astype(jnp.bfloat16)
        image_ref[x, :, pl.ds(lanes - LANES, LANES)] = (
            value[:, lanes - LANES :] - jnp.where(edge, after, 0.0)
        ).astype(jnp.bfloat16)
    gram(cell_volume, image_ref, flipped, hamil_sum, True)
    hamil = BlockSum(hamil_sum, hamil_recv, hamil_gath, hamil_send, hamil_arrive, sum_levels(doms, groups))
    pending = list(hamil.steps())
    pending.pop(0)()
    steps = steps[3:]
    while steps:
        for _ in range(2):
            if steps:
                steps.pop(0)()
        for _ in range(2):
            if steps:
                pending.pop(0)()
    unpack(corr_gath, full)

    def pause():
        for _ in range(2):
            if len(pending) > 1:
                pending.pop(0)()

    calls = [0]

    def sometimes():
        calls[0] += 1
        if calls[0] % PAUSE == 0:
            pause()

    value = inverse_root(full, work, other, sometimes)
    turn[0], turn[1] = split(value)

    bands = out_ref.shape[0]
    parts = groups // 2
    size = total // parts
    place = out_ref.at[:, :, pl.ds(pl.multiple_of(band * lanes, LANES), lanes)]
    returned = []
    for n, shift in enumerate(sorted(range(parts), key=lambda r: -min(r, parts - r))):
        which = lax.rem(band // 2 + shift, parts)
        rows_here = pl.ds(pl.multiple_of(which * size, size), size)
        for x in range(slab):
            points = filt_ref[x]
            product = dot(turn[0, rows_here, :], points) + dot(turn[1, rows_here, :], points)
            for t in range(lanes // LANES):
                spread[t, pl.ds(x, size, stride=slab), :] = product[:, t * LANES : (t + 1) * LANES]
        for t in range(lanes // LANES):
            turned[rows_here, :, pl.ds(t * LANES, LANES)] = spread[t].reshape(size, slab, LANES).astype(jnp.bfloat16)
        for q in (1, 0):
            to = which * 2 + lax.rem(band + q, 2)
            source = turned.at[pl.ds(to * bands, bands)]
            recv = back_recv.at[n * 2 + q]
            if shift == 0 and q == 0:
                copy = pltpu.make_async_copy(source, place, recv)
            else:
                copy = remote(source, place, back_send.at[n * 2 + q], recv, {"band": to})
            copy.start()
            returned.append(copy)

    while pending:
        pending.pop(0)()
    unpack(hamil_gath, full)
    halfway = split(dot3((turn[0], turn[1]), split(full[...])))
    proj_ref[...] = dot3(halfway, (turn[0], turn[1]))
    for copy in returned:
        copy.wait()


def step_call(sent, potential, bounds, groups, cell_volume):
    doms, slab, mine, width = sent.shape
    devices = doms * groups
    total = devices * mine
    planes = doms * slab
    part = min(mine, 8)
    chunks = mine // part
    levels = width // LANES
    lanes = width // groups
    size = LANES * (LANES // GRID_Z)
    packed = LANES * len(upper_blocks(total))
    vmem = pl.BlockSpec(memory_space=pltpu.VMEM)
    hbm = pl.BlockSpec(memory_space=pl.ANY)
    order = pltpu.VMEM((size, size), jnp.bfloat16)
    field = pltpu.VMEM((levels + 2, planes * part, LANES), jnp.float32)
    triangle = pltpu.VMEM((packed, LANES), jnp.float32)
    square = pltpu.VMEM((total, total), jnp.float32)
    dma = pltpu.SemaphoreType.DMA
    most = max(2, doms, groups // 2)
    return pl.pallas_call(
        functools.partial(step_kernel, groups, cell_volume),
        out_shape=(
            jax.ShapeDtypeStruct((mine * doms, slab, width), jnp.bfloat16),
            jax.ShapeDtypeStruct((total, total), jnp.float32),
        ),
        in_specs=[pl.BlockSpec(memory_space=pltpu.SMEM), hbm, hbm],
        out_specs=(hbm, vmem),
        scratch_shapes=[
            pltpu.VMEM((slab + 1, total, lanes), jnp.bfloat16),
            pltpu.VMEM((total, LANES), jnp.bfloat16),
            pltpu.VMEM((slab, total, lanes), jnp.bfloat16),
            pltpu.VMEM((slab, lanes, total), jnp.bfloat16),
            pltpu.VMEM((lanes, lanes), jnp.bfloat16),
            pltpu.VMEM(sent.shape, jnp.bfloat16),
            pltpu.VMEM((doms, slab, width), jnp.float32),
            order,
            order,
            pltpu.VMEM((2 * LANES, LANES), jnp.bfloat16),
            field,
            field,
            pltpu.VMEM((levels, planes * part, LANES), jnp.float32),
            pltpu.VMEM((planes + 1, mine, width), jnp.bfloat16),
            pltpu.VMEM((doms, mine, groups * LANES), jnp.bfloat16),
        ]
        + [triangle] * 6
        + [square] * 3
        + [
            pltpu.VMEM((2, total, total), jnp.bfloat16),
            pltpu.VMEM((lanes // LANES, total // (groups // 2) * slab, LANES), jnp.float32),
            pltpu.VMEM((total, slab, lanes), jnp.bfloat16),
            dma((chunks, doms)),
            dma((chunks, doms)),
            dma((doms,)),
            dma((doms,)),
            dma((chunks + 2, devices)),
            dma((chunks + 2, devices)),
        ]
        + [dma((2, 3, most))] * 4
        + [dma((groups,))] * 2,
        cost_estimate=pl.CostEstimate(flops=60 * total**3, bytes_accessed=8 << 20, transcendentals=0),
        compiler_params=pltpu.CompilerParams(vmem_limit_bytes=48 << 20, collective_id=2, has_side_effects=True),
    )(bounds, sent, potential)


def body_plain(orbitals, potential, bounds):
    bands, slab, width = orbitals.shape
    doms = lax.axis_size("dom")
    groups = lax.axis_size("band")
    devices = doms * groups
    total_bands = bands * groups
    mine = bands // doms
    everyone = ("dom", "band")
    half_width = (bounds[1] - bounds[0]) / 2.0
    centre = (bounds[1] + bounds[0]) / 2.0
    cell_volume = 1.0 / (slab * doms * width)

    sent = orbitals.reshape(doms, mine, slab, width).transpose(0, 2, 1, 3)
    cells = lax.all_to_all(sent, "dom", split_axis=0, concat_axis=0, tiled=True)
    cells = cells.reshape(doms * slab, mine, width)
    pot = lax.all_to_all(
        jnp.broadcast_to(potential, (doms, slab, width)), "dom", split_axis=0, concat_axis=0, tiled=True
    ).reshape(doms * slab, 1, width)
    filt, applied = filter_bands(cells, pot, jnp.stack([1.0 / half_width, centre]), devices)
    filt = lax.all_to_all(filt, everyone, split_axis=0, concat_axis=0, tiled=True)
    applied = lax.all_to_all(applied, everyone, split_axis=0, concat_axis=0, tiled=True)
    filt = filt.reshape(total_bands, -1)
    applied = applied.reshape(total_bands, -1)
    bits = exchange_bits(doms, groups)
    square = jax.ShapeDtypeStruct((total_bands, total_bands), jnp.float32)
    rotated, trans = sum_call(
        functools.partial(orthonormal_kernel, bits, cell_volume, (doms, groups, mine)),
        (filt,),
        (jax.ShapeDtypeStruct(filt.shape, jnp.bfloat16), square),
        3,
        bits,
        0,
        40 * total_bands**3,
    )
    out = lax.all_to_all(rotated, "band", split_axis=0, concat_axis=1, tiled=True)
    projected = sum_call(
        functools.partial(project_kernel, bits, cell_volume),
        (filt, applied, trans),
        square,
        0,
        bits,
        1,
        40 * total_bands**3,
    )
    return out.reshape(bands, slab, width), projected


def body(orbitals, potential, bounds):
    bands, slab, width = orbitals.shape
    doms = lax.axis_size("dom")
    groups = lax.axis_size("band")
    mine = bands // doms
    total = bands * groups
    blocks = len(upper_blocks(total))
    if mine % 8 or slab * GRID_Z != LANES or width % (groups * LANES) or total % (2 * LANES) or blocks * LANES % (8 * doms * groups):
        return body_plain(orbitals, potential, bounds)
    cell_volume = 1.0 / (slab * doms * width)
    sent = orbitals.reshape(doms, mine, slab, width).transpose(0, 2, 1, 3)
    return step_call(sent, potential, bounds, groups, cell_volume)


def solution(mesh):
    return jax.shard_map(
        body,
        mesh=mesh,
        in_specs=(P("band", "dom", None), P("dom", None), P()),
        out_specs=(P("band", "dom", None), P()),
        check_vma=False,
    )
```
